32 devices in a mesh: grp: 2 (over x), row: 8 (over z, y), col: 2 (over core).
Axes of the slice: x: 2, y: 2, z: 4, core: 2. Of those that a mesh axis runs over, the one named last changes fastest.
Arguments:
- pair_act: bfloat16 [64, 32, 128], P(('grp', 'row'), 'col'), parts along dimension 0, may hold values from -200 to 200
- cotangent: bfloat16 [64, 32, 128], P(('grp', 'row'), 'col'), parts along dimension 0, may hold values from -6 to 6
- residue_mask: int32 [64], P('grp'), parts along dimension 0, may hold values from 0 to 1, as said below
- front_weight: bfloat16 [2, 128, 640], replicated, may hold values from -0.5 to 0.5
- out_weight: bfloat16 [2, 128, 128], replicated, may hold values from -0.5 to 0.5
Outputs:
- pair_grad: bfloat16 [64, 32, 128], P(('grp', 'row'), 'col'), parts along dimension 0
The draws below stay inside these ranges and needn't reach their ends.
There are 2 independent parts, one for each index of `grp`. The reference program is written for one: setup_inputs(seed, part) draws one part's arguments, and reference() takes and returns one part's arrays. A program takes and returns all parts, laid end to end along the dimension named above; an argument that names none is the same for every part. Nothing has to cross between parts.
Inputs may be any that keep to these rules, and one draw needn't show every extreme that they name: residue_mask is 1 on residues 0 to L - 1 and 0 from L on, for a chain length L of at least 24.
All inputs are finite; a program needn't handle non-finite values.
Results may differ from the reference program's by a relative error of at most 0.01.
Values may be sent and summed in bfloat16 or wider, within the bound.
No kernel may reach another device: no remote copies, remote signals or barrier semaphores. Data moves between devices by JAX's collectives and lax.ppermute only.
A program may use at most 64 MiB of HBM per device.

```python
import math
import jax
import jax.numpy as jnp
from jax import lax

C = 128
H = 128
N = 32


def draw_pair_act(key, part):
    keys = jax.random.split(jax.random.fold_in(key, 11), 3)
    base = jax.random.normal(keys[0], (N, N, C), jnp.float32)
    cell_scale = jnp.exp(jax.random.uniform(keys[1], (N, N, 1), jnp.float32, 0.0, math.log(10.0)))
    channel_scale = jnp.exp(jax.random.uniform(keys[2], (1, 1, C), jnp.float32, 0.0, math.log(10.0)))
    values = base * channel_scale * cell_scale
    return jnp.clip(values / 3.0, -200.0, 200.0).astype(jnp.bfloat16)


def draw_residue_mask(key, part):
    lowest = (3 * N + 3) // 4
    span_len = N - lowest + 1
    offset = jax.random.randint(jax.random.fold_in(key, 23), (), 0, span_len)
    length = lowest + (offset + jnp.asarray(part, jnp.int32)) % span_len
    return (jnp.arange(N, dtype=jnp.int32) < length).astype(jnp.int32)


def block_levels(key, dims, shards, least, high):
    factor_of, own = 1.0, jax.random.fold_in(key, 6)
    for position, parts in shards:
        heights = jnp.exp(jax.random.uniform(jax.random.fold_in(own, position), (parts,), jnp.float32, least / len(shards), high / len(shards)))
        factor_of = factor_of * jnp.repeat(heights, dims[position] // parts).reshape([-1 if axis == position else 1 for axis in range(len(dims))])
    return factor_of


def bell_draw(own_key, extent, scale, limit, pieces=(), kind=jnp.bfloat16):
    factor_of = block_levels(own_key, extent, pieces, -0.22, 0.18) if pieces else 1.0
    array = jax.random.normal(own_key, extent, jnp.float32) * scale * factor_of
    return jnp.minimum(jnp.maximum(array, -limit), limit).astype(kind)


def setup_inputs(seed: int = 0, part: int = 0) -> dict:
    seeds = jax.random.split(jax.random.key(seed), 6)
    own_keys = jax.random.split(jax.random.fold_in(seeds[5], part), 6)
    pair_act = draw_pair_act(jax.random.fold_in(jax.random.fold_in(seeds[5], part), 71), part)
    cotangent = bell_draw(own_keys[1], (N, N, C), 1.0, 6.0, ((0, 8), (1, 2)))
    residue_mask = draw_residue_mask(jax.random.fold_in(jax.random.fold_in(seeds[5], part), 71), part)
    front_weight = bell_draw(seeds[3], (2, C, 4 * H + C), C ** -0.5, 0.5)
    out_weight = bell_draw(seeds[4], (2, H, C), H ** -0.5, 0.5)
    return dict(pair_act=pair_act, cotangent=cotangent, residue_mask=residue_mask, front_weight=front_weight, out_weight=out_weight)


def layer_norm(values):
    centred = values - lax.optimization_barrier(jnp.mean(values, axis=-1, keepdims=True))
    spread = lax.optimization_barrier(jnp.mean(centred * centred, axis=-1, keepdims=True))
    return centred * lax.rsqrt(spread + 1e-05)

def project_pair(inner_pair, mask_pair, weight):
    normed = layer_norm(inner_pair.astype(jnp.float32)).astype(jnp.bfloat16)
    linear = jnp.dot(normed, weight, preferred_element_type=jnp.float32)
    left_side = jax.nn.sigmoid(linear[..., :H]) * linear[..., H:2 * H]
    right_side = jax.nn.sigmoid(linear[..., 2 * H:3 * H]) * linear[..., 3 * H:4 * H]
    operands = (jnp.stack((left_side, right_side)) * mask_pair[None, :, :, None]).astype(jnp.bfloat16)
    return (operands, jax.nn.sigmoid(linear[..., 4 * H:]))

def finish(mixed_part, gate_value, inner_pair, weight):
    normed = layer_norm(mixed_part).astype(jnp.bfloat16)
    update = jnp.dot(normed, weight, preferred_element_type=jnp.float32)
    return (inner_pair.astype(jnp.float32) + gate_value * update).astype(jnp.bfloat16)

def rounded(values):
    return lax.optimization_barrier(values.astype(jnp.bfloat16)).astype(jnp.float32)

def reference(pair_act, cotangent, residue_mask, front_weight, out_weight):
    chain_mask = residue_mask.astype(jnp.float32)
    mask_pair = chain_mask[:, None] * chain_mask[None, :]
    (out_ops, out_gate), out_front_back = jax.vjp(lambda inner_pair: project_pair(inner_pair, mask_pair, front_weight[0]), pair_act)
    out_left = out_ops[0].astype(jnp.float32)
    out_right = out_ops[1].astype(jnp.float32)
    out_mixed = jnp.einsum('ikc,jkc->ijc', out_left, out_right)
    pair_mid, out_finish_back = jax.vjp(lambda mixed_part, gate_value, inner_pair: finish(mixed_part, gate_value, inner_pair, out_weight[0]), out_mixed, out_gate, pair_act)
    (in_ops, in_gate), in_front_back = jax.vjp(lambda inner_pair: project_pair(inner_pair, mask_pair, front_weight[1]), pair_mid)
    in_left = in_ops[0].astype(jnp.float32)
    in_right = in_ops[1].astype(jnp.float32)
    in_mixed = jnp.einsum('kic,kjc->ijc', in_left, in_right)
    unused_pair, in_finish_back = jax.vjp(lambda mixed_part, gate_value, inner_pair: finish(mixed_part, gate_value, inner_pair, out_weight[1]), in_mixed, in_gate, pair_mid)
    grad_mixed, grad_gate, grad_inner = in_finish_back(cotangent)
    signal = rounded(grad_mixed)
    grad_left = jnp.einsum('ijc,kjc->kic', signal, in_right)
    grad_right = jnp.einsum('ijc,kic->kjc', signal, in_left)
    grad_front, = in_front_back((jnp.stack((grad_left, grad_right)).astype(jnp.bfloat16), grad_gate))
    grad_mid = (grad_inner.astype(jnp.float32) + grad_front.astype(jnp.float32)).astype(jnp.bfloat16)
    grad_mixed, grad_gate, grad_inner = out_finish_back(grad_mid)
    signal = rounded(grad_mixed)
    grad_left = jnp.einsum('ijc,jkc->ikc', signal, out_right)
    grad_right = jnp.einsum('ijc,ikc->jkc', signal, out_left)
    grad_front, = out_front_back((jnp.stack((grad_left, grad_right)).astype(jnp.bfloat16), grad_gate))
    return (grad_inner.astype(jnp.float32) + grad_front.astype(jnp.float32)).astype(jnp.bfloat16)
```

```python
import functools

import jax
import jax.numpy as jnp
from jax import lax
from jax.experimental import pallas as pl
from jax.experimental.pallas import tpu as pltpu
from jax.sharding import PartitionSpec as P

H = 128
EPS = 1e-05
VMEM_BUDGET = 40 << 20
F32 = jnp.float32
BF16 = jnp.bfloat16


def from_root(array, axis, root):
    mine = lax.axis_index(axis) == root
    return lax.psum(jnp.where(mine, array, jnp.zeros_like(array)), axis)


def layer_norm(values):
    centred = values - jnp.mean(values, axis=-1, keepdims=True)
    spread = jnp.mean(centred * centred, axis=-1, keepdims=True)
    return centred * lax.rsqrt(spread + 1e-05)


def project_pair(inner_pair, mask_pair, weight):
    normed = layer_norm(inner_pair.astype(jnp.float32)).astype(jnp.bfloat16)
    linear = jnp.dot(normed, weight, preferred_element_type=jnp.float32)
    left_side = jax.nn.sigmoid(linear[..., :H]) * linear[..., H : 2 * H]
    right_side = jax.nn.sigmoid(linear[..., 2 * H : 3 * H]) * linear[..., 3 * H : 4 * H]
    operands = (jnp.stack((left_side, right_side)) * mask_pair[None, :, :, None]).astype(
        jnp.bfloat16
    )
    return (operands, jax.nn.sigmoid(linear[..., 4 * H :]))


def finish(mixed_part, gate_value, inner_pair, weight):
    normed = layer_norm(mixed_part).astype(jnp.bfloat16)
    update = jnp.dot(normed, weight, preferred_element_type=jnp.float32)
    return (inner_pair.astype(jnp.float32) + gate_value * update).astype(jnp.bfloat16)


def spread_body(pair_act, cotangent, residue_mask, front_weight, out_weight):
    local_rows = pair_act.shape[0]
    local_cols = pair_act.shape[1]
    row_index = lax.axis_index("row")
    col_index = lax.axis_index("col")
    block_rows = lax.axis_size("row") // lax.axis_size("col")
    owner_col = row_index // block_rows
    offset = row_index % block_rows * local_rows
    chain_mask = residue_mask.astype(jnp.float32)
    mask_rows = lax.dynamic_slice_in_dim(chain_mask, row_index * local_rows, local_rows)
    mask_cols = lax.dynamic_slice_in_dim(chain_mask, col_index * local_cols, local_cols)
    mask_pair = mask_rows[:, None] * mask_cols[None, :]

    def gather_rows(stacked):
        return lax.all_gather(stacked, "row", axis=1, tiled=True)

    def column_block(gathered):
        slab = lax.dynamic_slice_in_dim(gathered, offset, local_rows, 1)
        return from_root(slab, "col", owner_col)

    def gather_cols(values):
        return lax.all_gather(values, "col", axis=1, tiled=True)

    def sum_cols(partial_term):
        return lax.psum_scatter(
            partial_term.astype(jnp.bfloat16), "col", scatter_dimension=1, tiled=True
        ).astype(jnp.float32)

    (out_ops, out_gate), out_front_back = jax.vjp(
        lambda inner_pair: project_pair(inner_pair, mask_pair, front_weight[0]), pair_act
    )
    fetched = gather_rows(out_ops)
    out_mixed = sum_cols(
        jnp.einsum("ikc,jkc->ijc", out_ops[0], fetched[-1], preferred_element_type=jnp.float32)
    )
    pair_mid, out_finish_back = jax.vjp(
        lambda mixed_part, gate_value, inner_pair: finish(
            mixed_part, gate_value, inner_pair, out_weight[0]
        ),
        out_mixed,
        out_gate,
        pair_act,
    )
    (in_ops, in_gate), in_front_back = jax.vjp(
        lambda inner_pair: project_pair(inner_pair, mask_pair, front_weight[1]), pair_mid
    )
    in_fetched = gather_rows(in_ops)
    left_block = column_block(in_fetched[0])
    in_mixed = jnp.einsum(
        "kic,kjc->ijc", left_block, in_fetched[1], preferred_element_type=jnp.float32
    )
    unused_pair, in_finish_back = jax.vjp(
        lambda mixed_part, gate_value, inner_pair: finish(
            mixed_part, gate_value, inner_pair, out_weight[1]
        ),
        in_mixed,
        in_gate,
        pair_mid,
    )
    grad_mixed, grad_gate, grad_inner = in_finish_back(cotangent)
    signal = grad_mixed.astype(jnp.bfloat16)
    signal_rows = gather_rows(signal[None])[0]
    left_rows = gather_cols(in_ops[0])
    grad_right = jnp.einsum(
        "kic,ijc->kjc", left_rows, signal_rows, preferred_element_type=jnp.float32
    )
    grad_left = sum_cols(
        jnp.einsum("kjc,ijc->kic", in_ops[1], signal_rows, preferred_element_type=jnp.float32)
    )
    (grad_front,) = in_front_back(
        (jnp.stack((grad_left, grad_right)).astype(jnp.bfloat16), grad_gate)
    )
    grad_mid = (grad_inner.astype(jnp.float32) + grad_front.astype(jnp.float32)).astype(
        jnp.bfloat16
    )
    grad_mixed, grad_gate, grad_inner = out_finish_back(grad_mid)
    signal = grad_mixed.astype(jnp.bfloat16)
    signal_cols = gather_cols(signal)
    grad_left = jnp.einsum(
        "ijc,jkc->ikc", signal_cols, fetched[-1], preferred_element_type=jnp.float32
    )
    signal_block = column_block(gather_rows(signal[None])[0])
    grad_right = jnp.einsum(
        "ijc,ikc->jkc", signal_block, fetched[0], preferred_element_type=jnp.float32
    )
    (grad_front,) = out_front_back(
        (jnp.stack((grad_left, grad_right)).astype(jnp.bfloat16), grad_gate)
    )
    return (grad_inner.astype(jnp.float32) + grad_front.astype(jnp.float32)).astype(jnp.bfloat16)


def sigmoid(values):
    return 0.5 + 0.5 * jnp.tanh(0.5 * values)


def lane_mean(values):
    return jnp.mean(values, axis=-1, keepdims=True)


def normalize(values):
    centred = values - lane_mean(values)
    inverse = lax.rsqrt(lane_mean(centred * centred) + EPS)
    return centred * inverse, inverse


def normalize_back(grad, normed, inverse):
    return inverse * (grad - lane_mean(grad) - normed * lane_mean(grad * normed))


def rounded(values):
    return values.astype(BF16).astype(F32)


def matmul(values, weight):
    return jnp.dot(values.astype(BF16), weight, preferred_element_type=F32)


def matmul_t(values, weight):
    return lax.dot_general(
        values.astype(BF16), weight, (((1,), (1,)), ((), ())), preferred_element_type=F32
    )


def split(linear):
    return [linear[:, i * H : (i + 1) * H] for i in range(5)]


def front_back(linear, mask, grad_left, grad_right, grad_gate, weight, normed, inverse):
    gate_l, val_l, gate_r, val_r, gate = split(linear)
    gate_l, gate_r, gate = sigmoid(gate_l), sigmoid(gate_r), sigmoid(gate)
    grad_left, grad_right = grad_left * mask, grad_right * mask
    pieces = (
        grad_left * val_l * (gate_l * (1.0 - gate_l)),
        grad_left * gate_l,
        grad_right * val_r * (gate_r * (1.0 - gate_r)),
        grad_right * gate_r,
        grad_gate * (gate * (1.0 - gate)),
    )
    grad = jnp.concatenate([piece.astype(BF16) for piece in pieces], axis=1)
    return rounded(normalize_back(rounded(matmul_t(grad, weight)), normed, inverse))


def crop_kernel(
    n, rows, cols, blocks, mask_ref, own_ref, other_ref, front_ref, out_ref, grad_ref,
    act, cot, left, right, right_t, gate0, mixed0, mid, left1, right1, left1_t, right1_t,
    gate1, mixed1, sig, sig_t, grow, s_mid, s_sig, dl, dr,
):
    row_index = lax.axis_index("row")
    col_index = lax.axis_index("col")
    chain = lax.fori_loop(0, n, lambda i, total: total + mask_ref[i], jnp.int32(0))
    first = pl.multiple_of(row_index * rows * n, rows * n)
    mine = pl.multiple_of(col_index * cols, cols)
    theirs = pl.multiple_of((1 - col_index) * cols, cols)
    step = rows * n

    for position, block in enumerate(blocks):
        place = (row_index ^ block) * rows
        for a in range(rows):
            base = (place + a) * n
            for source, offset in ((own_ref, mine), (other_ref, theirs)):
                where = pl.ds(pl.multiple_of(base + offset, cols), cols)
                act[where, :] = source[position, 0, a].astype(F32)
                cot[where, :] = source[position, 1, a].astype(F32)

    def mask_of(start_row):
        major = lax.broadcasted_iota(jnp.int32, (rows, n, H), 0) + start_row
        minor = lax.broadcasted_iota(jnp.int32, (rows, n, H), 1)
        return jnp.where((major < chain) & (minor < chain), 1.0, 0.0).reshape(step, H)

    def chunk(c):
        return pl.ds(pl.multiple_of(c * step, step), step)

    def put_t(ref, c, values):
        for a in range(rows):
            ref[pl.ds(c * rows + a, n, stride=n), :] = values[a * n : (a + 1) * n]

    def get_t(ref):
        return jnp.concatenate(
            [ref[pl.ds(row_index * rows + a, n, stride=n), :] for a in range(rows)], axis=0
        )

    def projection(u, source, c):
        mask = mask_of(c * rows)
        normed, _ = normalize(source)
        linear = matmul(normed, front_ref[u])
        gate_l, val_l, gate_r, val_r, gate = split(linear)
        return (
            rounded(mask * (sigmoid(gate_l) * val_l)),
            rounded(mask * (sigmoid(gate_r) * val_r)),
            sigmoid(gate),
        )

    def front0(c, _):
        a, b, g = projection(0, act[chunk(c), :], c)
        left[chunk(c), :] = a
        right[chunk(c), :] = b
        put_t(right_t, c, b)
        gate0[chunk(c), :] = g
        return 0

    lax.fori_loop(0, n // rows, front0, 0)

    def bcast(ref, index):
        return jnp.broadcast_to(ref[pl.ds(index, 1), :], (n, H))

    def product(count, span, row_of, ref_a, ref_b, minor, width):
        totals = [None] * count
        for s in range(span):
            block = ref_b[pl.ds(s * n + minor, width), :]
            for p in range(count):
                term = jnp.broadcast_to(ref_a[pl.ds(row_of(p, s), 1), :], (width, H)) * block
                totals[p] = term if totals[p] is None else totals[p] + term
        return totals

    def triangle0(c, _):
        totals = product(rows, n, lambda p, s: (c * rows + p) * n + s, left, right_t, 0, n)
        mixed0[chunk(c), :] = jnp.concatenate(totals, axis=0)
        return 0

    lax.fori_loop(0, n // rows, triangle0, 0)

    def middle(c, _):
        normed, _ = normalize(mixed0[chunk(c), :])
        update = matmul(normed, out_ref[0])
        value = rounded(act[chunk(c), :] + gate0[chunk(c), :] * update)
        mid[chunk(c), :] = value
        a, b, g = projection(1, value, c)
        left1[chunk(c), :] = a
        right1[chunk(c), :] = b
        put_t(left1_t, c, a)
        put_t(right1_t, c, b)
        gate1[chunk(c), :] = g
        return 0

    lax.fori_loop(0, n // rows, middle, 0)

    def triangle1(c, _):
        totals = product(rows, n, lambda p, s: s * n + c * rows + p, left1, right1, 0, n)
        mixed1[chunk(c), :] = jnp.concatenate(totals, axis=0)
        return 0

    lax.fori_loop(0, n // rows, triangle1, 0)

    def signal1(c, _):
        normed, inverse = normalize(mixed1[chunk(c), :])
        grad = rounded(matmul_t(cot[chunk(c), :] * gate1[chunk(c), :], out_ref[1]))
        value = rounded(normalize_back(grad, normed, inverse))
        sig[chunk(c), :] = value
        put_t(sig_t, c, value)
        return 0

    lax.fori_loop(0, n // rows, signal1, 0)

    me = row_index * rows
    dl[pl.ds(0, step), :] = jnp.concatenate(
        product(rows, n, lambda p, s: (me + p) * n + s, right1, sig_t, 0, n), axis=0)
    dl[pl.ds(step, step), :] = jnp.concatenate(
        product(rows, n, lambda p, s: (me + p) * n + s, sig, right1_t, 0, n), axis=0)
    dr[pl.ds(0, step), :] = jnp.concatenate(
        product(rows, n, lambda p, s: (me + p) * n + s, left1, sig, 0, n), axis=0)
    dr[pl.ds(step, step), :] = jnp.concatenate(
        product(rows, n, lambda p, s: s * n + me + p, sig, left1_t, 0, n), axis=0)

    mask_rows = mask_of(me)
    for half in range(2):
        def take(ref):
            return ref[pl.ds(first, step), :] if half == 0 else get_t(ref)

        here = pl.ds(half * step, step)
        cot_s = take(cot)
        mixed, _ = normalize(take(mixed1))
        normed, inverse = normalize(take(mid))
        grad_gate = cot_s * matmul(mixed, out_ref[1])
        grad = front_back(
            matmul(normed, front_ref[1]), mask_rows, rounded(dl[here, :]), rounded(dr[here, :]),
            grad_gate, front_ref[1], normed, inverse)
        grad_mid = rounded(cot_s + grad)
        mixed, inverse = normalize(take(mixed0))
        if half == 0:
            grow[...] = grad_mid
            s_mid[...] = grad_mid * matmul(mixed, out_ref[0])
        grad = rounded(matmul_t(grad_mid * take(gate0), out_ref[0]))
        s_sig[here, :] = rounded(normalize_back(grad, mixed, inverse))

    grad_left = product(rows, n, lambda p, s: p * n + s, s_sig, right, mine, cols)
    grad_right = product(rows, n, lambda p, s: step + p * n + s, s_sig, left, mine, cols)

    def own(ref, base):
        return jnp.concatenate(
            [ref[pl.ds(base + a * n + mine, cols), :] for a in range(rows)], axis=0)

    major = lax.broadcasted_iota(jnp.int32, (rows, cols, H), 0) + me
    minor = lax.broadcasted_iota(jnp.int32, (rows, cols, H), 1) + mine
    mask = jnp.where((major < chain) & (minor < chain), 1.0, 0.0).reshape(rows * cols, H)
    normed, inverse = normalize(own(act, first))
    grad = front_back(
        matmul(normed, front_ref[0]), mask,
        rounded(jnp.concatenate(grad_left, axis=0)), rounded(jnp.concatenate(grad_right, axis=0)),
        own(s_mid, 0), front_ref[0], normed, inverse)
    grad_ref[...] = (own(grow, 0) + grad).astype(BF16).reshape(rows, cols, H)


def whole_body(pair_act, cotangent, residue_mask, front_weight, out_weight):
    rows, cols, width = pair_act.shape
    n = residue_mask.shape[0]
    row_count, col_count = lax.axis_size("row"), lax.axis_size("col")
    bits = row_count.bit_length() - 1
    gathered = jnp.stack((pair_act, cotangent))[None]
    blocks = [0]
    for bit in [1 << b for b in range(1, bits)] + [1]:
        other = lax.ppermute(gathered, "row", [(i, i ^ bit) for i in range(row_count)])
        gathered = jnp.concatenate((gathered, other))
        blocks = blocks + [b ^ bit for b in blocks]
    other = lax.ppermute(gathered, "col", [(0, 1), (1, 0)])
    full = pltpu.VMEM((n * n, H), F32)
    some = pltpu.VMEM((rows * n, H), F32)
    twice = pltpu.VMEM((2 * rows * n, H), F32)
    vmem = pl.BlockSpec(memory_space=pltpu.VMEM)
    return pl.pallas_call(
        functools.partial(crop_kernel, n, rows, cols, blocks),
        out_shape=jax.ShapeDtypeStruct(pair_act.shape, BF16),
        in_specs=[pl.BlockSpec(memory_space=pltpu.SMEM)] + [vmem] * 4,
        out_specs=vmem,
        scratch_shapes=[full] * 16 + [some, some, twice, twice, twice],
        compiler_params=pltpu.CompilerParams(vmem_limit_bytes=VMEM_BUDGET),
        interpret=INTERPRET,
    )(residue_mask, gathered, other, front_weight, out_weight)


INTERPRET = False


def body(pair_act, cotangent, residue_mask, front_weight, out_weight):
    n = residue_mask.shape[0]
    row_count = lax.axis_size("row")
    fits = 20 * n * n * H * 4 <= VMEM_BUDGET
    doubling = row_count & (row_count - 1) == 0 and lax.axis_size("col") == 2
    run = whole_body if fits and doubling else spread_body
    return run(pair_act, cotangent, residue_mask, front_weight, out_weight)


def solution(mesh):
    placed = (P(("grp", "row"), "col", None), P(("grp", "row"), "col", None), P("grp"), P(), P())
    return jax.shard_map(
        body, mesh=mesh, in_specs=placed, out_specs=P(("grp", "row"), "col", None), check_vma=False
    )
```

```python
import functools

import jax
import jax.numpy as jnp
from jax import lax
from jax.experimental import pallas as pl
from jax.experimental.pallas import tpu as pltpu
from jax.sharding import PartitionSpec as P

H = 128
EPS = 1e-05
PAD = 4
GROUPS = 2
VMEM_BUDGET = 40 << 20
F32 = jnp.float32
BF16 = jnp.bfloat16


def from_root(array, axis, root):
    mine = lax.axis_index(axis) == root
    return lax.psum(jnp.where(mine, array, jnp.zeros_like(array)), axis)


def layer_norm(values):
    centred = values - jnp.mean(values, axis=-1, keepdims=True)
    spread = jnp.mean(centred * centred, axis=-1, keepdims=True)
    return centred * lax.rsqrt(spread + 1e-05)


def project_pair(inner_pair, mask_pair, weight):
    normed = layer_norm(inner_pair.astype(jnp.float32)).astype(jnp.bfloat16)
    linear = jnp.dot(normed, weight, preferred_element_type=jnp.float32)
    left_side = jax.nn.sigmoid(linear[..., :H]) * linear[..., H : 2 * H]
    right_side = jax.nn.sigmoid(linear[..., 2 * H : 3 * H]) * linear[..., 3 * H : 4 * H]
    operands = (jnp.stack((left_side, right_side)) * mask_pair[None, :, :, None]).astype(
        jnp.bfloat16
    )
    return (operands, jax.nn.sigmoid(linear[..., 4 * H :]))


def finish(mixed_part, gate_value, inner_pair, weight):
    normed = layer_norm(mixed_part).astype(jnp.bfloat16)
    update = jnp.dot(normed, weight, preferred_element_type=jnp.float32)
    return (inner_pair.astype(jnp.float32) + gate_value * update).astype(jnp.bfloat16)


def spread_body(pair_act, cotangent, residue_mask, front_weight, out_weight):
    local_rows = pair_act.shape[0]
    local_cols = pair_act.shape[1]
    row_index = lax.axis_index("row")
    col_index = lax.axis_index("col")
    block_rows = lax.axis_size("row") // lax.axis_size("col")
    owner_col = row_index // block_rows
    offset = row_index % block_rows * local_rows
    chain_mask = residue_mask.astype(jnp.float32)
    mask_rows = lax.dynamic_slice_in_dim(chain_mask, row_index * local_rows, local_rows)
    mask_cols = lax.dynamic_slice_in_dim(chain_mask, col_index * local_cols, local_cols)
    mask_pair = mask_rows[:, None] * mask_cols[None, :]

    def gather_rows(stacked):
        return lax.all_gather(stacked, "row", axis=1, tiled=True)

    def column_block(gathered):
        slab = lax.dynamic_slice_in_dim(gathered, offset, local_rows, 1)
        return from_root(slab, "col", owner_col)

    def gather_cols(values):
        return lax.all_gather(values, "col", axis=1, tiled=True)

    def sum_cols(partial_term):
        return lax.psum_scatter(
            partial_term.astype(jnp.bfloat16), "col", scatter_dimension=1, tiled=True
        ).astype(jnp.float32)

    (out_ops, out_gate), out_front_back = jax.vjp(
        lambda inner_pair: project_pair(inner_pair, mask_pair, front_weight[0]), pair_act
    )
    fetched = gather_rows(out_ops)
    out_mixed = sum_cols(
        jnp.einsum("ikc,jkc->ijc", out_ops[0], fetched[-1], preferred_element_type=jnp.float32)
    )
    pair_mid, out_finish_back = jax.vjp(
        lambda mixed_part, gate_value, inner_pair: finish(
            mixed_part, gate_value, inner_pair, out_weight[0]
        ),
        out_mixed,
        out_gate,
        pair_act,
    )
    (in_ops, in_gate), in_front_back = jax.vjp(
        lambda inner_pair: project_pair(inner_pair, mask_pair, front_weight[1]), pair_mid
    )
    in_fetched = gather_rows(in_ops)
    left_block = column_block(in_fetched[0])
    in_mixed = jnp.einsum(
        "kic,kjc->ijc", left_block, in_fetched[1], preferred_element_type=jnp.float32
    )
    unused_pair, in_finish_back = jax.vjp(
        lambda mixed_part, gate_value, inner_pair: finish(
            mixed_part, gate_value, inner_pair, out_weight[1]
        ),
        in_mixed,
        in_gate,
        pair_mid,
    )
    grad_mixed, grad_gate, grad_inner = in_finish_back(cotangent)
    signal = grad_mixed.astype(jnp.bfloat16)
    signal_rows = gather_rows(signal[None])[0]
    left_rows = gather_cols(in_ops[0])
    grad_right = jnp.einsum(
        "kic,ijc->kjc", left_rows, signal_rows, preferred_element_type=jnp.float32
    )
    grad_left = sum_cols(
        jnp.einsum("kjc,ijc->kic", in_ops[1], signal_rows, preferred_element_type=jnp.float32)
    )
    (grad_front,) = in_front_back(
        (jnp.stack((grad_left, grad_right)).astype(jnp.bfloat16), grad_gate)
    )
    grad_mid = (grad_inner.astype(jnp.float32) + grad_front.astype(jnp.float32)).astype(
        jnp.bfloat16
    )
    grad_mixed, grad_gate, grad_inner = out_finish_back(grad_mid)
    signal = grad_mixed.astype(jnp.bfloat16)
    signal_cols = gather_cols(signal)
    grad_left = jnp.einsum(
        "ijc,jkc->ikc", signal_cols, fetched[-1], preferred_element_type=jnp.float32
    )
    signal_block = column_block(gather_rows(signal[None])[0])
    grad_right = jnp.einsum(
        "ijc,ikc->jkc", signal_block, fetched[0], preferred_element_type=jnp.float32
    )
    (grad_front,) = out_front_back(
        (jnp.stack((grad_left, grad_right)).astype(jnp.bfloat16), grad_gate)
    )
    return (grad_inner.astype(jnp.float32) + grad_front.astype(jnp.float32)).astype(jnp.bfloat16)


def sigmoid(values):
    return 0.5 + 0.5 * jnp.tanh(0.5 * values)


def lane_mean(values):
    return jnp.mean(values, axis=-1, keepdims=True)


def normalize(values):
    centred = values - lane_mean(values)
    inverse = lax.rsqrt(lane_mean(centred * centred) + EPS)
    return centred * inverse, inverse


def normalize_back(grad, normed, inverse):
    return inverse * (grad - lane_mean(grad) - normed * lane_mean(grad * normed))


def rounded(values):
    return values.astype(BF16).astype(F32)


def matmul(values, weight):
    return jnp.dot(values.astype(BF16), weight, preferred_element_type=F32)


def matmul_t(values, weight):
    return lax.dot_general(
        values.astype(BF16), weight, (((1,), (1,)), ((), ())), preferred_element_type=F32
    )


def split(linear):
    return [linear[:, i * H : (i + 1) * H] for i in range(5)]


def front_back(linear, mask, grad_left, grad_right, grad_gate, weight, normed, inverse):
    gate_l, val_l, gate_r, val_r, gate = split(linear)
    gate_l, gate_r, gate = sigmoid(gate_l), sigmoid(gate_r), sigmoid(gate)
    grad_left, grad_right = grad_left * mask, grad_right * mask
    pieces = (
        grad_left * val_l * (gate_l * (1.0 - gate_l)),
        grad_left * gate_l,
        grad_right * val_r * (gate_r * (1.0 - gate_r)),
        grad_right * gate_r,
        grad_gate * (gate * (1.0 - gate)),
    )
    grad = jnp.concatenate([piece.astype(BF16) for piece in pieces], axis=1)
    return rounded(normalize_back(rounded(matmul_t(grad, weight)), normed, inverse))


def crop_kernel(
    n, rows, cols, blocks, mask_ref, own_ref, other_ref, front_ref, out_ref, grad_ref,
    act, cot, left, right, right_t, gate0, mixed0, mid, left1, right1, left1_t, right1_t,
    gate1, mixed1, sig, sig_t, grow, s_gate, s_sig, dl, dr,
):
    pitch = n + PAD
    group = n // GROUPS
    row_index = lax.axis_index("row")
    col_index = lax.axis_index("col")
    chain = sum(mask_ref[i] for i in range(n))
    me = row_index * rows
    mine = pl.multiple_of(col_index * cols, cols)
    theirs = pl.multiple_of((1 - col_index) * cols, cols)
    step = rows * n

    for position, block in enumerate(blocks):
        place = (row_index ^ block) * rows
        for a in range(rows):
            base = (place + a) * pitch
            for source, offset in ((own_ref, mine), (other_ref, theirs)):
                where = pl.ds(base + offset, cols)
                act[where, :] = source[position, 0, a].astype(F32)
                cot[where, :] = source[position, 1, a].astype(F32)

    def mask_of(count, span, start, offset):
        major = lax.broadcasted_iota(jnp.int32, (count, span, H), 0) + start
        minor = lax.broadcasted_iota(jnp.int32, (count, span, H), 1) + offset
        return jnp.where((major < chain) & (minor < chain), 1.0, 0.0).reshape(count * span, H)

    def get(ref, start, count=group):
        return jnp.concatenate(
            [ref[pl.ds((start + a) * pitch, n), :] for a in range(count)], axis=0
        )

    def put(ref, start, values, count=group):
        for a in range(count):
            ref[pl.ds((start + a) * pitch, n), :] = values[a * n : (a + 1) * n]

    def put_t(ref, start, values, count=group):
        for a in range(count):
            ref[pl.ds(start + a, n, stride=pitch), :] = values[a * n : (a + 1) * n]

    def get_t(ref):
        return [ref[pl.ds(me + a, n, stride=pitch), :] for a in range(rows)]

    def take(ref):
        return jnp.concatenate([get(ref, me, rows)] + get_t(ref), axis=0)

    def projection(u, source, start):
        mask = mask_of(group, n, start, 0)
        normed, _ = normalize(source)
        linear = matmul(normed, front_ref[u])
        gate_l, val_l, gate_r, val_r, gate = split(linear)
        return (
            rounded(mask * (sigmoid(gate_l) * val_l)),
            rounded(mask * (sigmoid(gate_r) * val_r)),
            sigmoid(gate),
        )

    def product(count, span, row_of, ref_a, ref_b, minor, width, pitch_b=pitch):
        totals = [None] * count
        for s in range(span):
            block = ref_b[pl.ds(s * pitch_b + minor, width), :]
            for p in range(count):
                term = jnp.broadcast_to(ref_a[pl.ds(row_of(p, s), 1), :], (width, H)) * block
                totals[p] = term if totals[p] is None else totals[p] + term
        return totals

    def front0(c, _):
        start = c * group
        a, b, g = projection(0, get(act, start), start)
        put(left, start, a)
        put(right, start, b)
        put_t(right_t, start, b)
        put(gate0, start, g)
        return 0

    lax.fori_loop(0, GROUPS, front0, 0)

    def triangle0(c, _):
        start = c * rows
        totals = product(rows, n, lambda p, s: (start + p) * pitch + s, left, right_t, 0, n)
        put(mixed0, start, jnp.concatenate(totals, axis=0), rows)
        return 0

    lax.fori_loop(0, n // rows, triangle0, 0)

    def middle(c, _):
        start = c * group
        normed, _ = normalize(get(mixed0, start))
        update = matmul(normed, out_ref[0])
        value = rounded(get(act, start) + get(gate0, start) * update)
        put(mid, start, value)
        a, b, g = projection(1, value, start)
        put(left1, start, a)
        put(right1, start, b)
        put_t(left1_t, start, a)
        put_t(right1_t, start, b)
        put(gate1, start, g)
        return 0

    lax.fori_loop(0, GROUPS, middle, 0)

    def triangle1(c, _):
        start = c * rows
        totals = product(rows, n, lambda p, s: s * pitch + start + p, left1, right1, 0, n)
        put(mixed1, start, jnp.concatenate(totals, axis=0), rows)
        return 0

    lax.fori_loop(0, n // rows, triangle1, 0)

    def signal1(c, _):
        start = c * group
        normed, inverse = normalize(get(mixed1, start))
        grad = rounded(matmul_t(get(cot, start) * get(gate1, start), out_ref[1]))
        value = rounded(normalize_back(grad, normed, inverse))
        put(sig, start, value)
        put_t(sig_t, start, value)
        return 0

    lax.fori_loop(0, GROUPS, signal1, 0)

    def row_of(p, s):
        return (me + p) * pitch + s

    dl[pl.ds(0, step), :] = jnp.concatenate(
        product(rows, n, row_of, right1, sig_t, 0, n), axis=0)
    dl[pl.ds(step, step), :] = jnp.concatenate(
        product(rows, n, row_of, sig, right1_t, 0, n), axis=0)
    dr[pl.ds(0, step), :] = jnp.concatenate(
        product(rows, n, row_of, left1, sig, 0, n), axis=0)
    dr[pl.ds(step, step), :] = jnp.concatenate(
        product(rows, n, lambda p, s: s * pitch + me + p, sig, left1_t, 0, n), axis=0)

    mask_rows = mask_of(rows, n, me, 0)
    cot_s = take(cot)
    mixed, _ = normalize(take(mixed1))
    normed, inverse = normalize(take(mid))
    grad_gate = cot_s * matmul(mixed, out_ref[1])
    grad = front_back(
        matmul(normed, front_ref[1]), jnp.concatenate([mask_rows, mask_rows], axis=0),
        rounded(dl[...]), rounded(dr[...]), grad_gate, front_ref[1], normed, inverse)
    grad_mid = rounded(cot_s + grad)
    mixed, inverse = normalize(take(mixed0))
    grow[...] = grad_mid[:step]
    s_gate[...] = grad_mid[:step] * matmul(mixed[:step], out_ref[0])
    grad = rounded(matmul_t(grad_mid * take(gate0), out_ref[0]))
    s_sig[...] = rounded(normalize_back(grad, mixed, inverse))

    grad_left = product(rows, n, lambda p, s: p * n + s, s_sig, right, mine, cols)
    grad_right = product(rows, n, lambda p, s: step + p * n + s, s_sig, left, mine, cols)

    def own(ref, base, stride):
        return jnp.concatenate(
            [ref[pl.ds(base + a * stride + mine, cols), :] for a in range(rows)], axis=0)

    normed, inverse = normalize(own(act, me * pitch, pitch))
    grad = front_back(
        matmul(normed, front_ref[0]), mask_of(rows, cols, me, mine),
        rounded(jnp.concatenate(grad_left, axis=0)), rounded(jnp.concatenate(grad_right, axis=0)),
        own(s_gate, 0, n), front_ref[0], normed, inverse)
    grad_ref[...] = (own(grow, 0, n) + grad).astype(BF16).reshape(rows, cols, H)


def whole_body(pair_act, cotangent, residue_mask, front_weight, out_weight):
    rows, cols, width = pair_act.shape
    n = residue_mask.shape[0]
    row_count, col_count = lax.axis_size("row"), lax.axis_size("col")
    bits = row_count.bit_length() - 1
    gathered = jnp.stack((pair_act, cotangent))[None]
    blocks = [0]
    for bit in [1 << b for b in range(1, bits)] + [1]:
        other = lax.ppermute(gathered, "row", [(i, i ^ bit) for i in range(row_count)])
        gathered = jnp.concatenate((gathered, other))
        blocks = blocks + [b ^ bit for b in blocks]
    other = lax.ppermute(gathered, "col", [(0, 1), (1, 0)])
    full = pltpu.VMEM((n * (n + PAD), H), F32)
    some = pltpu.VMEM((rows * n, H), F32)
    twice = pltpu.VMEM((2 * rows * n, H), F32)
    vmem = pl.BlockSpec(memory_space=pltpu.VMEM)
    return pl.pallas_call(
        functools.partial(crop_kernel, n, rows, cols, blocks),
        out_shape=jax.ShapeDtypeStruct(pair_act.shape, BF16),
        in_specs=[pl.BlockSpec(memory_space=pltpu.SMEM)] + [vmem] * 4,
        out_specs=vmem,
        scratch_shapes=[full] * 16 + [some, some, twice, twice, twice],
        compiler_params=pltpu.CompilerParams(vmem_limit_bytes=VMEM_BUDGET),
    )(residue_mask, gathered, other, front_weight, out_weight)


def body(pair_act, cotangent, residue_mask, front_weight, out_weight):
    n = residue_mask.shape[0]
    row_count = lax.axis_size("row")
    fits = 20 * n * (n + PAD) * H * 4 <= VMEM_BUDGET
    doubling = row_count & (row_count - 1) == 0 and lax.axis_size("col") == 2
    run = whole_body if fits and doubling else spread_body
    return run(pair_act, cotangent, residue_mask, front_weight, out_weight)


def solution(mesh):
    placed = (P(("grp", "row"), "col", None), P(("grp", "row"), "col", None), P("grp"), P(), P())
    return jax.shard_map(
        body, mesh=mesh, in_specs=placed, out_specs=P(("grp", "row"), "col", None), check_vma=False
    )
```

```python
import functools

import jax
import jax.numpy as jnp
from jax import lax
from jax.experimental import pallas as pl
from jax.experimental.pallas import tpu as pltpu
from jax.sharding import PartitionSpec as P

H = 128
EPS = 1e-05
PAD = 4
GROUPS = 2
VMEM_BUDGET = 40 << 20
F32 = jnp.float32
BF16 = jnp.bfloat16


def from_root(array, axis, root):
    mine = lax.axis_index(axis) == root
    return lax.psum(jnp.where(mine, array, jnp.zeros_like(array)), axis)


def layer_norm(values):
    centred = values - jnp.mean(values, axis=-1, keepdims=True)
    spread = jnp.mean(centred * centred, axis=-1, keepdims=True)
    return centred * lax.rsqrt(spread + 1e-05)


def project_pair(inner_pair, mask_pair, weight):
    normed = layer_norm(inner_pair.astype(jnp.float32)).astype(jnp.bfloat16)
    linear = jnp.dot(normed, weight, preferred_element_type=jnp.float32)
    left_side = jax.nn.sigmoid(linear[..., :H]) * linear[..., H : 2 * H]
    right_side = jax.nn.sigmoid(linear[..., 2 * H : 3 * H]) * linear[..., 3 * H : 4 * H]
    operands = (jnp.stack((left_side, right_side)) * mask_pair[None, :, :, None]).astype(
        jnp.bfloat16
    )
    return (operands, jax.nn.sigmoid(linear[..., 4 * H :]))


def finish(mixed_part, gate_value, inner_pair, weight):
    normed = layer_norm(mixed_part).astype(jnp.bfloat16)
    update = jnp.dot(normed, weight, preferred_element_type=jnp.float32)
    return (inner_pair.astype(jnp.float32) + gate_value * update).astype(jnp.bfloat16)


def spread_body(pair_act, cotangent, residue_mask, front_weight, out_weight):
    local_rows = pair_act.shape[0]
    local_cols = pair_act.shape[1]
    row_index = lax.axis_index("row")
    col_index = lax.axis_index("col")
    block_rows = lax.axis_size("row") // lax.axis_size("col")
    owner_col = row_index // block_rows
    offset = row_index % block_rows * local_rows
    chain_mask = residue_mask.astype(jnp.float32)
    mask_rows = lax.dynamic_slice_in_dim(chain_mask, row_index * local_rows, local_rows)
    mask_cols = lax.dynamic_slice_in_dim(chain_mask, col_index * local_cols, local_cols)
    mask_pair = mask_rows[:, None] * mask_cols[None, :]

    def gather_rows(stacked):
        return lax.all_gather(stacked, "row", axis=1, tiled=True)

    def column_block(gathered):
        slab = lax.dynamic_slice_in_dim(gathered, offset, local_rows, 1)
        return from_root(slab, "col", owner_col)

    def gather_cols(values):
        return lax.all_gather(values, "col", axis=1, tiled=True)

    def sum_cols(partial_term):
        return lax.psum_scatter(
            partial_term.astype(jnp.bfloat16), "col", scatter_dimension=1, tiled=True
        ).astype(jnp.float32)

    (out_ops, out_gate), out_front_back = jax.vjp(
        lambda inner_pair: project_pair(inner_pair, mask_pair, front_weight[0]), pair_act
    )
    fetched = gather_rows(out_ops)
    out_mixed = sum_cols(
        jnp.einsum("ikc,jkc->ijc", out_ops[0], fetched[-1], preferred_element_type=jnp.float32)
    )
    pair_mid, out_finish_back = jax.vjp(
        lambda mixed_part, gate_value, inner_pair: finish(
            mixed_part, gate_value, inner_pair, out_weight[0]
        ),
        out_mixed,
        out_gate,
        pair_act,
    )
    (in_ops, in_gate), in_front_back = jax.vjp(
        lambda inner_pair: project_pair(inner_pair, mask_pair, front_weight[1]), pair_mid
    )
    in_fetched = gather_rows(in_ops)
    left_block = column_block(in_fetched[0])
    in_mixed = jnp.einsum(
        "kic,kjc->ijc", left_block, in_fetched[1], preferred_element_type=jnp.float32
    )
    unused_pair, in_finish_back = jax.vjp(
        lambda mixed_part, gate_value, inner_pair: finish(
            mixed_part, gate_value, inner_pair, out_weight[1]
        ),
        in_mixed,
        in_gate,
        pair_mid,
    )
    grad_mixed, grad_gate, grad_inner = in_finish_back(cotangent)
    signal = grad_mixed.astype(jnp.bfloat16)
    signal_rows = gather_rows(signal[None])[0]
    left_rows = gather_cols(in_ops[0])
    grad_right = jnp.einsum(
        "kic,ijc->kjc", left_rows, signal_rows, preferred_element_type=jnp.float32
    )
    grad_left = sum_cols(
        jnp.einsum("kjc,ijc->kic", in_ops[1], signal_rows, preferred_element_type=jnp.float32)
    )
    (grad_front,) = in_front_back(
        (jnp.stack((grad_left, grad_right)).astype(jnp.bfloat16), grad_gate)
    )
    grad_mid = (grad_inner.astype(jnp.float32) + grad_front.astype(jnp.float32)).astype(
        jnp.bfloat16
    )
    grad_mixed, grad_gate, grad_inner = out_finish_back(grad_mid)
    signal = grad_mixed.astype(jnp.bfloat16)
    signal_cols = gather_cols(signal)
    grad_left = jnp.einsum(
        "ijc,jkc->ikc", signal_cols, fetched[-1], preferred_element_type=jnp.float32
    )
    signal_block = column_block(gather_rows(signal[None])[0])
    grad_right = jnp.einsum(
        "ijc,ikc->jkc", signal_block, fetched[0], preferred_element_type=jnp.float32
    )
    (grad_front,) = out_front_back(
        (jnp.stack((grad_left, grad_right)).astype(jnp.bfloat16), grad_gate)
    )
    return (grad_inner.astype(jnp.float32) + grad_front.astype(jnp.float32)).astype(jnp.bfloat16)


def sigmoid(values):
    return 0.5 + 0.5 * jnp.tanh(0.5 * values)


def lane_mean(values):
    return jnp.mean(values, axis=-1, keepdims=True)


def normalize(values):
    centred = values - lane_mean(values)
    inverse = lax.rsqrt(lane_mean(centred * centred) + EPS)
    return centred * inverse, inverse


def normalize_back(grad, normed, inverse):
    return inverse * (grad - lane_mean(grad) - normed * lane_mean(grad * normed))


def rounded(values):
    return values.astype(BF16).astype(F32)


def matmul(values, weight):
    return jnp.dot(values.astype(BF16), weight, preferred_element_type=F32)


def matmul_t(values, weight):
    return lax.dot_general(
        values.astype(BF16), weight, (((1,), (1,)), ((), ())), preferred_element_type=F32
    )


def split(linear):
    return [linear[:, i * H : (i + 1) * H] for i in range(5)]


def front_back(linear, mask, grad_left, grad_right, grad_gate, weight, normed, inverse):
    gate_l, val_l, gate_r, val_r, gate = split(linear)
    gate_l, gate_r, gate = sigmoid(gate_l), sigmoid(gate_r), sigmoid(gate)
    grad_left, grad_right = grad_left * mask, grad_right * mask
    pieces = (
        grad_left * val_l * (gate_l * (1.0 - gate_l)),
        grad_left * gate_l,
        grad_right * val_r * (gate_r * (1.0 - gate_r)),
        grad_right * gate_r,
        grad_gate * (gate * (1.0 - gate)),
    )
    grad = jnp.concatenate([piece.astype(BF16) for piece in pieces], axis=1)
    return rounded(normalize_back(rounded(matmul_t(grad, weight)), normed, inverse))


class Crop:
    def __init__(self, n, rows, cols, mask_ref):
        self.n, self.rows, self.cols = n, rows, cols
        self.pitch = n + PAD
        self.group = n // GROUPS
        self.chain = sum(mask_ref[i] for i in range(n))
        self.row = lax.axis_index("row")
        col_index = lax.axis_index("col")
        self.me = self.row * rows
        self.mine = pl.multiple_of(col_index * cols, cols)
        self.theirs = pl.multiple_of((1 - col_index) * cols, cols)

    def place(self, ref, blocks, own_ref, other_ref):
        for position, block in enumerate(blocks):
            start = (self.row ^ block) * self.rows
            for a in range(self.rows):
                base = (start + a) * self.pitch
                ref[pl.ds(base + self.mine, self.cols), :] = own_ref[position, a].astype(F32)
                ref[pl.ds(base + self.theirs, self.cols), :] = other_ref[position, a].astype(F32)

    def mask(self, count, span, start, offset):
        major = lax.broadcasted_iota(jnp.int32, (count, span, H), 0) + start
        minor = lax.broadcasted_iota(jnp.int32, (count, span, H), 1) + offset
        inside = (major < self.chain) & (minor < self.chain)
        return jnp.where(inside, 1.0, 0.0).reshape(count * span, H)

    def get(self, ref, start, count):
        return jnp.concatenate(
            [ref[pl.ds((start + a) * self.pitch, self.n), :] for a in range(count)], axis=0
        )

    def put(self, ref, start, values):
        n = self.n
        for a in range(values.shape[0] // n):
            ref[pl.ds((start + a) * self.pitch, n), :] = values[a * n : (a + 1) * n]

    def put_t(self, ref, start, values):
        n = self.n
        for a in range(values.shape[0] // n):
            ref[pl.ds(start + a, n, stride=self.pitch), :] = values[a * n : (a + 1) * n]

    def take(self, ref):
        turned = [
            ref[pl.ds(self.me + a, self.n, stride=self.pitch), :] for a in range(self.rows)
        ]
        return jnp.concatenate([self.get(ref, self.me, self.rows)] + turned, axis=0)

    def own(self, ref, base, stride):
        return jnp.concatenate(
            [ref[pl.ds(base + a * stride + self.mine, self.cols), :] for a in range(self.rows)],
            axis=0,
        )

    def projection(self, weight, source, start):
        mask = self.mask(self.group, self.n, start, 0)
        normed, _ = normalize(source)
        gate_l, val_l, gate_r, val_r, gate = split(matmul(normed, weight))
        return (
            rounded(mask * (sigmoid(gate_l) * val_l)),
            rounded(mask * (sigmoid(gate_r) * val_r)),
            sigmoid(gate),
        )

    def product(self, row_of, ref_a, ref_b, minor, width):
        totals = [None] * self.rows
        for s in range(self.n):
            block = ref_b[pl.ds(s * self.pitch + minor, width), :]
            for p in range(self.rows):
                term = jnp.broadcast_to(ref_a[pl.ds(row_of(p, s), 1), :], (width, H)) * block
                totals[p] = term if totals[p] is None else totals[p] + term
        return jnp.concatenate(totals, axis=0)


def forward_kernel(
    n, rows, cols, blocks, mask_ref, own_ref, other_ref, front_ref, out_ref,
    left, right, gate0, mixed0, mid, left1, right1, left1_t, right1_t, gate1, mixed1,
    act, right_t,
):
    crop = Crop(n, rows, cols, mask_ref)
    group, pitch = crop.group, crop.pitch
    crop.place(act, blocks, own_ref, other_ref)

    def front0(c, _):
        start = c * group
        a, b, g = crop.projection(front_ref[0], crop.get(act, start, group), start)
        crop.put(left, start, a)
        crop.put(right, start, b)
        crop.put_t(right_t, start, b)
        crop.put(gate0, start, g)
        return 0

    lax.fori_loop(0, GROUPS, front0, 0)

    def triangle0(c, _):
        start = c * rows
        crop.put(mixed0, start, crop.product(
            lambda p, s: (start + p) * pitch + s, left, right_t, 0, n))
        return 0

    lax.fori_loop(0, n // rows, triangle0, 0)

    def middle(c, _):
        start = c * group
        normed, _ = normalize(crop.get(mixed0, start, group))
        update = matmul(normed, out_ref[0])
        value = rounded(crop.get(act, start, group) + crop.get(gate0, start, group) * update)
        crop.put(mid, start, value)
        a, b, g = crop.projection(front_ref[1], value, start)
        crop.put(left1, start, a)
        crop.put(right1, start, b)
        crop.put_t(left1_t, start, a)
        crop.put_t(right1_t, start, b)
        crop.put(gate1, start, g)
        return 0

    lax.fori_loop(0, GROUPS, middle, 0)

    def triangle1(c, _):
        start = c * rows
        crop.put(mixed1, start, crop.product(
            lambda p, s: s * pitch + start + p, left1, right1, 0, n))
        return 0

    lax.fori_loop(0, n // rows, triangle1, 0)


def backward_kernel(
    n, rows, cols, blocks, mask_ref, act_ref, own_ref, other_ref, front_ref, out_ref,
    left, right, gate0, mixed0, mid, left1, right1, left1_t, right1_t, gate1, mixed1,
    grad_ref, cot, sig, sig_t, grow, s_gate, s_sig, dl, dr,
):
    crop = Crop(n, rows, cols, mask_ref)
    group, pitch, me, take = crop.group, crop.pitch, crop.me, crop.take
    step = rows * n
    crop.place(cot, blocks, own_ref, other_ref)

    def signal1(c, _):
        start = c * group
        normed, inverse = normalize(crop.get(mixed1, start, group))
        grad = crop.get(cot, start, group) * crop.get(gate1, start, group)
        grad = rounded(matmul_t(grad, out_ref[1]))
        value = rounded(normalize_back(grad, normed, inverse))
        crop.put(sig, start, value)
        crop.put_t(sig_t, start, value)
        return 0

    lax.fori_loop(0, GROUPS, signal1, 0)

    def row_of(p, s):
        return (me + p) * pitch + s

    dl[pl.ds(0, step), :] = crop.product(row_of, right1, sig_t, 0, n)
    dl[pl.ds(step, step), :] = crop.product(row_of, sig, right1_t, 0, n)
    dr[pl.ds(0, step), :] = crop.product(row_of, left1, sig, 0, n)
    dr[pl.ds(step, step), :] = crop.product(
        lambda p, s: s * pitch + me + p, sig, left1_t, 0, n)

    mask_rows = crop.mask(rows, n, me, 0)
    cot_s = take(cot)
    mixed, _ = normalize(take(mixed1))
    normed, inverse = normalize(take(mid))
    grad_gate = cot_s * matmul(mixed, out_ref[1])
    grad = front_back(
        matmul(normed, front_ref[1]), jnp.concatenate([mask_rows, mask_rows], axis=0),
        rounded(dl[...]), rounded(dr[...]), grad_gate, front_ref[1], normed, inverse)
    grad_mid = rounded(cot_s + grad)
    mixed, inverse = normalize(take(mixed0))
    grow[...] = grad_mid[:step]
    s_gate[...] = grad_mid[:step] * matmul(mixed[:step], out_ref[0])
    grad = rounded(matmul_t(grad_mid * take(gate0), out_ref[0]))
    s_sig[...] = rounded(normalize_back(grad, mixed, inverse))

    grad_left = crop.product(lambda p, s: p * n + s, s_sig, right, crop.mine, cols)
    grad_right = crop.product(lambda p, s: step + p * n + s, s_sig, left, crop.mine, cols)

    normed, inverse = normalize(act_ref[...].astype(F32).reshape(rows * cols, H))
    grad = front_back(
        matmul(normed, front_ref[0]), crop.mask(rows, cols, me, crop.mine),
        rounded(grad_left), rounded(grad_right),
        crop.own(s_gate, 0, n), front_ref[0], normed, inverse)
    grad_ref[...] = (crop.own(grow, 0, n) + grad).astype(BF16).reshape(rows, cols, H)


def whole_body(pair_act, cotangent, residue_mask, front_weight, out_weight):
    rows, cols, _ = pair_act.shape
    n = residue_mask.shape[0]
    row_count = lax.axis_size("row")
    bits = row_count.bit_length() - 1
    blocks = [0]
    act, cot = pair_act[None], cotangent[None]
    for bit in [1 << b for b in range(1, bits)] + [1]:
        pairs = [(i, i ^ bit) for i in range(row_count)]
        act = jnp.concatenate((act, lax.ppermute(act, "row", pairs)))
        cot = jnp.concatenate((cot, lax.ppermute(cot, "row", pairs)))
        blocks = blocks + [b ^ bit for b in blocks]
    act_other = lax.ppermute(act, "col", [(0, 1), (1, 0)])
    cot_other = lax.ppermute(cot, "col", [(0, 1), (1, 0)])
    shape = (n * (n + PAD), H)
    full = pltpu.VMEM(shape, F32)
    some = pltpu.VMEM((rows * n, H), F32)
    twice = pltpu.VMEM((2 * rows * n, H), F32)
    vmem = pl.BlockSpec(memory_space=pltpu.VMEM)
    smem = pl.BlockSpec(memory_space=pltpu.SMEM)
    kept = pl.pallas_call(
        functools.partial(forward_kernel, n, rows, cols, blocks),
        out_shape=[jax.ShapeDtypeStruct(shape, F32)] * 11,
        in_specs=[smem] + [vmem] * 4,
        out_specs=[vmem] * 11,
        scratch_shapes=[full] * 2,
        compiler_params=pltpu.CompilerParams(vmem_limit_bytes=VMEM_BUDGET // 2),
    )(residue_mask, act, act_other, front_weight, out_weight)
    return pl.pallas_call(
        functools.partial(backward_kernel, n, rows, cols, blocks),
        out_shape=jax.ShapeDtypeStruct(pair_act.shape, BF16),
        in_specs=[smem] + [vmem] * 16,
        out_specs=vmem,
        scratch_shapes=[full] * 3 + [some, some, twice, twice, twice],
        compiler_params=pltpu.CompilerParams(vmem_limit_bytes=VMEM_BUDGET // 2),
    )(residue_mask, pair_act, cot, cot_other, front_weight, out_weight, *kept)


def body(pair_act, cotangent, residue_mask, front_weight, out_weight):
    n = residue_mask.shape[0]
    row_count = lax.axis_size("row")
    fits = 20 * n * (n + PAD) * H * 4 <= VMEM_BUDGET
    doubling = row_count & (row_count - 1) == 0 and lax.axis_size("col") == 2
    run = whole_body if fits and doubling else spread_body
    return run(pair_act, cotangent, residue_mask, front_weight, out_weight)


def solution(mesh):
    placed = (P(("grp", "row"), "col", None), P(("grp", "row"), "col", None), P("grp"), P(), P())
    return jax.shard_map(
        body, mesh=mesh, in_specs=placed, out_specs=P(("grp", "row"), "col", None), check_vma=False
    )
```

```python
import functools

import jax
import jax.numpy as jnp
from jax import lax
from jax.experimental import pallas as pl
from jax.experimental.pallas import tpu as pltpu
from jax.sharding import PartitionSpec as P

H = 128
EPS = 1e-05
PAD = 4
VMEM_BUDGET = 40 << 20
F32 = jnp.float32
BF16 = jnp.bfloat16


def from_root(array, axis, root):
    mine = lax.axis_index(axis) == root
    return lax.psum(jnp.where(mine, array, jnp.zeros_like(array)), axis)


def layer_norm(values):
    centred = values - jnp.mean(values, axis=-1, keepdims=True)
    spread = jnp.mean(centred * centred, axis=-1, keepdims=True)
    return centred * lax.rsqrt(spread + 1e-05)


def project_pair(inner_pair, mask_pair, weight):
    normed = layer_norm(inner_pair.astype(jnp.float32)).astype(jnp.bfloat16)
    linear = jnp.dot(normed, weight, preferred_element_type=jnp.float32)
    left_side = jax.nn.sigmoid(linear[..., :H]) * linear[..., H : 2 * H]
    right_side = jax.nn.sigmoid(linear[..., 2 * H : 3 * H]) * linear[..., 3 * H : 4 * H]
    operands = (jnp.stack((left_side, right_side)) * mask_pair[None, :, :, None]).astype(
        jnp.bfloat16
    )
    return (operands, jax.nn.sigmoid(linear[..., 4 * H :]))


def finish(mixed_part, gate_value, inner_pair, weight):
    normed = layer_norm(mixed_part).astype(jnp.bfloat16)
    update = jnp.dot(normed, weight, preferred_element_type=jnp.float32)
    return (inner_pair.astype(jnp.float32) + gate_value * update).astype(jnp.bfloat16)


def spread_body(pair_act, cotangent, residue_mask, front_weight, out_weight):
    local_rows = pair_act.shape[0]
    local_cols = pair_act.shape[1]
    row_index = lax.axis_index("row")
    col_index = lax.axis_index("col")
    block_rows = lax.axis_size("row") // lax.axis_size("col")
    owner_col = row_index // block_rows
    offset = row_index % block_rows * local_rows
    chain_mask = residue_mask.astype(jnp.float32)
    mask_rows = lax.dynamic_slice_in_dim(chain_mask, row_index * local_rows, local_rows)
    mask_cols = lax.dynamic_slice_in_dim(chain_mask, col_index * local_cols, local_cols)
    mask_pair = mask_rows[:, None] * mask_cols[None, :]

    def gather_rows(stacked):
        return lax.all_gather(stacked, "row", axis=1, tiled=True)

    def column_block(gathered):
        slab = lax.dynamic_slice_in_dim(gathered, offset, local_rows, 1)
        return from_root(slab, "col", owner_col)

    def gather_cols(values):
        return lax.all_gather(values, "col", axis=1, tiled=True)

    def sum_cols(partial_term):
        return lax.psum_scatter(
            partial_term.astype(jnp.bfloat16), "col", scatter_dimension=1, tiled=True
        ).astype(jnp.float32)

    (out_ops, out_gate), out_front_back = jax.vjp(
        lambda inner_pair: project_pair(inner_pair, mask_pair, front_weight[0]), pair_act
    )
    fetched = gather_rows(out_ops)
    out_mixed = sum_cols(
        jnp.einsum("ikc,jkc->ijc", out_ops[0], fetched[-1], preferred_element_type=jnp.float32)
    )
    pair_mid, out_finish_back = jax.vjp(
        lambda mixed_part, gate_value, inner_pair: finish(
            mixed_part, gate_value, inner_pair, out_weight[0]
        ),
        out_mixed,
        out_gate,
        pair_act,
    )
    (in_ops, in_gate), in_front_back = jax.vjp(
        lambda inner_pair: project_pair(inner_pair, mask_pair, front_weight[1]), pair_mid
    )
    in_fetched = gather_rows(in_ops)
    left_block = column_block(in_fetched[0])
    in_mixed = jnp.einsum(
        "kic,kjc->ijc", left_block, in_fetched[1], preferred_element_type=jnp.float32
    )
    unused_pair, in_finish_back = jax.vjp(
        lambda mixed_part, gate_value, inner_pair: finish(
            mixed_part, gate_value, inner_pair, out_weight[1]
        ),
        in_mixed,
        in_gate,
        pair_mid,
    )
    grad_mixed, grad_gate, grad_inner = in_finish_back(cotangent)
    signal = grad_mixed.astype(jnp.bfloat16)
    signal_rows = gather_rows(signal[None])[0]
    left_rows = gather_cols(in_ops[0])
    grad_right = jnp.einsum(
        "kic,ijc->kjc", left_rows, signal_rows, preferred_element_type=jnp.float32
    )
    grad_left = sum_cols(
        jnp.einsum("kjc,ijc->kic", in_ops[1], signal_rows, preferred_element_type=jnp.float32)
    )
    (grad_front,) = in_front_back(
        (jnp.stack((grad_left, grad_right)).astype(jnp.bfloat16), grad_gate)
    )
    grad_mid = (grad_inner.astype(jnp.float32) + grad_front.astype(jnp.float32)).astype(
        jnp.bfloat16
    )
    grad_mixed, grad_gate, grad_inner = out_finish_back(grad_mid)
    signal = grad_mixed.astype(jnp.bfloat16)
    signal_cols = gather_cols(signal)
    grad_left = jnp.einsum(
        "ijc,jkc->ikc", signal_cols, fetched[-1], preferred_element_type=jnp.float32
    )
    signal_block = column_block(gather_rows(signal[None])[0])
    grad_right = jnp.einsum(
        "ijc,ikc->jkc", signal_block, fetched[0], preferred_element_type=jnp.float32
    )
    (grad_front,) = out_front_back(
        (jnp.stack((grad_left, grad_right)).astype(jnp.bfloat16), grad_gate)
    )
    return (grad_inner.astype(jnp.float32) + grad_front.astype(jnp.float32)).astype(jnp.bfloat16)


def sigmoid(values):
    return 0.5 + 0.5 * jnp.tanh(0.5 * values)


def lane_mean(values):
    return jnp.mean(values, axis=-1, keepdims=True)


def normalize(values):
    centred = values - lane_mean(values)
    inverse = lax.rsqrt(lane_mean(centred * centred) + EPS)
    return centred * inverse, inverse


def normalize_back(grad, normed, inverse):
    return inverse * (grad - lane_mean(grad) - normed * lane_mean(grad * normed))


def rounded(values):
    return values.astype(BF16).astype(F32)


def matmul(values, weight):
    return jnp.dot(values.astype(BF16), weight, preferred_element_type=F32)


def matmul_t(values, weight):
    return lax.dot_general(
        values.astype(BF16), weight, (((1,), (1,)), ((), ())), preferred_element_type=F32
    )


def split(linear):
    return [linear[:, i * H : (i + 1) * H] for i in range(5)]


def front_back(linear, mask, grad_left, grad_right, grad_gate, weight, normed, inverse):
    gate_l, val_l, gate_r, val_r, gate = split(linear)
    gate_l, gate_r, gate = sigmoid(gate_l), sigmoid(gate_r), sigmoid(gate)
    grad_left, grad_right = grad_left * mask, grad_right * mask
    pieces = (
        grad_left * val_l * (gate_l * (1.0 - gate_l)),
        grad_left * gate_l,
        grad_right * val_r * (gate_r * (1.0 - gate_r)),
        grad_right * gate_r,
        grad_gate * (gate * (1.0 - gate)),
    )
    grad = jnp.concatenate([piece.astype(BF16) for piece in pieces], axis=1)
    return rounded(normalize_back(rounded(matmul_t(grad, weight)), normed, inverse))


def crop_kernel(
    n, rows, cols, blocks, mask_ref, own_ref, other_ref, front_ref, out_ref, grad_ref,
    act, cot, left, right, right_t, gate0, mixed0, mid, left1, right1, left1_t, right1_t,
    gate1, mixed1, sig, sig_t, grow, s_gate, s_sig, dl, dr,
):
    pitch = n + PAD
    row_index = lax.axis_index("row")
    col_index = lax.axis_index("col")
    chain = sum(mask_ref[i] for i in range(n))
    me = row_index * rows
    mine = pl.multiple_of(col_index * cols, cols)
    theirs = pl.multiple_of((1 - col_index) * cols, cols)
    step = rows * n

    for position in range(len(blocks[0])):
        here = [lists[position] for lists in blocks]
        for source, core, offset in ((own_ref, 0, mine), (other_ref, 1, theirs)):
            block = jnp.where(col_index == core, here[0], here[1])
            place = (row_index ^ block) * rows
            for a in range(rows):
                where = pl.ds((place + a) * pitch + offset, cols)
                act[where, :] = source[2 * position, a].astype(F32)
                cot[where, :] = source[2 * position + 1, a].astype(F32)

    def mask_of(count, span, start, offset):
        major = lax.broadcasted_iota(jnp.int32, (count, span, H), 0) + start
        minor = lax.broadcasted_iota(jnp.int32, (count, span, H), 1) + offset
        return jnp.where((major < chain) & (minor < chain), 1.0, 0.0).reshape(count * span, H)

    def get(ref, start=0, count=n):
        return jnp.concatenate(
            [ref[pl.ds((start + a) * pitch, n), :] for a in range(count)], axis=0
        )

    def put(ref, start, values, count=n):
        for a in range(count):
            ref[pl.ds((start + a) * pitch, n), :] = values[a * n : (a + 1) * n]

    def put_t(ref, values):
        for a in range(n):
            ref[pl.ds(a, n, stride=pitch), :] = values[a * n : (a + 1) * n]

    def get_t(ref):
        return [ref[pl.ds(me + a, n, stride=pitch), :] for a in range(rows)]

    def take(ref):
        return jnp.concatenate([get(ref, me, rows)] + get_t(ref), axis=0)

    def projection(u, source):
        mask = mask_of(n, n, 0, 0)
        normed, _ = normalize(source)
        linear = matmul(normed, front_ref[u])
        gate_l, val_l, gate_r, val_r, gate = split(linear)
        return (
            rounded(mask * (sigmoid(gate_l) * val_l)),
            rounded(mask * (sigmoid(gate_r) * val_r)),
            sigmoid(gate),
        )

    def product(count, span, row_of, ref_a, ref_b, minor, width, pitch_b=pitch):
        totals = [None] * count
        for s in range(span):
            block = ref_b[pl.ds(s * pitch_b + minor, width), :]
            for p in range(count):
                term = jnp.broadcast_to(ref_a[pl.ds(row_of(p, s), 1), :], (width, H)) * block
                totals[p] = term if totals[p] is None else totals[p] + term
        return totals

    a, b, g = projection(0, get(act))
    put(left, 0, a)
    put(right, 0, b)
    put_t(right_t, b)
    put(gate0, 0, g)

    for start in range(0, n, rows):
        totals = product(
            rows, n, lambda p, s: (start + p) * pitch + s, left, right_t, 0, n)
        put(mixed0, start, jnp.concatenate(totals, axis=0), rows)

    normed, _ = normalize(get(mixed0))
    value = rounded(get(act) + get(gate0) * matmul(normed, out_ref[0]))
    put(mid, 0, value)
    a, b, g = projection(1, value)
    put(left1, 0, a)
    put(right1, 0, b)
    put_t(left1_t, a)
    put_t(right1_t, b)
    put(gate1, 0, g)

    for start in range(0, n, rows):
        totals = product(rows, n, lambda p, s: s * pitch + start + p, left1, right1, 0, n)
        put(mixed1, start, jnp.concatenate(totals, axis=0), rows)

    normed, inverse = normalize(get(mixed1))
    grad = rounded(matmul_t(get(cot) * get(gate1), out_ref[1]))
    value = rounded(normalize_back(grad, normed, inverse))
    put(sig, 0, value)
    put_t(sig_t, value)

    def row_of(p, s):
        return (me + p) * pitch + s

    dl[pl.ds(0, step), :] = jnp.concatenate(
        product(rows, n, row_of, right1, sig_t, 0, n), axis=0)
    dl[pl.ds(step, step), :] = jnp.concatenate(
        product(rows, n, row_of, sig, right1_t, 0, n), axis=0)
    dr[pl.ds(0, step), :] = jnp.concatenate(
        product(rows, n, row_of, left1, sig, 0, n), axis=0)
    dr[pl.ds(step, step), :] = jnp.concatenate(
        product(rows, n, lambda p, s: s * pitch + me + p, sig, left1_t, 0, n), axis=0)

    mask_rows = mask_of(rows, n, me, 0)
    cot_s = take(cot)
    mixed, _ = normalize(take(mixed1))
    normed, inverse = normalize(take(mid))
    grad_gate = cot_s * matmul(mixed, out_ref[1])
    grad = front_back(
        matmul(normed, front_ref[1]), jnp.concatenate([mask_rows, mask_rows], axis=0),
        rounded(dl[...]), rounded(dr[...]), grad_gate, front_ref[1], normed, inverse)
    grad_mid = rounded(cot_s + grad)
    mixed, inverse = normalize(take(mixed0))
    grow[...] = grad_mid[:step]
    s_gate[...] = grad_mid[:step] * matmul(mixed[:step], out_ref[0])
    grad = rounded(matmul_t(grad_mid * take(gate0), out_ref[0]))
    s_sig[...] = rounded(normalize_back(grad, mixed, inverse))

    grad_left = product(rows, n, lambda p, s: p * n + s, s_sig, right, mine, cols)
    grad_right = product(rows, n, lambda p, s: step + p * n + s, s_sig, left, mine, cols)

    def own(ref, base, stride):
        return jnp.concatenate(
            [ref[pl.ds(base + a * stride + mine, cols), :] for a in range(rows)], axis=0)

    normed, inverse = normalize(own(act, me * pitch, pitch))
    grad = front_back(
        matmul(normed, front_ref[0]), mask_of(rows, cols, me, mine),
        rounded(jnp.concatenate(grad_left, axis=0)), rounded(jnp.concatenate(grad_right, axis=0)),
        own(s_gate, 0, n), front_ref[0], normed, inverse)
    grad_ref[...] = (own(grow, 0, n) + grad).astype(BF16).reshape(rows, cols, H)


def whole_body(pair_act, cotangent, residue_mask, front_weight, out_weight):
    rows, cols, width = pair_act.shape
    n = residue_mask.shape[0]
    row_count = lax.axis_size("row")
    bits = row_count.bit_length() - 1
    first = [1 << b for b in range(1, bits)] + [1]
    orders = (first, first[1:] + first[:1])
    blocks = ([0], [0])
    gathered = None
    for steps in zip(*orders):
        pairs = [
            (2 * i + core, 2 * (i ^ step) + core)
            for i in range(row_count) for core, step in enumerate(steps)
        ]

        def swap(array):
            return lax.ppermute(array, ("row", "col"), pairs)

        if gathered is None:
            mine = lax.optimization_barrier(jnp.stack((pair_act, cotangent)))
            gathered = jnp.concatenate(
                (mine, swap(pair_act[None]), swap(cotangent[None])))
        else:
            gathered = jnp.concatenate((gathered, swap(gathered)))
        blocks = tuple(b + [x ^ step for x in b] for b, step in zip(blocks, steps))
    other = lax.ppermute(gathered, "col", [(0, 1), (1, 0)])
    full = pltpu.VMEM((n * (n + PAD), H), F32)
    some = pltpu.VMEM((rows * n, H), F32)
    twice = pltpu.VMEM((2 * rows * n, H), F32)
    vmem = pl.BlockSpec(memory_space=pltpu.VMEM)
    return pl.pallas_call(
        functools.partial(crop_kernel, n, rows, cols, blocks),
        out_shape=jax.ShapeDtypeStruct(pair_act.shape, BF16),
        in_specs=[pl.BlockSpec(memory_space=pltpu.SMEM)] + [vmem] * 4,
        out_specs=vmem,
        scratch_shapes=[full] * 16 + [some, some, twice, twice, twice],
        compiler_params=pltpu.CompilerParams(vmem_limit_bytes=VMEM_BUDGET),
    )(residue_mask, gathered, other, front_weight, out_weight)


def body(pair_act, cotangent, residue_mask, front_weight, out_weight):
    n = residue_mask.shape[0]
    row_count = lax.axis_size("row")
    fits = 20 * n * (n + PAD) * H * 4 <= VMEM_BUDGET
    doubling = row_count & (row_count - 1) == 0 and lax.axis_size("col") == 2
    run = whole_body if fits and doubling else spread_body
    return run(pair_act, cotangent, residue_mask, front_weight, out_weight)


def solution(mesh):
    placed = (P(("grp", "row"), "col", None), P(("grp", "row"), "col", None), P("grp"), P(), P())
    return jax.shard_map(
        body, mesh=mesh, in_specs=placed, out_specs=P(("grp", "row"), "col", None), check_vma=False
    )
```

```python
import functools

import jax
import jax.numpy as jnp
from jax import lax
from jax.experimental import pallas as pl
from jax.experimental.pallas import tpu as pltpu
from jax.sharding import PartitionSpec as P

H = 128
EPS = 1e-05
PAD = 4
VMEM_BUDGET = 40 << 20
F32 = jnp.float32
BF16 = jnp.bfloat16


def from_root(array, axis, root):
    mine = lax.axis_index(axis) == root
    return lax.psum(jnp.where(mine, array, jnp.zeros_like(array)), axis)


def layer_norm(values):
    centred = values - jnp.mean(values, axis=-1, keepdims=True)
    spread = jnp.mean(centred * centred, axis=-1, keepdims=True)
    return centred * lax.rsqrt(spread + 1e-05)


def project_pair(inner_pair, mask_pair, weight):
    normed = layer_norm(inner_pair.astype(jnp.float32)).astype(jnp.bfloat16)
    linear = jnp.dot(normed, weight, preferred_element_type=jnp.float32)
    left_side = jax.nn.sigmoid(linear[..., :H]) * linear[..., H : 2 * H]
    right_side = jax.nn.sigmoid(linear[..., 2 * H : 3 * H]) * linear[..., 3 * H : 4 * H]
    operands = (jnp.stack((left_side, right_side)) * mask_pair[None, :, :, None]).astype(
        jnp.bfloat16
    )
    return (operands, jax.nn.sigmoid(linear[..., 4 * H :]))


def finish(mixed_part, gate_value, inner_pair, weight):
    normed = layer_norm(mixed_part).astype(jnp.bfloat16)
    update = jnp.dot(normed, weight, preferred_element_type=jnp.float32)
    return (inner_pair.astype(jnp.float32) + gate_value * update).astype(jnp.bfloat16)


def spread_body(pair_act, cotangent, residue_mask, front_weight, out_weight):
    local_rows = pair_act.shape[0]
    local_cols = pair_act.shape[1]
    row_index = lax.axis_index("row")
    col_index = lax.axis_index("col")
    block_rows = lax.axis_size("row") // lax.axis_size("col")
    owner_col = row_index // block_rows
    offset = row_index % block_rows * local_rows
    chain_mask = residue_mask.astype(jnp.float32)
    mask_rows = lax.dynamic_slice_in_dim(chain_mask, row_index * local_rows, local_rows)
    mask_cols = lax.dynamic_slice_in_dim(chain_mask, col_index * local_cols, local_cols)
    mask_pair = mask_rows[:, None] * mask_cols[None, :]

    def gather_rows(stacked):
        return lax.all_gather(stacked, "row", axis=1, tiled=True)

    def column_block(gathered):
        slab = lax.dynamic_slice_in_dim(gathered, offset, local_rows, 1)
        return from_root(slab, "col", owner_col)

    def gather_cols(values):
        return lax.all_gather(values, "col", axis=1, tiled=True)

    def sum_cols(partial_term):
        return lax.psum_scatter(
            partial_term.astype(jnp.bfloat16), "col", scatter_dimension=1, tiled=True
        ).astype(jnp.float32)

    (out_ops, out_gate), out_front_back = jax.vjp(
        lambda inner_pair: project_pair(inner_pair, mask_pair, front_weight[0]), pair_act
    )
    fetched = gather_rows(out_ops)
    out_mixed = sum_cols(
        jnp.einsum("ikc,jkc->ijc", out_ops[0], fetched[-1], preferred_element_type=jnp.float32)
    )
    pair_mid, out_finish_back = jax.vjp(
        lambda mixed_part, gate_value, inner_pair: finish(
            mixed_part, gate_value, inner_pair, out_weight[0]
        ),
        out_mixed,
        out_gate,
        pair_act,
    )
    (in_ops, in_gate), in_front_back = jax.vjp(
        lambda inner_pair: project_pair(inner_pair, mask_pair, front_weight[1]), pair_mid
    )
    in_fetched = gather_rows(in_ops)
    left_block = column_block(in_fetched[0])
    in_mixed = jnp.einsum(
        "kic,kjc->ijc", left_block, in_fetched[1], preferred_element_type=jnp.float32
    )
    unused_pair, in_finish_back = jax.vjp(
        lambda mixed_part, gate_value, inner_pair: finish(
            mixed_part, gate_value, inner_pair, out_weight[1]
        ),
        in_mixed,
        in_gate,
        pair_mid,
    )
    grad_mixed, grad_gate, grad_inner = in_finish_back(cotangent)
    signal = grad_mixed.astype(jnp.bfloat16)
    signal_rows = gather_rows(signal[None])[0]
    left_rows = gather_cols(in_ops[0])
    grad_right = jnp.einsum(
        "kic,ijc->kjc", left_rows, signal_rows, preferred_element_type=jnp.float32
    )
    grad_left = sum_cols(
        jnp.einsum("kjc,ijc->kic", in_ops[1], signal_rows, preferred_element_type=jnp.float32)
    )
    (grad_front,) = in_front_back(
        (jnp.stack((grad_left, grad_right)).astype(jnp.bfloat16), grad_gate)
    )
    grad_mid = (grad_inner.astype(jnp.float32) + grad_front.astype(jnp.float32)).astype(
        jnp.bfloat16
    )
    grad_mixed, grad_gate, grad_inner = out_finish_back(grad_mid)
    signal = grad_mixed.astype(jnp.bfloat16)
    signal_cols = gather_cols(signal)
    grad_left = jnp.einsum(
        "ijc,jkc->ikc", signal_cols, fetched[-1], preferred_element_type=jnp.float32
    )
    signal_block = column_block(gather_rows(signal[None])[0])
    grad_right = jnp.einsum(
        "ijc,ikc->jkc", signal_block, fetched[0], preferred_element_type=jnp.float32
    )
    (grad_front,) = out_front_back(
        (jnp.stack((grad_left, grad_right)).astype(jnp.bfloat16), grad_gate)
    )
    return (grad_inner.astype(jnp.float32) + grad_front.astype(jnp.float32)).astype(jnp.bfloat16)


def sigmoid(values):
    return 0.5 + 0.5 * jnp.tanh(0.5 * values)


def lane_mean(values):
    return jnp.mean(values, axis=-1, keepdims=True)


def normalize(values):
    centred = values - lane_mean(values)
    inverse = lax.rsqrt(lane_mean(centred * centred) + EPS)
    return centred * inverse, inverse


def normalize_back(grad, normed, inverse):
    return inverse * (grad - lane_mean(grad) - normed * lane_mean(grad * normed))


def rounded(values):
    return values.astype(BF16).astype(F32)


def matmul(values, weight):
    return jnp.dot(values.astype(BF16), weight, preferred_element_type=F32)


def matmul_t(values, weight):
    return lax.dot_general(
        values.astype(BF16), weight, (((1,), (1,)), ((), ())), preferred_element_type=F32
    )


def split(linear):
    return [linear[:, i * H : (i + 1) * H] for i in range(5)]


def front_back(linear, mask, grad_left, grad_right, grad_gate, weight, normed, inverse):
    gate_l, val_l, gate_r, val_r, gate = split(linear)
    gate_l, gate_r, gate = sigmoid(gate_l), sigmoid(gate_r), sigmoid(gate)
    grad_left, grad_right = grad_left * mask, grad_right * mask
    pieces = (
        grad_left * val_l * (gate_l * (1.0 - gate_l)),
        grad_left * gate_l,
        grad_right * val_r * (gate_r * (1.0 - gate_r)),
        grad_right * gate_r,
        grad_gate * (gate * (1.0 - gate)),
    )
    grad = jnp.concatenate([piece.astype(BF16) for piece in pieces], axis=1)
    return rounded(normalize_back(rounded(matmul_t(grad, weight)), normed, inverse))


def crop_kernel(
    n, rows, cols, blocks, mask_ref, own_ref, other_ref, front_ref, out_ref, grad_ref,
    act, cot, left, right, right_t, gate0, mixed0, mid, left1, right1, left1_t, right1_t,
    gate1, mixed1, sig, sig_t, grow, s_gate, s_sig, dl, dr,
):
    pitch = n + PAD
    row_index = lax.axis_index("row")
    col_index = lax.axis_index("col")
    chain = sum(mask_ref[i] for i in range(n))
    me = row_index * rows
    mine = pl.multiple_of(col_index * cols, cols)
    theirs = pl.multiple_of((1 - col_index) * cols, cols)
    step = rows * n

    for position, block in enumerate(blocks):
        place = (row_index ^ block) * rows
        for a in range(rows):
            base = (place + a) * pitch
            for source, offset in ((own_ref, mine), (other_ref, theirs)):
                act[pl.ds(base + offset, cols), :] = source[2 * position, a].astype(F32)
                cot[pl.ds(base + offset, cols), :] = source[2 * position + 1, a].astype(F32)

    def mask_of(count, span, start, offset):
        major = lax.broadcasted_iota(jnp.int32, (count, span, H), 0) + start
        minor = lax.broadcasted_iota(jnp.int32, (count, span, H), 1) + offset
        return jnp.where((major < chain) & (minor < chain), 1.0, 0.0).reshape(count * span, H)

    def get(ref, start=0, count=n):
        return jnp.concatenate(
            [ref[pl.ds((start + a) * pitch, n), :] for a in range(count)], axis=0
        )

    def put(ref, start, values, count=n):
        for a in range(count):
            ref[pl.ds((start + a) * pitch, n), :] = values[a * n : (a + 1) * n]

    def put_t(ref, values):
        for a in range(n):
            ref[pl.ds(a, n, stride=pitch), :] = values[a * n : (a + 1) * n]

    def get_t(ref):
        return [ref[pl.ds(me + a, n, stride=pitch), :] for a in range(rows)]

    def take(ref):
        return jnp.concatenate([get(ref, me, rows)] + get_t(ref), axis=0)

    def projection(u, source):
        mask = mask_of(n, n, 0, 0)
        normed, _ = normalize(source)
        linear = matmul(normed, front_ref[u])
        gate_l, val_l, gate_r, val_r, gate = split(linear)
        return (
            rounded(mask * (sigmoid(gate_l) * val_l)),
            rounded(mask * (sigmoid(gate_r) * val_r)),
            sigmoid(gate),
        )

    def product(count, span, row_of, ref_a, ref_b, minor, width, pitch_b=pitch):
        totals = [None] * count
        for s in range(span):
            block = ref_b[pl.ds(s * pitch_b + minor, width), :]
            for p in range(count):
                term = jnp.broadcast_to(ref_a[pl.ds(row_of(p, s), 1), :], (width, H)) * block
                totals[p] = term if totals[p] is None else totals[p] + term
        return totals

    a, b, g = projection(0, get(act))
    put(left, 0, a)
    put(right, 0, b)
    put_t(right_t, b)
    put(gate0, 0, g)

    for start in range(0, n, rows):
        totals = product(
            rows, n, lambda p, s: (start + p) * pitch + s, left, right_t, 0, n)
        put(mixed0, start, jnp.concatenate(totals, axis=0), rows)

    normed, _ = normalize(get(mixed0))
    value = rounded(get(act) + get(gate0) * matmul(normed, out_ref[0]))
    put(mid, 0, value)
    a, b, g = projection(1, value)
    put(left1, 0, a)
    put(right1, 0, b)
    put_t(left1_t, a)
    put_t(right1_t, b)
    put(gate1, 0, g)

    for start in range(0, n, rows):
        totals = product(rows, n, lambda p, s: s * pitch + start + p, left1, right1, 0, n)
        put(mixed1, start, jnp.concatenate(totals, axis=0), rows)

    normed, inverse = normalize(get(mixed1))
    grad = rounded(matmul_t(get(cot) * get(gate1), out_ref[1]))
    value = rounded(normalize_back(grad, normed, inverse))
    put(sig, 0, value)
    put_t(sig_t, value)

    def row_of(p, s):
        return (me + p) * pitch + s

    dl[pl.ds(0, step), :] = jnp.concatenate(
        product(rows, n, row_of, right1, sig_t, 0, n), axis=0)
    dl[pl.ds(step, step), :] = jnp.concatenate(
        product(rows, n, row_of, sig, right1_t, 0, n), axis=0)
    dr[pl.ds(0, step), :] = jnp.concatenate(
        product(rows, n, row_of, left1, sig, 0, n), axis=0)
    dr[pl.ds(step, step), :] = jnp.concatenate(
        product(rows, n, lambda p, s: s * pitch + me + p, sig, left1_t, 0, n), axis=0)

    mask_rows = mask_of(rows, n, me, 0)
    cot_s = take(cot)
    mixed, _ = normalize(take(mixed1))
    normed, inverse = normalize(take(mid))
    grad_gate = cot_s * matmul(mixed, out_ref[1])
    grad = front_back(
        matmul(normed, front_ref[1]), jnp.concatenate([mask_rows, mask_rows], axis=0),
        rounded(dl[...]), rounded(dr[...]), grad_gate, front_ref[1], normed, inverse)
    grad_mid = rounded(cot_s + grad)
    mixed, inverse = normalize(take(mixed0))
    grow[...] = grad_mid[:step]
    s_gate[...] = grad_mid[:step] * matmul(mixed[:step], out_ref[0])
    grad = rounded(matmul_t(grad_mid * take(gate0), out_ref[0]))
    s_sig[...] = rounded(normalize_back(grad, mixed, inverse))

    grad_left = product(rows, n, lambda p, s: p * n + s, s_sig, right, mine, cols)
    grad_right = product(rows, n, lambda p, s: step + p * n + s, s_sig, left, mine, cols)

    def own(ref, base, stride):
        return jnp.concatenate(
            [ref[pl.ds(base + a * stride + mine, cols), :] for a in range(rows)], axis=0)

    normed, inverse = normalize(own(act, me * pitch, pitch))
    grad = front_back(
        matmul(normed, front_ref[0]), mask_of(rows, cols, me, mine),
        rounded(jnp.concatenate(grad_left, axis=0)), rounded(jnp.concatenate(grad_right, axis=0)),
        own(s_gate, 0, n), front_ref[0], normed, inverse)
    grad_ref[...] = (own(grow, 0, n) + grad).astype(BF16).reshape(rows, cols, H)


def whole_body(pair_act, cotangent, residue_mask, front_weight, out_weight):
    rows, cols, width = pair_act.shape
    n = residue_mask.shape[0]
    row_count = lax.axis_size("row")
    bits = row_count.bit_length() - 1
    gathered = jnp.stack((pair_act, cotangent))
    blocks = [0]
    for step in [1 << b for b in range(1, bits)] + [1]:
        other = lax.ppermute(gathered, "row", [(i, i ^ step) for i in range(row_count)])
        gathered = jnp.concatenate((gathered, other))
        blocks = blocks + [b ^ step for b in blocks]
    other = lax.ppermute(gathered, "col", [(0, 1), (1, 0)])
    full = pltpu.VMEM((n * (n + PAD), H), F32)
    some = pltpu.VMEM((rows * n, H), F32)
    twice = pltpu.VMEM((2 * rows * n, H), F32)
    vmem = pl.BlockSpec(memory_space=pltpu.VMEM)
    return pl.pallas_call(
        functools.partial(crop_kernel, n, rows, cols, blocks),
        out_shape=jax.ShapeDtypeStruct(pair_act.shape, BF16),
        in_specs=[pl.BlockSpec(memory_space=pltpu.SMEM)] + [vmem] * 4,
        out_specs=vmem,
        scratch_shapes=[full] * 16 + [some, some, twice, twice, twice],
        compiler_params=pltpu.CompilerParams(vmem_limit_bytes=VMEM_BUDGET),
    )(residue_mask, gathered, other, front_weight, out_weight)


def body(pair_act, cotangent, residue_mask, front_weight, out_weight):
    n = residue_mask.shape[0]
    row_count = lax.axis_size("row")
    fits = 20 * n * (n + PAD) * H * 4 <= VMEM_BUDGET
    doubling = row_count & (row_count - 1) == 0 and lax.axis_size("col") == 2
    run = whole_body if fits and doubling else spread_body
    return run(pair_act, cotangent, residue_mask, front_weight, out_weight)


def solution(mesh):
    placed = (P(("grp", "row"), "col", None), P(("grp", "row"), "col", None), P("grp"), P(), P())
    return jax.shard_map(
        body, mesh=mesh, in_specs=placed, out_specs=P(("grp", "row"), "col", None), check_vma=False
    )
```

```python
import functools

import jax
import jax.numpy as jnp
from jax import lax
from jax.experimental import pallas as pl
from jax.experimental.pallas import tpu as pltpu
from jax.sharding import PartitionSpec as P

H = 128
EPS = 1e-05
PAD = 4
VMEM_BUDGET = 40 << 20
F32 = jnp.float32
BF16 = jnp.bfloat16


def from_root(array, axis, root):
    mine = lax.axis_index(axis) == root
    return lax.psum(jnp.where(mine, array, jnp.zeros_like(array)), axis)


def layer_norm(values):
    centred = values - jnp.mean(values, axis=-1, keepdims=True)
    spread = jnp.mean(centred * centred, axis=-1, keepdims=True)
    return centred * lax.rsqrt(spread + 1e-05)


def project_pair(inner_pair, mask_pair, weight):
    normed = layer_norm(inner_pair.astype(jnp.float32)).astype(jnp.bfloat16)
    linear = jnp.dot(normed, weight, preferred_element_type=jnp.float32)
    left_side = jax.nn.sigmoid(linear[..., :H]) * linear[..., H : 2 * H]
    right_side = jax.nn.sigmoid(linear[..., 2 * H : 3 * H]) * linear[..., 3 * H : 4 * H]
    operands = (jnp.stack((left_side, right_side)) * mask_pair[None, :, :, None]).astype(
        jnp.bfloat16
    )
    return (operands, jax.nn.sigmoid(linear[..., 4 * H :]))


def finish(mixed_part, gate_value, inner_pair, weight):
    normed = layer_norm(mixed_part).astype(jnp.bfloat16)
    update = jnp.dot(normed, weight, preferred_element_type=jnp.float32)
    return (inner_pair.astype(jnp.float32) + gate_value * update).astype(jnp.bfloat16)


def spread_body(pair_act, cotangent, residue_mask, front_weight, out_weight):
    local_rows = pair_act.shape[0]
    local_cols = pair_act.shape[1]
    row_index = lax.axis_index("row")
    col_index = lax.axis_index("col")
    block_rows = lax.axis_size("row") // lax.axis_size("col")
    owner_col = row_index // block_rows
    offset = row_index % block_rows * local_rows
    chain_mask = residue_mask.astype(jnp.float32)
    mask_rows = lax.dynamic_slice_in_dim(chain_mask, row_index * local_rows, local_rows)
    mask_cols = lax.dynamic_slice_in_dim(chain_mask, col_index * local_cols, local_cols)
    mask_pair = mask_rows[:, None] * mask_cols[None, :]

    def gather_rows(stacked):
        return lax.all_gather(stacked, "row", axis=1, tiled=True)

    def column_block(gathered):
        slab = lax.dynamic_slice_in_dim(gathered, offset, local_rows, 1)
        return from_root(slab, "col", owner_col)

    def gather_cols(values):
        return lax.all_gather(values, "col", axis=1, tiled=True)

    def sum_cols(partial_term):
        return lax.psum_scatter(
            partial_term.astype(jnp.bfloat16), "col", scatter_dimension=1, tiled=True
        ).astype(jnp.float32)

    (out_ops, out_gate), out_front_back = jax.vjp(
        lambda inner_pair: project_pair(inner_pair, mask_pair, front_weight[0]), pair_act
    )
    fetched = gather_rows(out_ops)
    out_mixed = sum_cols(
        jnp.einsum("ikc,jkc->ijc", out_ops[0], fetched[-1], preferred_element_type=jnp.float32)
    )
    pair_mid, out_finish_back = jax.vjp(
        lambda mixed_part, gate_value, inner_pair: finish(
            mixed_part, gate_value, inner_pair, out_weight[0]
        ),
        out_mixed,
        out_gate,
        pair_act,
    )
    (in_ops, in_gate), in_front_back = jax.vjp(
        lambda inner_pair: project_pair(inner_pair, mask_pair, front_weight[1]), pair_mid
    )
    in_fetched = gather_rows(in_ops)
    left_block = column_block(in_fetched[0])
    in_mixed = jnp.einsum(
        "kic,kjc->ijc", left_block, in_fetched[1], preferred_element_type=jnp.float32
    )
    unused_pair, in_finish_back = jax.vjp(
        lambda mixed_part, gate_value, inner_pair: finish(
            mixed_part, gate_value, inner_pair, out_weight[1]
        ),
        in_mixed,
        in_gate,
        pair_mid,
    )
    grad_mixed, grad_gate, grad_inner = in_finish_back(cotangent)
    signal = grad_mixed.astype(jnp.bfloat16)
    signal_rows = gather_rows(signal[None])[0]
    left_rows = gather_cols(in_ops[0])
    grad_right = jnp.einsum(
        "kic,ijc->kjc", left_rows, signal_rows, preferred_element_type=jnp.float32
    )
    grad_left = sum_cols(
        jnp.einsum("kjc,ijc->kic", in_ops[1], signal_rows, preferred_element_type=jnp.float32)
    )
    (grad_front,) = in_front_back(
        (jnp.stack((grad_left, grad_right)).astype(jnp.bfloat16), grad_gate)
    )
    grad_mid = (grad_inner.astype(jnp.float32) + grad_front.astype(jnp.float32)).astype(
        jnp.bfloat16
    )
    grad_mixed, grad_gate, grad_inner = out_finish_back(grad_mid)
    signal = grad_mixed.astype(jnp.bfloat16)
    signal_cols = gather_cols(signal)
    grad_left = jnp.einsum(
        "ijc,jkc->ikc", signal_cols, fetched[-1], preferred_element_type=jnp.float32
    )
    signal_block = column_block(gather_rows(signal[None])[0])
    grad_right = jnp.einsum(
        "ijc,ikc->jkc", signal_block, fetched[0], preferred_element_type=jnp.float32
    )
    (grad_front,) = out_front_back(
        (jnp.stack((grad_left, grad_right)).astype(jnp.bfloat16), grad_gate)
    )
    return (grad_inner.astype(jnp.float32) + grad_front.astype(jnp.float32)).astype(jnp.bfloat16)


def sigmoid(values):
    return 0.5 + 0.5 * jnp.tanh(0.5 * values)


def lane_mean(values):
    return jnp.mean(values, axis=-1, keepdims=True)


def normalize(values):
    centred = values - lane_mean(values)
    inverse = lax.rsqrt(lane_mean(centred * centred) + EPS)
    return centred * inverse, inverse


def normalize_back(grad, normed, inverse):
    return inverse * (grad - lane_mean(grad) - normed * lane_mean(grad * normed))


def rounded(values):
    return values.astype(BF16).astype(F32)


def matmul(values, weight):
    return jnp.dot(values.astype(BF16), weight, preferred_element_type=F32)


def matmul_t(values, weight):
    return lax.dot_general(
        values.astype(BF16), weight, (((1,), (1,)), ((), ())), preferred_element_type=F32
    )


def split(linear):
    return [linear[:, i * H : (i + 1) * H] for i in range(5)]


def front_back(linear, mask, grad_left, grad_right, grad_gate, weight, normed, inverse):
    gate_l, val_l, gate_r, val_r, gate = split(linear)
    gate_l, gate_r, gate = sigmoid(gate_l), sigmoid(gate_r), sigmoid(gate)
    grad_left, grad_right = grad_left * mask, grad_right * mask
    pieces = (
        grad_left * val_l * (gate_l * (1.0 - gate_l)),
        grad_left * gate_l,
        grad_right * val_r * (gate_r * (1.0 - gate_r)),
        grad_right * gate_r,
        grad_gate * (gate * (1.0 - gate)),
    )
    grad = jnp.concatenate([piece.astype(BF16) for piece in pieces], axis=1)
    return rounded(normalize_back(rounded(matmul_t(grad, weight)), normed, inverse))


def crop_kernel(
    n, rows, cols, blocks, mask_ref, own_ref, other_ref, front_ref, out_ref, grad_ref,
    act, cot, left, right, right_t, gate0, mixed0, mid, left1, right1, left1_t, right1_t,
    gate1, mixed1, sig, sig_t, grow, s_gate, s_sig, dl, dr,
):
    pitch = n + PAD
    row_index = lax.axis_index("row")
    col_index = lax.axis_index("col")
    chain = sum(mask_ref[i] for i in range(n))
    me = row_index * rows
    mine = pl.multiple_of(col_index * cols, cols)
    theirs = pl.multiple_of((1 - col_index) * cols, cols)
    step = rows * n

    for position, (block, half) in enumerate(blocks):
        here, there = (theirs, mine) if half else (mine, theirs)
        place = (row_index ^ block) * rows
        for a in range(rows):
            base = (place + a) * pitch
            for source, offset in ((own_ref, here), (other_ref, there)):
                act[pl.ds(base + offset, cols), :] = source[2 * position, a].astype(F32)
                cot[pl.ds(base + offset, cols), :] = source[2 * position + 1, a].astype(F32)

    def mask_of(count, span, start, offset):
        major = lax.broadcasted_iota(jnp.int32, (count, span, H), 0) + start
        minor = lax.broadcasted_iota(jnp.int32, (count, span, H), 1) + offset
        return jnp.where((major < chain) & (minor < chain), 1.0, 0.0).reshape(count * span, H)

    def get(ref, start=0, count=n):
        return jnp.concatenate(
            [ref[pl.ds((start + a) * pitch, n), :] for a in range(count)], axis=0
        )

    def put(ref, start, values, count=n):
        for a in range(count):
            ref[pl.ds((start + a) * pitch, n), :] = values[a * n : (a + 1) * n]

    def put_t(ref, values):
        for a in range(n):
            ref[pl.ds(a, n, stride=pitch), :] = values[a * n : (a + 1) * n]

    def get_t(ref):
        return [ref[pl.ds(me + a, n, stride=pitch), :] for a in range(rows)]

    def take(ref):
        return jnp.concatenate([get(ref, me, rows)] + get_t(ref), axis=0)

    def projection(u, source):
        mask = mask_of(n, n, 0, 0)
        normed, _ = normalize(source)
        linear = matmul(normed, front_ref[u])
        gate_l, val_l, gate_r, val_r, gate = split(linear)
        return (
            rounded(mask * (sigmoid(gate_l) * val_l)),
            rounded(mask * (sigmoid(gate_r) * val_r)),
            sigmoid(gate),
        )

    def product(count, span, row_of, ref_a, ref_b, minor, width, pitch_b=pitch):
        totals = [None] * count
        for s in range(span):
            block = ref_b[pl.ds(s * pitch_b + minor, width), :]
            for p in range(count):
                term = jnp.broadcast_to(ref_a[pl.ds(row_of(p, s), 1), :], (width, H)) * block
                totals[p] = term if totals[p] is None else totals[p] + term
        return totals

    a, b, g = projection(0, get(act))
    put(left, 0, a)
    put(right, 0, b)
    put_t(right_t, b)
    put(gate0, 0, g)

    for start in range(0, n, rows):
        totals = product(
            rows, n, lambda p, s: (start + p) * pitch + s, left, right_t, 0, n)
        put(mixed0, start, jnp.concatenate(totals, axis=0), rows)

    normed, _ = normalize(get(mixed0))
    value = rounded(get(act) + get(gate0) * matmul(normed, out_ref[0]))
    put(mid, 0, value)
    a, b, g = projection(1, value)
    put(left1, 0, a)
    put(right1, 0, b)
    put_t(left1_t, a)
    put_t(right1_t, b)
    put(gate1, 0, g)

    for start in range(0, n, rows):
        totals = product(rows, n, lambda p, s: s * pitch + start + p, left1, right1, 0, n)
        put(mixed1, start, jnp.concatenate(totals, axis=0), rows)

    normed, inverse = normalize(get(mixed1))
    grad = rounded(matmul_t(get(cot) * get(gate1), out_ref[1]))
    value = rounded(normalize_back(grad, normed, inverse))
    put(sig, 0, value)
    put_t(sig_t, value)

    def row_of(p, s):
        return (me + p) * pitch + s

    dl[pl.ds(0, step), :] = jnp.concatenate(
        product(rows, n, row_of, right1, sig_t, 0, n), axis=0)
    dl[pl.ds(step, step), :] = jnp.concatenate(
        product(rows, n, row_of, sig, right1_t, 0, n), axis=0)
    dr[pl.ds(0, step), :] = jnp.concatenate(
        product(rows, n, row_of, left1, sig, 0, n), axis=0)
    dr[pl.ds(step, step), :] = jnp.concatenate(
        product(rows, n, lambda p, s: s * pitch + me + p, sig, left1_t, 0, n), axis=0)

    mask_rows = mask_of(rows, n, me, 0)
    cot_s = take(cot)
    mixed, _ = normalize(take(mixed1))
    normed, inverse = normalize(take(mid))
    grad_gate = cot_s * matmul(mixed, out_ref[1])
    grad = front_back(
        matmul(normed, front_ref[1]), jnp.concatenate([mask_rows, mask_rows], axis=0),
        rounded(dl[...]), rounded(dr[...]), grad_gate, front_ref[1], normed, inverse)
    grad_mid = rounded(cot_s + grad)
    mixed, inverse = normalize(take(mixed0))
    grow[...] = grad_mid[:step]
    s_gate[...] = grad_mid[:step] * matmul(mixed[:step], out_ref[0])
    grad = rounded(matmul_t(grad_mid * take(gate0), out_ref[0]))
    s_sig[...] = rounded(normalize_back(grad, mixed, inverse))

    grad_left = product(rows, n, lambda p, s: p * n + s, s_sig, right, mine, cols)
    grad_right = product(rows, n, lambda p, s: step + p * n + s, s_sig, left, mine, cols)

    def own(ref, base, stride):
        return jnp.concatenate(
            [ref[pl.ds(base + a * stride + mine, cols), :] for a in range(rows)], axis=0)

    normed, inverse = normalize(own(act, me * pitch, pitch))
    grad = front_back(
        matmul(normed, front_ref[0]), mask_of(rows, cols, me, mine),
        rounded(jnp.concatenate(grad_left, axis=0)), rounded(jnp.concatenate(grad_right, axis=0)),
        own(s_gate, 0, n), front_ref[0], normed, inverse)
    grad_ref[...] = (own(grow, 0, n) + grad).astype(BF16).reshape(rows, cols, H)


def whole_body(pair_act, cotangent, residue_mask, front_weight, out_weight):
    rows, cols, width = pair_act.shape
    n = residue_mask.shape[0]
    row_count = lax.axis_size("row")
    bits = row_count.bit_length() - 1
    gathered = jnp.stack((pair_act, cotangent))
    blocks = [(0, 0)]
    for step in [1 << b for b in range(1, bits)] + [1]:
        pairs = [(2 * i + c, 2 * (i ^ step) + 1 - c) for i in range(row_count) for c in (0, 1)]
        gathered = jnp.concatenate((gathered, lax.ppermute(gathered, ("row", "col"), pairs)))
        blocks = blocks + [(b ^ step, 1 - half) for b, half in blocks]
    other = lax.ppermute(gathered, "col", [(0, 1), (1, 0)])
    full = pltpu.VMEM((n * (n + PAD), H), F32)
    some = pltpu.VMEM((rows * n, H), F32)
    twice = pltpu.VMEM((2 * rows * n, H), F32)
    vmem = pl.BlockSpec(memory_space=pltpu.VMEM)
    return pl.pallas_call(
        functools.partial(crop_kernel, n, rows, cols, blocks),
        out_shape=jax.ShapeDtypeStruct(pair_act.shape, BF16),
        in_specs=[pl.BlockSpec(memory_space=pltpu.SMEM)] + [vmem] * 4,
        out_specs=vmem,
        scratch_shapes=[full] * 16 + [some, some, twice, twice, twice],
        compiler_params=pltpu.CompilerParams(vmem_limit_bytes=VMEM_BUDGET),
    )(residue_mask, gathered, other, front_weight, out_weight)


def body(pair_act, cotangent, residue_mask, front_weight, out_weight):
    n = residue_mask.shape[0]
    row_count = lax.axis_size("row")
    fits = 20 * n * (n + PAD) * H * 4 <= VMEM_BUDGET
    doubling = row_count & (row_count - 1) == 0 and lax.axis_size("col") == 2
    run = whole_body if fits and doubling else spread_body
    return run(pair_act, cotangent, residue_mask, front_weight, out_weight)


def solution(mesh):
    placed = (P(("grp", "row"), "col", None), P(("grp", "row"), "col", None), P("grp"), P(), P())
    return jax.shard_map(
        body, mesh=mesh, in_specs=placed, out_specs=P(("grp", "row"), "col", None), check_vma=False
    )
```

```python
import functools

import jax
import jax.numpy as jnp
from jax import lax
from jax.experimental import pallas as pl
from jax.experimental.pallas import tpu as pltpu
from jax.sharding import PartitionSpec as P

H = 128
EPS = 1e-05
PAD = 4
VMEM_BUDGET = 40 << 20
F32 = jnp.float32
BF16 = jnp.bfloat16


def from_root(array, axis, root):
    mine = lax.axis_index(axis) == root
    return lax.psum(jnp.where(mine, array, jnp.zeros_like(array)), axis)


def layer_norm(values):
    centred = values - jnp.mean(values, axis=-1, keepdims=True)
    spread = jnp.mean(centred * centred, axis=-1, keepdims=True)
    return centred * lax.rsqrt(spread + 1e-05)


def project_pair(inner_pair, mask_pair, weight):
    normed = layer_norm(inner_pair.astype(jnp.float32)).astype(jnp.bfloat16)
    linear = jnp.dot(normed, weight, preferred_element_type=jnp.float32)
    left_side = jax.nn.sigmoid(linear[..., :H]) * linear[..., H : 2 * H]
    right_side = jax.nn.sigmoid(linear[..., 2 * H : 3 * H]) * linear[..., 3 * H : 4 * H]
    operands = (jnp.stack((left_side, right_side)) * mask_pair[None, :, :, None]).astype(
        jnp.bfloat16
    )
    return (operands, jax.nn.sigmoid(linear[..., 4 * H :]))


def finish(mixed_part, gate_value, inner_pair, weight):
    normed = layer_norm(mixed_part).astype(jnp.bfloat16)
    update = jnp.dot(normed, weight, preferred_element_type=jnp.float32)
    return (inner_pair.astype(jnp.float32) + gate_value * update).astype(jnp.bfloat16)


def spread_body(pair_act, cotangent, residue_mask, front_weight, out_weight):
    local_rows = pair_act.shape[0]
    local_cols = pair_act.shape[1]
    row_index = lax.axis_index("row")
    col_index = lax.axis_index("col")
    block_rows = lax.axis_size("row") // lax.axis_size("col")
    owner_col = row_index // block_rows
    offset = row_index % block_rows * local_rows
    chain_mask = residue_mask.astype(jnp.float32)
    mask_rows = lax.dynamic_slice_in_dim(chain_mask, row_index * local_rows, local_rows)
    mask_cols = lax.dynamic_slice_in_dim(chain_mask, col_index * local_cols, local_cols)
    mask_pair = mask_rows[:, None] * mask_cols[None, :]

    def gather_rows(stacked):
        return lax.all_gather(stacked, "row", axis=1, tiled=True)

    def column_block(gathered):
        slab = lax.dynamic_slice_in_dim(gathered, offset, local_rows, 1)
        return from_root(slab, "col", owner_col)

    def gather_cols(values):
        return lax.all_gather(values, "col", axis=1, tiled=True)

    def sum_cols(partial_term):
        return lax.psum_scatter(
            partial_term.astype(jnp.bfloat16), "col", scatter_dimension=1, tiled=True
        ).astype(jnp.float32)

    (out_ops, out_gate), out_front_back = jax.vjp(
        lambda inner_pair: project_pair(inner_pair, mask_pair, front_weight[0]), pair_act
    )
    fetched = gather_rows(out_ops)
    out_mixed = sum_cols(
        jnp.einsum("ikc,jkc->ijc", out_ops[0], fetched[-1], preferred_element_type=jnp.float32)
    )
    pair_mid, out_finish_back = jax.vjp(
        lambda mixed_part, gate_value, inner_pair: finish(
            mixed_part, gate_value, inner_pair, out_weight[0]
        ),
        out_mixed,
        out_gate,
        pair_act,
    )
    (in_ops, in_gate), in_front_back = jax.vjp(
        lambda inner_pair: project_pair(inner_pair, mask_pair, front_weight[1]), pair_mid
    )
    in_fetched = gather_rows(in_ops)
    left_block = column_block(in_fetched[0])
    in_mixed = jnp.einsum(
        "kic,kjc->ijc", left_block, in_fetched[1], preferred_element_type=jnp.float32
    )
    unused_pair, in_finish_back = jax.vjp(
        lambda mixed_part, gate_value, inner_pair: finish(
            mixed_part, gate_value, inner_pair, out_weight[1]
        ),
        in_mixed,
        in_gate,
        pair_mid,
    )
    grad_mixed, grad_gate, grad_inner = in_finish_back(cotangent)
    signal = grad_mixed.astype(jnp.bfloat16)
    signal_rows = gather_rows(signal[None])[0]
    left_rows = gather_cols(in_ops[0])
    grad_right = jnp.einsum(
        "kic,ijc->kjc", left_rows, signal_rows, preferred_element_type=jnp.float32
    )
    grad_left = sum_cols(
        jnp.einsum("kjc,ijc->kic", in_ops[1], signal_rows, preferred_element_type=jnp.float32)
    )
    (grad_front,) = in_front_back(
        (jnp.stack((grad_left, grad_right)).astype(jnp.bfloat16), grad_gate)
    )
    grad_mid = (grad_inner.astype(jnp.float32) + grad_front.astype(jnp.float32)).astype(
        jnp.bfloat16
    )
    grad_mixed, grad_gate, grad_inner = out_finish_back(grad_mid)
    signal = grad_mixed.astype(jnp.bfloat16)
    signal_cols = gather_cols(signal)
    grad_left = jnp.einsum(
        "ijc,jkc->ikc", signal_cols, fetched[-1], preferred_element_type=jnp.float32
    )
    signal_block = column_block(gather_rows(signal[None])[0])
    grad_right = jnp.einsum(
        "ijc,ikc->jkc", signal_block, fetched[0], preferred_element_type=jnp.float32
    )
    (grad_front,) = out_front_back(
        (jnp.stack((grad_left, grad_right)).astype(jnp.bfloat16), grad_gate)
    )
    return (grad_inner.astype(jnp.float32) + grad_front.astype(jnp.float32)).astype(jnp.bfloat16)


def sigmoid(values):
    return 0.5 + 0.5 * jnp.tanh(0.5 * values)


def lane_mean(values):
    return jnp.mean(values, axis=-1, keepdims=True)


def normalize(values):
    centred = values - lane_mean(values)
    inverse = lax.rsqrt(lane_mean(centred * centred) + EPS)
    return centred * inverse, inverse


def normalize_back(grad, normed, inverse):
    return inverse * (grad - lane_mean(grad) - normed * lane_mean(grad * normed))


def rounded(values):
    return values.astype(BF16).astype(F32)


def matmul(values, weight):
    return jnp.dot(values.astype(BF16), weight, preferred_element_type=F32)


def matmul_t(values, weight):
    return lax.dot_general(
        values.astype(BF16), weight, (((1,), (1,)), ((), ())), preferred_element_type=F32
    )


def split(linear):
    return [linear[:, i * H : (i + 1) * H] for i in range(5)]


def front_back(linear, mask, grad_left, grad_right, grad_gate, weight, normed, inverse):
    gate_l, val_l, gate_r, val_r, gate = split(linear)
    gate_l, gate_r, gate = sigmoid(gate_l), sigmoid(gate_r), sigmoid(gate)
    grad_left, grad_right = grad_left * mask, grad_right * mask
    pieces = (
        grad_left * val_l * (gate_l * (1.0 - gate_l)),
        grad_left * gate_l,
        grad_right * val_r * (gate_r * (1.0 - gate_r)),
        grad_right * gate_r,
        grad_gate * (gate * (1.0 - gate)),
    )
    grad = jnp.concatenate([piece.astype(BF16) for piece in pieces], axis=1)
    return rounded(normalize_back(rounded(matmul_t(grad, weight)), normed, inverse))


def pair_mask(chain, count, span, start, offset):
    major = lax.broadcasted_iota(jnp.int32, (count, span, H), 0) + start
    minor = lax.broadcasted_iota(jnp.int32, (count, span, H), 1) + offset
    return jnp.where((major < chain) & (minor < chain), 1.0, 0.0).reshape(count * span, H)


def projection(weight, source, mask):
    normed, _ = normalize(source)
    gate_l, val_l, gate_r, val_r, gate = split(matmul(normed, weight))
    return (
        rounded(mask * (sigmoid(gate_l) * val_l)),
        rounded(mask * (sigmoid(gate_r) * val_r)),
        sigmoid(gate),
    )


def product(count, span, row_of, ref_a, ref_b, pitch, minor, width):
    totals = [None] * count
    for s in range(span):
        block = ref_b[pl.ds(s * pitch + minor, width), :]
        for p in range(count):
            term = jnp.broadcast_to(ref_a[pl.ds(row_of(p, s), 1), :], (width, H)) * block
            totals[p] = term if totals[p] is None else totals[p] + term
    return totals


def half_kernel(
    n, rows, cols, blocks, mask_ref, own_ref, front_ref, left, right, gate, part, act, right_t,
):
    pitch = n + PAD
    row_index = lax.axis_index("row")
    chain = sum(mask_ref[i] for i in range(n))
    for position, block in enumerate(blocks):
        place = (row_index ^ block) * rows
        for a in range(rows):
            where = pl.ds(pl.multiple_of((place + a) * cols, cols), cols)
            act[where, :] = own_ref[2 * position, a].astype(F32)
    mask = pair_mask(chain, n, cols, 0, lax.axis_index("col") * cols)
    a, b, g = projection(front_ref[0], act[...], mask)
    left[...] = a
    right[...] = b
    gate[...] = g
    for i in range(n):
        right_t[pl.ds(i, cols, stride=pitch), :] = b[i * cols : (i + 1) * cols]
    for start in range(0, n, rows):
        totals = product(
            rows, cols, lambda p, s: (start + p) * cols + s, left, right_t, pitch, 0, n)
        part[pl.ds(start * n, rows * n), :] = jnp.concatenate(totals, axis=0)


def crop_kernel(
    n, rows, cols, blocks, mask_ref, own_ref, other_ref, front_ref, out_ref,
    half_left, half_right, half_gate, part, grad_ref,
    act, cot, left, right, right_t, gate0, mixed0, mid, left1, right1, left1_t, right1_t,
    gate1, mixed1, sig, sig_t, grow, s_gate, s_sig, dl, dr,
):
    pitch = n + PAD
    row_index = lax.axis_index("row")
    col_index = lax.axis_index("col")
    chain = sum(mask_ref[i] for i in range(n))
    me = row_index * rows
    mine = pl.multiple_of(col_index * cols, cols)
    theirs = pl.multiple_of((1 - col_index) * cols, cols)
    step = rows * n

    for position, block in enumerate(blocks):
        place = (row_index ^ block) * rows
        for a in range(rows):
            base = (place + a) * pitch
            for source, offset in ((own_ref, mine), (other_ref, theirs)):
                act[pl.ds(base + offset, cols), :] = source[2 * position, a].astype(F32)
                cot[pl.ds(base + offset, cols), :] = source[2 * position + 1, a].astype(F32)

    def mask_of(count, span, start, offset):
        return pair_mask(chain, count, span, start, offset)

    def get(ref, start=0, count=n):
        return jnp.concatenate(
            [ref[pl.ds((start + a) * pitch, n), :] for a in range(count)], axis=0
        )

    def put(ref, start, values, count=n):
        for a in range(count):
            ref[pl.ds((start + a) * pitch, n), :] = values[a * n : (a + 1) * n]

    def put_t(ref, values):
        for a in range(n):
            ref[pl.ds(a, n, stride=pitch), :] = values[a * n : (a + 1) * n]

    def get_t(ref):
        return [ref[pl.ds(me + a, n, stride=pitch), :] for a in range(rows)]

    def take(ref):
        return jnp.concatenate([get(ref, me, rows)] + get_t(ref), axis=0)

    source = jnp.concatenate(
        [act[pl.ds(i * pitch + theirs, cols), :] for i in range(n)], axis=0)
    a, b, g = projection(front_ref[0], source, mask_of(n, cols, 0, theirs))
    for i in range(n):
        these = slice(i * cols, (i + 1) * cols)
        right_t[pl.ds(i, cols, stride=pitch), :] = b[these]
        for ref, done, new in (
            (left, half_left, a), (right, half_right, b), (gate0, half_gate, g)):
            ref[pl.ds(i * pitch + theirs, cols), :] = new[these]
            ref[pl.ds(i * pitch + mine, cols), :] = done[pl.ds(i * cols, cols), :]

    for start in range(0, n, rows):
        totals = product(
            rows, cols, lambda p, s: (start + p) * pitch + theirs + s, left, right_t, pitch, 0, n)
        rest = part[pl.ds(start * n, rows * n), :]
        put(mixed0, start, jnp.concatenate(totals, axis=0) + rest, rows)

    normed, _ = normalize(get(mixed0))
    value = rounded(get(act) + get(gate0) * matmul(normed, out_ref[0]))
    put(mid, 0, value)
    a, b, g = projection(front_ref[1], value, mask_of(n, n, 0, 0))
    put(left1, 0, a)
    put(right1, 0, b)
    put_t(left1_t, a)
    put_t(right1_t, b)
    put(gate1, 0, g)

    for start in range(0, n, rows):
        totals = product(rows, n, lambda p, s: s * pitch + start + p, left1, right1, pitch, 0, n)
        put(mixed1, start, jnp.concatenate(totals, axis=0), rows)

    normed, inverse = normalize(get(mixed1))
    grad = rounded(matmul_t(get(cot) * get(gate1), out_ref[1]))
    value = rounded(normalize_back(grad, normed, inverse))
    put(sig, 0, value)
    put_t(sig_t, value)

    def row_of(p, s):
        return (me + p) * pitch + s

    dl[pl.ds(0, step), :] = jnp.concatenate(
        product(rows, n, row_of, right1, sig_t, pitch, 0, n), axis=0)
    dl[pl.ds(step, step), :] = jnp.concatenate(
        product(rows, n, row_of, sig, right1_t, pitch, 0, n), axis=0)
    dr[pl.ds(0, step), :] = jnp.concatenate(
        product(rows, n, row_of, left1, sig, pitch, 0, n), axis=0)
    dr[pl.ds(step, step), :] = jnp.concatenate(
        product(rows, n, lambda p, s: s * pitch + me + p, sig, left1_t, pitch, 0, n), axis=0)

    mask_rows = mask_of(rows, n, me, 0)
    cot_s = take(cot)
    mixed, _ = normalize(take(mixed1))
    normed, inverse = normalize(take(mid))
    grad_gate = cot_s * matmul(mixed, out_ref[1])
    grad = front_back(
        matmul(normed, front_ref[1]), jnp.concatenate([mask_rows, mask_rows], axis=0),
        rounded(dl[...]), rounded(dr[...]), grad_gate, front_ref[1], normed, inverse)
    grad_mid = rounded(cot_s + grad)
    mixed, inverse = normalize(take(mixed0))
    grow[...] = grad_mid[:step]
    s_gate[...] = grad_mid[:step] * matmul(mixed[:step], out_ref[0])
    grad = rounded(matmul_t(grad_mid * take(gate0), out_ref[0]))
    s_sig[...] = rounded(normalize_back(grad, mixed, inverse))

    grad_left = product(rows, n, lambda p, s: p * n + s, s_sig, right, pitch, mine, cols)
    grad_right = product(rows, n, lambda p, s: step + p * n + s, s_sig, left, pitch, mine, cols)

    def own(ref, base, stride):
        return jnp.concatenate(
            [ref[pl.ds(base + a * stride + mine, cols), :] for a in range(rows)], axis=0)

    normed, inverse = normalize(own(act, me * pitch, pitch))
    grad = front_back(
        matmul(normed, front_ref[0]), mask_of(rows, cols, me, mine),
        rounded(jnp.concatenate(grad_left, axis=0)), rounded(jnp.concatenate(grad_right, axis=0)),
        own(s_gate, 0, n), front_ref[0], normed, inverse)
    grad_ref[...] = (own(grow, 0, n) + grad).astype(BF16).reshape(rows, cols, H)


def whole_body(pair_act, cotangent, residue_mask, front_weight, out_weight):
    rows, cols, width = pair_act.shape
    n = residue_mask.shape[0]
    row_count = lax.axis_size("row")
    bits = row_count.bit_length() - 1
    gathered = jnp.stack((pair_act, cotangent))
    blocks = [0]
    for step in [1 << b for b in range(1, bits)] + [1]:
        other = lax.ppermute(gathered, "row", [(i, i ^ step) for i in range(row_count)])
        gathered = jnp.concatenate((gathered, other))
        blocks = blocks + [b ^ step for b in blocks]
    other = lax.ppermute(gathered, "col", [(0, 1), (1, 0)])
    full = pltpu.VMEM((n * (n + PAD), H), F32)
    some = pltpu.VMEM((rows * n, H), F32)
    twice = pltpu.VMEM((2 * rows * n, H), F32)
    vmem = pl.BlockSpec(memory_space=pltpu.VMEM)
    smem = pl.BlockSpec(memory_space=pltpu.SMEM)
    part_of = jax.ShapeDtypeStruct((n * cols, H), F32)
    halves = pl.pallas_call(
        functools.partial(half_kernel, n, rows, cols, blocks),
        out_shape=[part_of] * 3 + [jax.ShapeDtypeStruct((n * n, H), F32)],
        in_specs=[smem, vmem, vmem],
        out_specs=[vmem] * 4,
        scratch_shapes=[pltpu.VMEM((n * cols, H), F32), pltpu.VMEM((cols * (n + PAD), H), F32)],
        compiler_params=pltpu.CompilerParams(vmem_limit_bytes=VMEM_BUDGET // 4),
    )(residue_mask, gathered, front_weight)
    return pl.pallas_call(
        functools.partial(crop_kernel, n, rows, cols, blocks),
        out_shape=jax.ShapeDtypeStruct(pair_act.shape, BF16),
        in_specs=[smem] + [vmem] * 8,
        out_specs=vmem,
        scratch_shapes=[full] * 16 + [some, some, twice, twice, twice],
        compiler_params=pltpu.CompilerParams(vmem_limit_bytes=VMEM_BUDGET),
    )(residue_mask, gathered, other, front_weight, out_weight, *halves)


def body(pair_act, cotangent, residue_mask, front_weight, out_weight):
    n = residue_mask.shape[0]
    row_count = lax.axis_size("row")
    fits = 20 * n * (n + PAD) * H * 4 <= VMEM_BUDGET
    doubling = row_count & (row_count - 1) == 0 and lax.axis_size("col") == 2
    run = whole_body if fits and doubling else spread_body
    return run(pair_act, cotangent, residue_mask, front_weight, out_weight)


def solution(mesh):
    placed = (P(("grp", "row"), "col", None), P(("grp", "row"), "col", None), P("grp"), P(), P())
    return jax.shard_map(
        body, mesh=mesh, in_specs=placed, out_specs=P(("grp", "row"), "col", None), check_vma=False
    )
```

```python
import functools

import jax
import jax.numpy as jnp
from jax import lax
from jax.experimental import pallas as pl
from jax.experimental.pallas import tpu as pltpu
from jax.sharding import PartitionSpec as P

H = 128
EPS = 1e-05
PAD = 4
VMEM_BUDGET = 40 << 20
F32 = jnp.float32
BF16 = jnp.bfloat16


def from_root(array, axis, root):
    mine = lax.axis_index(axis) == root
    return lax.psum(jnp.where(mine, array, jnp.zeros_like(array)), axis)


def layer_norm(values):
    centred = values - jnp.mean(values, axis=-1, keepdims=True)
    spread = jnp.mean(centred * centred, axis=-1, keepdims=True)
    return centred * lax.rsqrt(spread + 1e-05)


def project_pair(inner_pair, mask_pair, weight):
    normed = layer_norm(inner_pair.astype(jnp.float32)).astype(jnp.bfloat16)
    linear = jnp.dot(normed, weight, preferred_element_type=jnp.float32)
    left_side = jax.nn.sigmoid(linear[..., :H]) * linear[..., H : 2 * H]
    right_side = jax.nn.sigmoid(linear[..., 2 * H : 3 * H]) * linear[..., 3 * H : 4 * H]
    operands = (jnp.stack((left_side, right_side)) * mask_pair[None, :, :, None]).astype(
        jnp.bfloat16
    )
    return (operands, jax.nn.sigmoid(linear[..., 4 * H :]))


def finish(mixed_part, gate_value, inner_pair, weight):
    normed = layer_norm(mixed_part).astype(jnp.bfloat16)
    update = jnp.dot(normed, weight, preferred_element_type=jnp.float32)
    return (inner_pair.astype(jnp.float32) + gate_value * update).astype(jnp.bfloat16)


def spread_body(pair_act, cotangent, residue_mask, front_weight, out_weight):
    local_rows = pair_act.shape[0]
    local_cols = pair_act.shape[1]
    row_index = lax.axis_index("row")
    col_index = lax.axis_index("col")
    block_rows = lax.axis_size("row") // lax.axis_size("col")
    owner_col = row_index // block_rows
    offset = row_index % block_rows * local_rows
    chain_mask = residue_mask.astype(jnp.float32)
    mask_rows = lax.dynamic_slice_in_dim(chain_mask, row_index * local_rows, local_rows)
    mask_cols = lax.dynamic_slice_in_dim(chain_mask, col_index * local_cols, local_cols)
    mask_pair = mask_rows[:, None] * mask_cols[None, :]

    def gather_rows(stacked):
        return lax.all_gather(stacked, "row", axis=1, tiled=True)

    def column_block(gathered):
        slab = lax.dynamic_slice_in_dim(gathered, offset, local_rows, 1)
        return from_root(slab, "col", owner_col)

    def gather_cols(values):
        return lax.all_gather(values, "col", axis=1, tiled=True)

    def sum_cols(partial_term):
        return lax.psum_scatter(
            partial_term.astype(jnp.bfloat16), "col", scatter_dimension=1, tiled=True
        ).astype(jnp.float32)

    (out_ops, out_gate), out_front_back = jax.vjp(
        lambda inner_pair: project_pair(inner_pair, mask_pair, front_weight[0]), pair_act
    )
    fetched = gather_rows(out_ops)
    out_mixed = sum_cols(
        jnp.einsum("ikc,jkc->ijc", out_ops[0], fetched[-1], preferred_element_type=jnp.float32)
    )
    pair_mid, out_finish_back = jax.vjp(
        lambda mixed_part, gate_value, inner_pair: finish(
            mixed_part, gate_value, inner_pair, out_weight[0]
        ),
        out_mixed,
        out_gate,
        pair_act,
    )
    (in_ops, in_gate), in_front_back = jax.vjp(
        lambda inner_pair: project_pair(inner_pair, mask_pair, front_weight[1]), pair_mid
    )
    in_fetched = gather_rows(in_ops)
    left_block = column_block(in_fetched[0])
    in_mixed = jnp.einsum(
        "kic,kjc->ijc", left_block, in_fetched[1], preferred_element_type=jnp.float32
    )
    unused_pair, in_finish_back = jax.vjp(
        lambda mixed_part, gate_value, inner_pair: finish(
            mixed_part, gate_value, inner_pair, out_weight[1]
        ),
        in_mixed,
        in_gate,
        pair_mid,
    )
    grad_mixed, grad_gate, grad_inner = in_finish_back(cotangent)
    signal = grad_mixed.astype(jnp.bfloat16)
    signal_rows = gather_rows(signal[None])[0]
    left_rows = gather_cols(in_ops[0])
    grad_right = jnp.einsum(
        "kic,ijc->kjc", left_rows, signal_rows, preferred_element_type=jnp.float32
    )
    grad_left = sum_cols(
        jnp.einsum("kjc,ijc->kic", in_ops[1], signal_rows, preferred_element_type=jnp.float32)
    )
    (grad_front,) = in_front_back(
        (jnp.stack((grad_left, grad_right)).astype(jnp.bfloat16), grad_gate)
    )
    grad_mid = (grad_inner.astype(jnp.float32) + grad_front.astype(jnp.float32)).astype(
        jnp.bfloat16
    )
    grad_mixed, grad_gate, grad_inner = out_finish_back(grad_mid)
    signal = grad_mixed.astype(jnp.bfloat16)
    signal_cols = gather_cols(signal)
    grad_left = jnp.einsum(
        "ijc,jkc->ikc", signal_cols, fetched[-1], preferred_element_type=jnp.float32
    )
    signal_block = column_block(gather_rows(signal[None])[0])
    grad_right = jnp.einsum(
        "ijc,ikc->jkc", signal_block, fetched[0], preferred_element_type=jnp.float32
    )
    (grad_front,) = out_front_back(
        (jnp.stack((grad_left, grad_right)).astype(jnp.bfloat16), grad_gate)
    )
    return (grad_inner.astype(jnp.float32) + grad_front.astype(jnp.float32)).astype(jnp.bfloat16)


def sigmoid(values):
    return 0.5 + 0.5 * jnp.tanh(0.5 * values)


def lane_mean(values):
    return jnp.mean(values, axis=-1, keepdims=True)


def normalize(values):
    centred = values - lane_mean(values)
    inverse = lax.rsqrt(lane_mean(centred * centred) + EPS)
    return centred * inverse, inverse


def normalize_back(grad, normed, inverse):
    return inverse * (grad - lane_mean(grad) - normed * lane_mean(grad * normed))


def rounded(values):
    return values.astype(BF16).astype(F32)


def matmul(values, weight):
    return jnp.dot(values.astype(BF16), weight, preferred_element_type=F32)


def matmul_t(values, weight):
    return lax.dot_general(
        values.astype(BF16), weight, (((1,), (1,)), ((), ())), preferred_element_type=F32
    )


def split(linear):
    return [linear[:, i * H : (i + 1) * H] for i in range(5)]


def front_back(linear, mask, grad_left, grad_right, grad_gate, weight, normed, inverse):
    gate_l, val_l, gate_r, val_r, gate = split(linear)
    gate_l, gate_r, gate = sigmoid(gate_l), sigmoid(gate_r), sigmoid(gate)
    grad_left, grad_right = grad_left * mask, grad_right * mask
    pieces = (
        grad_left * val_l * (gate_l * (1.0 - gate_l)),
        grad_left * gate_l,
        grad_right * val_r * (gate_r * (1.0 - gate_r)),
        grad_right * gate_r,
        grad_gate * (gate * (1.0 - gate)),
    )
    grad = jnp.concatenate([piece.astype(BF16) for piece in pieces], axis=1)
    return rounded(normalize_back(rounded(matmul_t(grad, weight)), normed, inverse))


def chain_length(mask_ref):
    return jnp.sum(mask_ref[...].astype(F32), axis=1, keepdims=True).astype(jnp.int32)


def pair_mask(chain, count, span, start, offset):
    major = lax.broadcasted_iota(jnp.int32, (count, span, H), 0) + start
    minor = lax.broadcasted_iota(jnp.int32, (count, span, H), 1) + offset
    inside = jnp.maximum(major, minor).reshape(count * span, H) < chain
    return jnp.where(inside, 1.0, 0.0)


def projection(weight, source, mask):
    normed, _ = normalize(source)
    gate_l, val_l, gate_r, val_r, gate = split(matmul(normed, weight))
    return (
        rounded(mask * (sigmoid(gate_l) * val_l)),
        rounded(mask * (sigmoid(gate_r) * val_r)),
        sigmoid(gate),
    )


def product(count, span, row_of, ref_a, ref_b, pitch, minor, width):
    totals = [None] * count
    for s in range(span):
        block = ref_b[pl.ds(s * pitch + minor, width), :]
        for p in range(count):
            term = jnp.broadcast_to(ref_a[pl.ds(row_of(p, s), 1), :], (width, H)) * block
            totals[p] = term if totals[p] is None else totals[p] + term
    return totals


def half_kernel(
    n, rows, cols, blocks, mask_ref, own_ref, front_ref, left, right, gate, part, act, right_t,
):
    pitch = n + PAD
    row_index = lax.axis_index("row")
    chain = chain_length(mask_ref)
    for position, block in enumerate(blocks):
        place = (row_index ^ block) * rows
        for a in range(rows):
            where = pl.ds(pl.multiple_of((place + a) * cols, cols), cols)
            act[where, :] = own_ref[2 * position, a].astype(F32)
    mask = pair_mask(chain, n, cols, 0, lax.axis_index("col") * cols)
    a, b, g = projection(front_ref[0], act[...], mask)
    left[...] = a
    right[...] = b
    gate[...] = g
    for i in range(n):
        right_t[pl.ds(i, cols, stride=pitch), :] = b[i * cols : (i + 1) * cols]
    for start in range(0, n, rows):
        totals = product(
            rows, cols, lambda p, s: (start + p) * cols + s, left, right_t, pitch, 0, n)
        part[pl.ds(start * n, rows * n), :] = jnp.concatenate(totals, axis=0)


def crop_kernel(
    n, rows, cols, blocks, mask_ref, own_ref, other_ref, front_ref, out_ref,
    half_left, half_right, half_gate, part, grad_ref,
    act, cot, left, right, right_t, gate0, mixed0, mid, left1, right1, left1_t, right1_t,
    gate1, mixed1, sig, sig_t, grow, s_gate, s_sig, dl, dr,
):
    pitch = n + PAD
    row_index = lax.axis_index("row")
    col_index = lax.axis_index("col")
    chain = chain_length(mask_ref)
    me = row_index * rows
    mine = pl.multiple_of(col_index * cols, cols)
    theirs = pl.multiple_of((1 - col_index) * cols, cols)
    step = rows * n

    for position, block in enumerate(blocks):
        place = (row_index ^ block) * rows
        for a in range(rows):
            base = (place + a) * pitch
            for source, offset in ((own_ref, mine), (other_ref, theirs)):
                act[pl.ds(base + offset, cols), :] = source[2 * position, a].astype(F32)
                cot[pl.ds(base + offset, cols), :] = source[2 * position + 1, a].astype(F32)

    def mask_of(count, span, start, offset):
        return pair_mask(chain, count, span, start, offset)

    def get(ref, start=0, count=n):
        return jnp.concatenate(
            [ref[pl.ds((start + a) * pitch, n), :] for a in range(count)], axis=0
        )

    def put(ref, start, values, count=n):
        for a in range(count):
            ref[pl.ds((start + a) * pitch, n), :] = values[a * n : (a + 1) * n]

    def put_t(ref, values):
        for a in range(n):
            ref[pl.ds(a, n, stride=pitch), :] = values[a * n : (a + 1) * n]

    def get_t(ref):
        return [ref[pl.ds(me + a, n, stride=pitch), :] for a in range(rows)]

    def take(ref):
        return jnp.concatenate([get(ref, me, rows)] + get_t(ref), axis=0)

    source = jnp.concatenate(
        [act[pl.ds(i * pitch + theirs, cols), :] for i in range(n)], axis=0)
    a, b, g = projection(front_ref[0], source, mask_of(n, cols, 0, theirs))
    for i in range(n):
        these = slice(i * cols, (i + 1) * cols)
        right_t[pl.ds(i, cols, stride=pitch), :] = b[these]
        for ref, done, new in (
            (left, half_left, a), (right, half_right, b), (gate0, half_gate, g)):
            ref[pl.ds(i * pitch + theirs, cols), :] = new[these]
            ref[pl.ds(i * pitch + mine, cols), :] = done[pl.ds(i * cols, cols), :]

    for start in range(0, n, rows):
        totals = product(
            rows, cols, lambda p, s: (start + p) * pitch + theirs + s, left, right_t, pitch, 0, n)
        rest = part[pl.ds(start * n, rows * n), :]
        put(mixed0, start, jnp.concatenate(totals, axis=0) + rest, rows)

    normed, _ = normalize(get(mixed0))
    value = rounded(get(act) + get(gate0) * matmul(normed, out_ref[0]))
    put(mid, 0, value)
    a, b, g = projection(front_ref[1], value, mask_of(n, n, 0, 0))
    put(left1, 0, a)
    put(right1, 0, b)
    put_t(left1_t, a)
    put_t(right1_t, b)
    put(gate1, 0, g)

    for start in range(0, n, rows):
        totals = product(rows, n, lambda p, s: s * pitch + start + p, left1, right1, pitch, 0, n)
        put(mixed1, start, jnp.concatenate(totals, axis=0), rows)

    normed, inverse = normalize(get(mixed1))
    grad = rounded(matmul_t(get(cot) * get(gate1), out_ref[1]))
    value = rounded(normalize_back(grad, normed, inverse))
    put(sig, 0, value)
    put_t(sig_t, value)

    def row_of(p, s):
        return (me + p) * pitch + s

    dl[pl.ds(0, step), :] = jnp.concatenate(
        product(rows, n, row_of, right1, sig_t, pitch, 0, n), axis=0)
    dl[pl.ds(step, step), :] = jnp.concatenate(
        product(rows, n, row_of, sig, right1_t, pitch, 0, n), axis=0)
    dr[pl.ds(0, step), :] = jnp.concatenate(
        product(rows, n, row_of, left1, sig, pitch, 0, n), axis=0)
    dr[pl.ds(step, step), :] = jnp.concatenate(
        product(rows, n, lambda p, s: s * pitch + me + p, sig, left1_t, pitch, 0, n), axis=0)

    mask_rows = mask_of(rows, n, me, 0)
    cot_s = take(cot)
    mixed, _ = normalize(take(mixed1))
    normed, inverse = normalize(take(mid))
    grad_gate = cot_s * matmul(mixed, out_ref[1])
    grad = front_back(
        matmul(normed, front_ref[1]), jnp.concatenate([mask_rows, mask_rows], axis=0),
        rounded(dl[...]), rounded(dr[...]), grad_gate, front_ref[1], normed, inverse)
    grad_mid = rounded(cot_s + grad)
    mixed, inverse = normalize(take(mixed0))
    grow[...] = grad_mid[:step]
    s_gate[...] = grad_mid[:step] * matmul(mixed[:step], out_ref[0])
    grad = rounded(matmul_t(grad_mid * take(gate0), out_ref[0]))
    s_sig[...] = rounded(normalize_back(grad, mixed, inverse))

    grad_left = product(rows, n, lambda p, s: p * n + s, s_sig, right, pitch, mine, cols)
    grad_right = product(rows, n, lambda p, s: step + p * n + s, s_sig, left, pitch, mine, cols)

    def own(ref, base, stride):
        return jnp.concatenate(
            [ref[pl.ds(base + a * stride + mine, cols), :] for a in range(rows)], axis=0)

    normed, inverse = normalize(own(act, me * pitch, pitch))
    grad = front_back(
        matmul(normed, front_ref[0]), mask_of(rows, cols, me, mine),
        rounded(jnp.concatenate(grad_left, axis=0)), rounded(jnp.concatenate(grad_right, axis=0)),
        own(s_gate, 0, n), front_ref[0], normed, inverse)
    grad_ref[...] = (own(grow, 0, n) + grad).astype(BF16).reshape(rows, cols, H)


def whole_body(pair_act, cotangent, residue_mask, front_weight, out_weight):
    rows, cols, width = pair_act.shape
    n = residue_mask.shape[0]
    mask = residue_mask.reshape(1, n)
    row_count = lax.axis_size("row")
    bits = row_count.bit_length() - 1
    gathered = jnp.stack((pair_act, cotangent))
    blocks = [0]
    for step in [1 << b for b in range(1, bits)] + [1]:
        other = lax.ppermute(gathered, "row", [(i, i ^ step) for i in range(row_count)])
        gathered = jnp.concatenate((gathered, other))
        blocks = blocks + [b ^ step for b in blocks]
    other = lax.ppermute(gathered, "col", [(0, 1), (1, 0)])
    full = pltpu.VMEM((n * (n + PAD), H), F32)
    some = pltpu.VMEM((rows * n, H), F32)
    twice = pltpu.VMEM((2 * rows * n, H), F32)
    vmem = pl.BlockSpec(memory_space=pltpu.VMEM)
    part_of = jax.ShapeDtypeStruct((n * cols, H), F32)
    halves = pl.pallas_call(
        functools.partial(half_kernel, n, rows, cols, blocks),
        out_shape=[part_of] * 3 + [jax.ShapeDtypeStruct((n * n, H), F32)],
        in_specs=[vmem] * 3,
        out_specs=[vmem] * 4,
        scratch_shapes=[pltpu.VMEM((n * cols, H), F32), pltpu.VMEM((cols * (n + PAD), H), F32)],
        compiler_params=pltpu.CompilerParams(vmem_limit_bytes=VMEM_BUDGET // 4),
    )(mask, gathered, front_weight)
    return pl.pallas_call(
        functools.partial(crop_kernel, n, rows, cols, blocks),
        out_shape=jax.ShapeDtypeStruct(pair_act.shape, BF16),
        in_specs=[vmem] * 9,
        out_specs=vmem,
        scratch_shapes=[full] * 16 + [some, some, twice, twice, twice],
        compiler_params=pltpu.CompilerParams(vmem_limit_bytes=VMEM_BUDGET),
    )(mask, gathered, other, front_weight, out_weight, *halves)


def body(pair_act, cotangent, residue_mask, front_weight, out_weight):
    n = residue_mask.shape[0]
    row_count = lax.axis_size("row")
    fits = 20 * n * (n + PAD) * H * 4 <= VMEM_BUDGET
    doubling = row_count & (row_count - 1) == 0 and lax.axis_size("col") == 2
    run = whole_body if fits and doubling else spread_body
    return run(pair_act, cotangent, residue_mask, front_weight, out_weight)


def solution(mesh):
    placed = (P(("grp", "row"), "col", None), P(("grp", "row"), "col", None), P("grp"), P(), P())
    return jax.shard_map(
        body, mesh=mesh, in_specs=placed, out_specs=P(("grp", "row"), "col", None), check_vma=False
    )
```

```python
import functools

import jax
import jax.numpy as jnp
from jax import lax
from jax.experimental import pallas as pl
from jax.experimental.pallas import tpu as pltpu
from jax.sharding import PartitionSpec as P

H = 128
EPS = 1e-05
PAD = 4
VMEM_BUDGET = 40 << 20
F32 = jnp.float32
BF16 = jnp.bfloat16


def from_root(array, axis, root):
    mine = lax.axis_index(axis) == root
    return lax.psum(jnp.where(mine, array, jnp.zeros_like(array)), axis)


def layer_norm(values):
    centred = values - jnp.mean(values, axis=-1, keepdims=True)
    spread = jnp.mean(centred * centred, axis=-1, keepdims=True)
    return centred * lax.rsqrt(spread + 1e-05)


def project_pair(inner_pair, mask_pair, weight):
    normed = layer_norm(inner_pair.astype(jnp.float32)).astype(jnp.bfloat16)
    linear = jnp.dot(normed, weight, preferred_element_type=jnp.float32)
    left_side = jax.nn.sigmoid(linear[..., :H]) * linear[..., H : 2 * H]
    right_side = jax.nn.sigmoid(linear[..., 2 * H : 3 * H]) * linear[..., 3 * H : 4 * H]
    operands = (jnp.stack((left_side, right_side)) * mask_pair[None, :, :, None]).astype(
        jnp.bfloat16
    )
    return (operands, jax.nn.sigmoid(linear[..., 4 * H :]))


def finish(mixed_part, gate_value, inner_pair, weight):
    normed = layer_norm(mixed_part).astype(jnp.bfloat16)
    update = jnp.dot(normed, weight, preferred_element_type=jnp.float32)
    return (inner_pair.astype(jnp.float32) + gate_value * update).astype(jnp.bfloat16)


def spread_body(pair_act, cotangent, residue_mask, front_weight, out_weight):
    local_rows = pair_act.shape[0]
    local_cols = pair_act.shape[1]
    row_index = lax.axis_index("row")
    col_index = lax.axis_index("col")
    block_rows = lax.axis_size("row") // lax.axis_size("col")
    owner_col = row_index // block_rows
    offset = row_index % block_rows * local_rows
    chain_mask = residue_mask.astype(jnp.float32)
    mask_rows = lax.dynamic_slice_in_dim(chain_mask, row_index * local_rows, local_rows)
    mask_cols = lax.dynamic_slice_in_dim(chain_mask, col_index * local_cols, local_cols)
    mask_pair = mask_rows[:, None] * mask_cols[None, :]

    def gather_rows(stacked):
        return lax.all_gather(stacked, "row", axis=1, tiled=True)

    def column_block(gathered):
        slab = lax.dynamic_slice_in_dim(gathered, offset, local_rows, 1)
        return from_root(slab, "col", owner_col)

    def gather_cols(values):
        return lax.all_gather(values, "col", axis=1, tiled=True)

    def sum_cols(partial_term):
        return lax.psum_scatter(
            partial_term.astype(jnp.bfloat16), "col", scatter_dimension=1, tiled=True
        ).astype(jnp.float32)

    (out_ops, out_gate), out_front_back = jax.vjp(
        lambda inner_pair: project_pair(inner_pair, mask_pair, front_weight[0]), pair_act
    )
    fetched = gather_rows(out_ops)
    out_mixed = sum_cols(
        jnp.einsum("ikc,jkc->ijc", out_ops[0], fetched[-1], preferred_element_type=jnp.float32)
    )
    pair_mid, out_finish_back = jax.vjp(
        lambda mixed_part, gate_value, inner_pair: finish(
            mixed_part, gate_value, inner_pair, out_weight[0]
        ),
        out_mixed,
        out_gate,
        pair_act,
    )
    (in_ops, in_gate), in_front_back = jax.vjp(
        lambda inner_pair: project_pair(inner_pair, mask_pair, front_weight[1]), pair_mid
    )
    in_fetched = gather_rows(in_ops)
    left_block = column_block(in_fetched[0])
    in_mixed = jnp.einsum(
        "kic,kjc->ijc", left_block, in_fetched[1], preferred_element_type=jnp.float32
    )
    unused_pair, in_finish_back = jax.vjp(
        lambda mixed_part, gate_value, inner_pair: finish(
            mixed_part, gate_value, inner_pair, out_weight[1]
        ),
        in_mixed,
        in_gate,
        pair_mid,
    )
    grad_mixed, grad_gate, grad_inner = in_finish_back(cotangent)
    signal = grad_mixed.astype(jnp.bfloat16)
    signal_rows = gather_rows(signal[None])[0]
    left_rows = gather_cols(in_ops[0])
    grad_right = jnp.einsum(
        "kic,ijc->kjc", left_rows, signal_rows, preferred_element_type=jnp.float32
    )
    grad_left = sum_cols(
        jnp.einsum("kjc,ijc->kic", in_ops[1], signal_rows, preferred_element_type=jnp.float32)
    )
    (grad_front,) = in_front_back(
        (jnp.stack((grad_left, grad_right)).astype(jnp.bfloat16), grad_gate)
    )
    grad_mid = (grad_inner.astype(jnp.float32) + grad_front.astype(jnp.float32)).astype(
        jnp.bfloat16
    )
    grad_mixed, grad_gate, grad_inner = out_finish_back(grad_mid)
    signal = grad_mixed.astype(jnp.bfloat16)
    signal_cols = gather_cols(signal)
    grad_left = jnp.einsum(
        "ijc,jkc->ikc", signal_cols, fetched[-1], preferred_element_type=jnp.float32
    )
    signal_block = column_block(gather_rows(signal[None])[0])
    grad_right = jnp.einsum(
        "ijc,ikc->jkc", signal_block, fetched[0], preferred_element_type=jnp.float32
    )
    (grad_front,) = out_front_back(
        (jnp.stack((grad_left, grad_right)).astype(jnp.bfloat16), grad_gate)
    )
    return (grad_inner.astype(jnp.float32) + grad_front.astype(jnp.float32)).astype(jnp.bfloat16)


def sigmoid(values):
    return 0.5 + 0.5 * jnp.tanh(0.5 * values)


def lane_mean(values):
    return jnp.mean(values, axis=-1, keepdims=True)


def normalize(values):
    centred = values - lane_mean(values)
    inverse = lax.rsqrt(lane_mean(centred * centred) + EPS)
    return centred * inverse, inverse


def normalize_back(grad, normed, inverse):
    return inverse * (grad - lane_mean(grad) - normed * lane_mean(grad * normed))


def rounded(values):
    return values.astype(BF16).astype(F32)


def matmul(values, weight):
    return jnp.dot(values.astype(BF16), weight, preferred_element_type=F32)


def matmul_t(values, weight):
    return lax.dot_general(
        values.astype(BF16), weight, (((1,), (1,)), ((), ())), preferred_element_type=F32
    )


def split(linear):
    return [linear[:, i * H : (i + 1) * H] for i in range(5)]


def front_back(linear, mask, grad_left, grad_right, grad_gate, weight, normed, inverse):
    gate_l, val_l, gate_r, val_r, gate = split(linear)
    gate_l, gate_r, gate = sigmoid(gate_l), sigmoid(gate_r), sigmoid(gate)
    grad_left, grad_right = grad_left * mask, grad_right * mask
    pieces = (
        grad_left * val_l * (gate_l * (1.0 - gate_l)),
        grad_left * gate_l,
        grad_right * val_r * (gate_r * (1.0 - gate_r)),
        grad_right * gate_r,
        grad_gate * (gate * (1.0 - gate)),
    )
    grad = jnp.concatenate([piece.astype(BF16) for piece in pieces], axis=1)
    return rounded(normalize_back(rounded(matmul_t(grad, weight)), normed, inverse))


def chain_length(mask_ref):
    return jnp.sum(mask_ref[...], axis=1, keepdims=True).astype(jnp.int32)


def pair_mask(chain, count, span, start, offset):
    major = lax.broadcasted_iota(jnp.int32, (count, span, H), 0) + start
    minor = lax.broadcasted_iota(jnp.int32, (count, span, H), 1) + offset
    inside = jnp.maximum(major, minor).reshape(count * span, H) < chain
    return jnp.where(inside, 1.0, 0.0)


def projection(weight, source, mask):
    normed, _ = normalize(source)
    gate_l, val_l, gate_r, val_r, gate = split(matmul(normed, weight))
    return (
        rounded(mask * (sigmoid(gate_l) * val_l)),
        rounded(mask * (sigmoid(gate_r) * val_r)),
        sigmoid(gate),
    )


def product(count, span, row_of, ref_a, ref_b, pitch, minor, width):
    totals = [None] * count
    for s in range(span):
        block = ref_b[pl.ds(s * pitch + minor, width), :]
        for p in range(count):
            term = jnp.broadcast_to(ref_a[pl.ds(row_of(p, s), 1), :], (width, H)) * block
            totals[p] = term if totals[p] is None else totals[p] + term
    return totals


def half_kernel(
    n, rows, cols, blocks, mask_ref, own_ref, weight_ref, left, right, gate, part, act, right_t,
):
    pitch = n + PAD
    row_index = lax.axis_index("row")
    chain = chain_length(mask_ref)
    for position, block in enumerate(blocks):
        place = (row_index ^ block) * rows
        for a in range(rows):
            where = pl.ds(pl.multiple_of((place + a) * cols, cols), cols)
            act[where, :] = own_ref[position, a].astype(F32)
    mask = pair_mask(chain, n, cols, 0, lax.axis_index("col") * cols)
    a, b, g = projection(weight_ref[0, :, : 5 * H], act[...], mask)
    left[...] = a
    right[...] = b
    gate[...] = g
    for i in range(n):
        right_t[pl.ds(i, cols, stride=pitch), :] = b[i * cols : (i + 1) * cols]
    for start in range(0, n, rows):
        totals = product(
            rows, cols, lambda p, s: (start + p) * cols + s, left, right_t, pitch, 0, n)
        part[pl.ds(start * n, rows * n), :] = jnp.concatenate(totals, axis=0)


def access(n, rows, cols, blocks, mask_ref):
    pitch = n + PAD
    row_index = lax.axis_index("row")
    col_index = lax.axis_index("col")
    chain = chain_length(mask_ref)
    me = row_index * rows
    mine = pl.multiple_of(col_index * cols, cols)
    theirs = pl.multiple_of((1 - col_index) * cols, cols)
    step = rows * n

    def mask_of(count, span, start, offset):
        return pair_mask(chain, count, span, start, offset)

    def get(ref, start=0, count=n):
        return jnp.concatenate(
            [ref[pl.ds((start + a) * pitch, n), :] for a in range(count)], axis=0
        )

    def put(ref, start, values, count=n):
        for a in range(count):
            ref[pl.ds((start + a) * pitch, n), :] = values[a * n : (a + 1) * n]

    def put_t(ref, values):
        for a in range(n):
            ref[pl.ds(a, n, stride=pitch), :] = values[a * n : (a + 1) * n]

    def get_t(ref):
        return [ref[pl.ds(me + a, n, stride=pitch), :] for a in range(rows)]

    def take(ref):
        return jnp.concatenate([get(ref, me, rows)] + get_t(ref), axis=0)

    def own(ref, base, stride):
        return jnp.concatenate(
            [ref[pl.ds(base + a * stride + mine, cols), :] for a in range(rows)], axis=0)

    def place(ref, own_ref, other_ref):
        for position, block in enumerate(blocks):
            start = (row_index ^ block) * rows
            for a in range(rows):
                base = (start + a) * pitch
                ref[pl.ds(base + mine, cols), :] = own_ref[position, a].astype(F32)
                ref[pl.ds(base + theirs, cols), :] = other_ref[position, a].astype(F32)

    return me, mine, theirs, step, pitch, mask_of, place, get, put, put_t, take, own


def forward_kernel(
    n, rows, cols, blocks, mask_ref, own_ref, other_ref, weight_ref,
    half_left, half_right, half_gate, part,
    left, right, gate0, mixed0, mid, left1, right1, left1_t, right1_t, gate1, mixed1,
    act, right_t,
):
    (me, mine, theirs, step, pitch, mask_of, place, get, put, put_t, take, own) = access(
        n, rows, cols, blocks, mask_ref)
    front_ref, out_ref = weight_ref.at[:, :, : 5 * H], weight_ref.at[:, :, 5 * H :]
    place(act, own_ref, other_ref)

    source = jnp.concatenate(
        [act[pl.ds(i * pitch + theirs, cols), :] for i in range(n)], axis=0)
    a, b, g = projection(front_ref[0], source, mask_of(n, cols, 0, theirs))
    for i in range(n):
        these = slice(i * cols, (i + 1) * cols)
        right_t[pl.ds(i, cols, stride=pitch), :] = b[these]
        for ref, done, new in (
            (left, half_left, a), (right, half_right, b), (gate0, half_gate, g)):
            ref[pl.ds(i * pitch + theirs, cols), :] = new[these]
            ref[pl.ds(i * pitch + mine, cols), :] = done[pl.ds(i * cols, cols), :]

    for start in range(0, n, rows):
        totals = product(
            rows, cols, lambda p, s: (start + p) * pitch + theirs + s, left, right_t, pitch, 0, n)
        rest = part[pl.ds(start * n, rows * n), :]
        put(mixed0, start, jnp.concatenate(totals, axis=0) + rest, rows)

    normed, _ = normalize(get(mixed0))
    value = rounded(get(act) + get(gate0) * matmul(normed, out_ref[0]))
    put(mid, 0, value)
    a, b, g = projection(front_ref[1], value, mask_of(n, n, 0, 0))
    put(left1, 0, a)
    put(right1, 0, b)
    put_t(left1_t, a)
    put_t(right1_t, b)
    put(gate1, 0, g)

    for start in range(0, n, rows):
        totals = product(rows, n, lambda p, s: s * pitch + start + p, left1, right1, pitch, 0, n)
        put(mixed1, start, jnp.concatenate(totals, axis=0), rows)


def backward_kernel(
    n, rows, cols, blocks, mask_ref, act_ref, own_ref, other_ref, weight_ref,
    left, right, gate0, mixed0, mid, left1, right1, left1_t, right1_t, gate1, mixed1,
    grad_ref, cot, sig, sig_t, grow, s_gate, s_sig, dl, dr,
):
    (me, mine, theirs, step, pitch, mask_of, place, get, put, put_t, take, own) = access(
        n, rows, cols, blocks, mask_ref)
    front_ref, out_ref = weight_ref.at[:, :, : 5 * H], weight_ref.at[:, :, 5 * H :]
    place(cot, own_ref, other_ref)

    normed, inverse = normalize(get(mixed1))
    grad = rounded(matmul_t(get(cot) * get(gate1), out_ref[1]))
    value = rounded(normalize_back(grad, normed, inverse))
    put(sig, 0, value)
    put_t(sig_t, value)

    def row_of(p, s):
        return (me + p) * pitch + s

    dl[pl.ds(0, step), :] = jnp.concatenate(
        product(rows, n, row_of, right1, sig_t, pitch, 0, n), axis=0)
    dl[pl.ds(step, step), :] = jnp.concatenate(
        product(rows, n, row_of, sig, right1_t, pitch, 0, n), axis=0)
    dr[pl.ds(0, step), :] = jnp.concatenate(
        product(rows, n, row_of, left1, sig, pitch, 0, n), axis=0)
    dr[pl.ds(step, step), :] = jnp.concatenate(
        product(rows, n, lambda p, s: s * pitch + me + p, sig, left1_t, pitch, 0, n), axis=0)

    mask_rows = mask_of(rows, n, me, 0)
    cot_s = take(cot)
    mixed, _ = normalize(take(mixed1))
    normed, inverse = normalize(take(mid))
    grad_gate = cot_s * matmul(mixed, out_ref[1])
    grad = front_back(
        matmul(normed, front_ref[1]), jnp.concatenate([mask_rows, mask_rows], axis=0),
        rounded(dl[...]), rounded(dr[...]), grad_gate, front_ref[1], normed, inverse)
    grad_mid = rounded(cot_s + grad)
    mixed, inverse = normalize(take(mixed0))
    grow[...] = grad_mid[:step]
    s_gate[...] = grad_mid[:step] * matmul(mixed[:step], out_ref[0])
    grad = rounded(matmul_t(grad_mid * take(gate0), out_ref[0]))
    s_sig[...] = rounded(normalize_back(grad, mixed, inverse))

    grad_left = product(rows, n, lambda p, s: p * n + s, s_sig, right, pitch, mine, cols)
    grad_right = product(rows, n, lambda p, s: step + p * n + s, s_sig, left, pitch, mine, cols)

    normed, inverse = normalize(act_ref[0].astype(F32).reshape(rows * cols, H))
    grad = front_back(
        matmul(normed, front_ref[0]), mask_of(rows, cols, me, mine),
        rounded(jnp.concatenate(grad_left, axis=0)), rounded(jnp.concatenate(grad_right, axis=0)),
        own(s_gate, 0, n), front_ref[0], normed, inverse)
    grad_ref[...] = (own(grow, 0, n) + grad).astype(BF16).reshape(rows, cols, H)


def whole_body(pair_act, cotangent, residue_mask, front_weight, out_weight):
    rows, cols, width = pair_act.shape
    n = residue_mask.shape[0]
    mask = residue_mask.reshape(1, n).astype(F32)
    row_count = lax.axis_size("row")
    bits = row_count.bit_length() - 1
    gathered = jnp.stack((pair_act, cotangent))[:, None]
    weights = jnp.concatenate((front_weight, out_weight), axis=2)
    blocks = [0]
    steps = [1 << b for b in range(1, bits)] + [1]

    def swap(array, step):
        return lax.ppermute(array, "row", [(i, i ^ step) for i in range(row_count)])

    for step in steps[:-1]:
        gathered = jnp.concatenate((gathered, swap(gathered, step)), axis=1)
        if step == steps[0]:
            gathered, mask, weights = lax.optimization_barrier((gathered, mask, weights))
        blocks = blocks + [b ^ step for b in blocks]
    act, cot = gathered[0], gathered[1]
    act = jnp.concatenate((act, swap(act, steps[-1])))
    cot_late = swap(cot, steps[-1])
    blocks = blocks + [b ^ steps[-1] for b in blocks]
    act_other = lax.ppermute(act, "col", [(0, 1), (1, 0)])
    full = pltpu.VMEM((n * (n + PAD), H), F32)
    some = pltpu.VMEM((rows * n, H), F32)
    twice = pltpu.VMEM((2 * rows * n, H), F32)
    vmem = pl.BlockSpec(memory_space=pltpu.VMEM)
    part_of = jax.ShapeDtypeStruct((n * cols, H), F32)
    halves = pl.pallas_call(
        functools.partial(half_kernel, n, rows, cols, blocks),
        out_shape=[part_of] * 3 + [jax.ShapeDtypeStruct((n * n, H), F32)],
        in_specs=[vmem] * 3,
        out_specs=[vmem] * 4,
        scratch_shapes=[pltpu.VMEM((n * cols, H), F32), pltpu.VMEM((cols * (n + PAD), H), F32)],
        compiler_params=pltpu.CompilerParams(vmem_limit_bytes=VMEM_BUDGET // 4),
    )(mask, act, weights)
    cot_late, *halves = lax.optimization_barrier((cot_late, *halves))
    cot = jnp.concatenate((cot, cot_late))
    cot_other = lax.ppermute(cot, "col", [(0, 1), (1, 0)])
    kept = pl.pallas_call(
        functools.partial(forward_kernel, n, rows, cols, blocks),
        out_shape=[jax.ShapeDtypeStruct((n * (n + PAD), H), F32)] * 11,
        in_specs=[vmem] * 8,
        out_specs=[vmem] * 11,
        scratch_shapes=[full, full],
        compiler_params=pltpu.CompilerParams(vmem_limit_bytes=VMEM_BUDGET // 2),
    )(mask, act, act_other, weights, *halves)
    return pl.pallas_call(
        functools.partial(backward_kernel, n, rows, cols, blocks),
        out_shape=jax.ShapeDtypeStruct(pair_act.shape, BF16),
        in_specs=[vmem] * 16,
        out_specs=vmem,
        scratch_shapes=[full] * 3 + [some, some, twice, twice, twice],
        compiler_params=pltpu.CompilerParams(vmem_limit_bytes=VMEM_BUDGET // 2),
    )(mask, act, cot, cot_other, weights, *kept)


def body(pair_act, cotangent, residue_mask, front_weight, out_weight):
    n = residue_mask.shape[0]
    row_count = lax.axis_size("row")
    fits = 20 * n * (n + PAD) * H * 4 <= VMEM_BUDGET
    doubling = row_count & (row_count - 1) == 0 and lax.axis_size("col") == 2
    run = whole_body if fits and doubling else spread_body
    return run(pair_act, cotangent, residue_mask, front_weight, out_weight)


def solution(mesh):
    placed = (P(("grp", "row"), "col", None), P(("grp", "row"), "col", None), P("grp"), P(), P())
    return jax.shard_map(
        body, mesh=mesh, in_specs=placed, out_specs=P(("grp", "row"), "col", None), check_vma=False
    )
```

```python
import functools

import jax
import jax.numpy as jnp
from jax import lax
from jax.experimental import pallas as pl
from jax.experimental.pallas import tpu as pltpu
from jax.sharding import PartitionSpec as P

H = 128
EPS = 1e-05
PAD = 4
VMEM_BUDGET = 40 << 20
F32 = jnp.float32
BF16 = jnp.bfloat16


def from_root(array, axis, root):
    mine = lax.axis_index(axis) == root
    return lax.psum(jnp.where(mine, array, jnp.zeros_like(array)), axis)


def layer_norm(values):
    centred = values - jnp.mean(values, axis=-1, keepdims=True)
    spread = jnp.mean(centred * centred, axis=-1, keepdims=True)
    return centred * lax.rsqrt(spread + 1e-05)


def project_pair(inner_pair, mask_pair, weight):
    normed = layer_norm(inner_pair.astype(jnp.float32)).astype(jnp.bfloat16)
    linear = jnp.dot(normed, weight, preferred_element_type=jnp.float32)
    left_side = jax.nn.sigmoid(linear[..., :H]) * linear[..., H : 2 * H]
    right_side = jax.nn.sigmoid(linear[..., 2 * H : 3 * H]) * linear[..., 3 * H : 4 * H]
    operands = (jnp.stack((left_side, right_side)) * mask_pair[None, :, :, None]).astype(
        jnp.bfloat16
    )
    return (operands, jax.nn.sigmoid(linear[..., 4 * H :]))


def finish(mixed_part, gate_value, inner_pair, weight):
    normed = layer_norm(mixed_part).astype(jnp.bfloat16)
    update = jnp.dot(normed, weight, preferred_element_type=jnp.float32)
    return (inner_pair.astype(jnp.float32) + gate_value * update).astype(jnp.bfloat16)


def spread_body(pair_act, cotangent, residue_mask, front_weight, out_weight):
    local_rows = pair_act.shape[0]
    local_cols = pair_act.shape[1]
    row_index = lax.axis_index("row")
    col_index = lax.axis_index("col")
    block_rows = lax.axis_size("row") // lax.axis_size("col")
    owner_col = row_index // block_rows
    offset = row_index % block_rows * local_rows
    chain_mask = residue_mask.astype(jnp.float32)
    mask_rows = lax.dynamic_slice_in_dim(chain_mask, row_index * local_rows, local_rows)
    mask_cols = lax.dynamic_slice_in_dim(chain_mask, col_index * local_cols, local_cols)
    mask_pair = mask_rows[:, None] * mask_cols[None, :]

    def gather_rows(stacked):
        return lax.all_gather(stacked, "row", axis=1, tiled=True)

    def column_block(gathered):
        slab = lax.dynamic_slice_in_dim(gathered, offset, local_rows, 1)
        return from_root(slab, "col", owner_col)

    def gather_cols(values):
        return lax.all_gather(values, "col", axis=1, tiled=True)

    def sum_cols(partial_term):
        return lax.psum_scatter(
            partial_term.astype(jnp.bfloat16), "col", scatter_dimension=1, tiled=True
        ).astype(jnp.float32)

    (out_ops, out_gate), out_front_back = jax.vjp(
        lambda inner_pair: project_pair(inner_pair, mask_pair, front_weight[0]), pair_act
    )
    fetched = gather_rows(out_ops)
    out_mixed = sum_cols(
        jnp.einsum("ikc,jkc->ijc", out_ops[0], fetched[-1], preferred_element_type=jnp.float32)
    )
    pair_mid, out_finish_back = jax.vjp(
        lambda mixed_part, gate_value, inner_pair: finish(
            mixed_part, gate_value, inner_pair, out_weight[0]
        ),
        out_mixed,
        out_gate,
        pair_act,
    )
    (in_ops, in_gate), in_front_back = jax.vjp(
        lambda inner_pair: project_pair(inner_pair, mask_pair, front_weight[1]), pair_mid
    )
    in_fetched = gather_rows(in_ops)
    left_block = column_block(in_fetched[0])
    in_mixed = jnp.einsum(
        "kic,kjc->ijc", left_block, in_fetched[1], preferred_element_type=jnp.float32
    )
    _, in_finish_back = jax.vjp(
        lambda mixed_part, gate_value, inner_pair: finish(
            mixed_part, gate_value, inner_pair, out_weight[1]
        ),
        in_mixed,
        in_gate,
        pair_mid,
    )
    grad_mixed, grad_gate, grad_inner = in_finish_back(cotangent)
    signal = grad_mixed.astype(jnp.bfloat16)
    signal_rows = gather_rows(signal[None])[0]
    left_rows = gather_cols(in_ops[0])
    grad_right = jnp.einsum(
        "kic,ijc->kjc", left_rows, signal_rows, preferred_element_type=jnp.float32
    )
    grad_left = sum_cols(
        jnp.einsum("kjc,ijc->kic", in_ops[1], signal_rows, preferred_element_type=jnp.float32)
    )
    (grad_front,) = in_front_back(
        (jnp.stack((grad_left, grad_right)).astype(jnp.bfloat16), grad_gate)
    )
    grad_mid = (grad_inner.astype(jnp.float32) + grad_front.astype(jnp.float32)).astype(
        jnp.bfloat16
    )
    grad_mixed, grad_gate, grad_inner = out_finish_back(grad_mid)
    signal = grad_mixed.astype(jnp.bfloat16)
    signal_cols = gather_cols(signal)
    grad_left = jnp.einsum(
        "ijc,jkc->ikc", signal_cols, fetched[-1], preferred_element_type=jnp.float32
    )
    signal_block = column_block(gather_rows(signal[None])[0])
    grad_right = jnp.einsum(
        "ijc,ikc->jkc", signal_block, fetched[0], preferred_element_type=jnp.float32
    )
    (grad_front,) = out_front_back(
        (jnp.stack((grad_left, grad_right)).astype(jnp.bfloat16), grad_gate)
    )
    return (grad_inner.astype(jnp.float32) + grad_front.astype(jnp.float32)).astype(jnp.bfloat16)


def sigmoid(values):
    return 0.5 + 0.5 * jnp.tanh(0.5 * values)


def lane_mean(values):
    return jnp.mean(values, axis=-1, keepdims=True)


def normalize(values):
    centred = values - lane_mean(values)
    inverse = lax.rsqrt(lane_mean(centred * centred) + EPS)
    return centred * inverse, inverse


def normalize_back(grad, normed, inverse):
    return inverse * (grad - lane_mean(grad) - normed * lane_mean(grad * normed))


def rounded(values):
    return values.astype(BF16).astype(F32)


def matmul(values, weight):
    return jnp.dot(values.astype(BF16), weight, preferred_element_type=F32)


def matmul_t(values, weight):
    return lax.dot_general(
        values.astype(BF16), weight, (((1,), (1,)), ((), ())), preferred_element_type=F32
    )


def split(linear):
    return [linear[:, i * H : (i + 1) * H] for i in range(5)]


def front_back(linear, mask, grad_left, grad_right, grad_gate, weight, normed, inverse):
    gate_l, val_l, gate_r, val_r, gate = split(linear)
    gate_l, gate_r, gate = sigmoid(gate_l), sigmoid(gate_r), sigmoid(gate)
    grad_left, grad_right = grad_left * mask, grad_right * mask
    pieces = (
        grad_left * val_l * (gate_l * (1.0 - gate_l)),
        grad_left * gate_l,
        grad_right * val_r * (gate_r * (1.0 - gate_r)),
        grad_right * gate_r,
        grad_gate * (gate * (1.0 - gate)),
    )
    grad = jnp.concatenate([piece.astype(BF16) for piece in pieces], axis=1)
    return rounded(normalize_back(rounded(matmul_t(grad, weight)), normed, inverse))


def chain_length(mask_ref):
    return jnp.sum(mask_ref[...], axis=1, keepdims=True).astype(jnp.int32)


def pair_mask(chain, count, span, start, offset):
    major = lax.broadcasted_iota(jnp.int32, (count, span, H), 0) + start
    minor = lax.broadcasted_iota(jnp.int32, (count, span, H), 1) + offset
    inside = jnp.maximum(major, minor).reshape(count * span, H) < chain
    return jnp.where(inside, 1.0, 0.0)


def projection(weight, source, mask):
    normed, _ = normalize(source)
    gate_l, val_l, gate_r, val_r, gate = split(matmul(normed, weight))
    return (
        rounded(mask * (sigmoid(gate_l) * val_l)),
        rounded(mask * (sigmoid(gate_r) * val_r)),
        sigmoid(gate),
    )


def product(count, span, row_of, ref_a, ref_b, pitch, minor, width):
    totals = [None] * count
    for s in range(span):
        block = ref_b[pl.ds(s * pitch + minor, width), :]
        for p in range(count):
            term = jnp.broadcast_to(ref_a[pl.ds(row_of(p, s), 1), :], (width, H)) * block
            totals[p] = term if totals[p] is None else totals[p] + term
    return totals


def half_kernel(
    n, rows, cols, blocks, mask_ref, own_ref, weight_ref, left, right, gate, part, act, right_t,
):
    pitch = n + PAD
    row_index = lax.axis_index("row")
    chain = chain_length(mask_ref)
    for position, block in enumerate(blocks):
        place = (row_index ^ block) * rows
        for a in range(rows):
            where = pl.ds(pl.multiple_of((place + a) * cols, cols), cols)
            act[where, :] = own_ref[position, a].astype(F32)
    mask = pair_mask(chain, n, cols, 0, lax.axis_index("col") * cols)
    a, b, g = projection(weight_ref[0, :, : 5 * H], act[...], mask)
    left[...] = a
    right[...] = b
    gate[...] = g
    for i in range(n):
        right_t[pl.ds(i, cols, stride=pitch), :] = b[i * cols : (i + 1) * cols]
    for start in range(0, n, rows):
        totals = product(
            rows, cols, lambda p, s: (start + p) * cols + s, left, right_t, pitch, 0, n)
        part[pl.ds(start * n, rows * n), :] = jnp.concatenate(totals, axis=0)


def access(n, rows, cols, blocks, mask_ref):
    pitch = n + PAD
    row_index = lax.axis_index("row")
    col_index = lax.axis_index("col")
    chain = chain_length(mask_ref)
    me = row_index * rows
    mine = pl.multiple_of(col_index * cols, cols)
    theirs = pl.multiple_of((1 - col_index) * cols, cols)
    step = rows * n

    def mask_of(count, span, start, offset):
        return pair_mask(chain, count, span, start, offset)

    def get(ref, start=0, count=n):
        return jnp.concatenate(
            [ref[pl.ds((start + a) * pitch, n), :] for a in range(count)], axis=0
        )

    def put(ref, start, values, count=n):
        for a in range(count):
            ref[pl.ds((start + a) * pitch, n), :] = values[a * n : (a + 1) * n]

    def put_t(ref, values):
        for a in range(n):
            ref[pl.ds(a, n, stride=pitch), :] = values[a * n : (a + 1) * n]

    def get_t(ref):
        return [ref[pl.ds(me + a, n, stride=pitch), :] for a in range(rows)]

    def take(ref):
        return jnp.concatenate([get(ref, me, rows)] + get_t(ref), axis=0)

    def own(ref, base, stride):
        return jnp.concatenate(
            [ref[pl.ds(base + a * stride + mine, cols), :] for a in range(rows)], axis=0)

    def place(ref, own_ref, other_ref):
        for position, block in enumerate(blocks):
            start = (row_index ^ block) * rows
            for a in range(rows):
                base = (start + a) * pitch
                ref[pl.ds(base + mine, cols), :] = own_ref[position, a].astype(F32)
                ref[pl.ds(base + theirs, cols), :] = other_ref[position, a].astype(F32)

    return me, mine, theirs, step, pitch, mask_of, place, get, put, put_t, take, own


def outgoing_kernel(
    n, rows, cols, blocks, mask_ref, own_ref, other_ref, weight_ref,
    half_left, half_right, half_gate, part, act, left, right, gate0, mixed0, right_t,
):
    (_, mine, theirs, _, pitch, mask_of, place, _, put, _, _, _) = access(
        n, rows, cols, blocks, mask_ref)
    front_ref = weight_ref.at[:, :, : 5 * H]
    place(act, own_ref, other_ref)

    source = jnp.concatenate(
        [act[pl.ds(i * pitch + theirs, cols), :] for i in range(n)], axis=0)
    a, b, g = projection(front_ref[0], source, mask_of(n, cols, 0, theirs))
    for i in range(n):
        these = slice(i * cols, (i + 1) * cols)
        right_t[pl.ds(i, cols, stride=pitch), :] = b[these]
        for ref, done, new in (
            (left, half_left, a), (right, half_right, b), (gate0, half_gate, g)):
            ref[pl.ds(i * pitch + theirs, cols), :] = new[these]
            ref[pl.ds(i * pitch + mine, cols), :] = done[pl.ds(i * cols, cols), :]

    for start in range(0, n, rows):
        totals = product(
            rows, cols, lambda p, s: (start + p) * pitch + theirs + s, left, right_t, pitch, 0, n)
        rest = part[pl.ds(start * n, rows * n), :]
        put(mixed0, start, jnp.concatenate(totals, axis=0) + rest, rows)


def incoming_kernel(
    n, rows, cols, blocks, mask_ref, weight_ref, act, gate0, mixed0,
    mid, left1, right1, left1_t, right1_t, gate1, mixed1,
):
    (_, _, _, _, pitch, mask_of, _, get, put, put_t, _, _) = access(
        n, rows, cols, blocks, mask_ref)
    front_ref, out_ref = weight_ref.at[:, :, : 5 * H], weight_ref.at[:, :, 5 * H :]
    normed, _ = normalize(get(mixed0))
    value = rounded(get(act) + get(gate0) * matmul(normed, out_ref[0]))
    put(mid, 0, value)
    a, b, g = projection(front_ref[1], value, mask_of(n, n, 0, 0))
    put(left1, 0, a)
    put(right1, 0, b)
    put_t(left1_t, a)
    put_t(right1_t, b)
    put(gate1, 0, g)

    for start in range(0, n, rows):
        totals = product(rows, n, lambda p, s: s * pitch + start + p, left1, right1, pitch, 0, n)
        put(mixed1, start, jnp.concatenate(totals, axis=0), rows)


def backward_kernel(
    n, rows, cols, blocks, mask_ref, act_ref, own_ref, other_ref, weight_ref,
    left, right, gate0, mixed0, mid, left1, right1, left1_t, right1_t, gate1, mixed1,
    grad_ref, cot, sig, sig_t, grow, s_gate, s_sig, dl, dr,
):
    (me, mine, _, step, pitch, mask_of, place, get, put, put_t, take, own) = access(
        n, rows, cols, blocks, mask_ref)
    front_ref, out_ref = weight_ref.at[:, :, : 5 * H], weight_ref.at[:, :, 5 * H :]
    place(cot, own_ref, other_ref)

    normed, inverse = normalize(get(mixed1))
    grad = rounded(matmul_t(get(cot) * get(gate1), out_ref[1]))
    value = rounded(normalize_back(grad, normed, inverse))
    put(sig, 0, value)
    put_t(sig_t, value)

    def row_of(p, s):
        return (me + p) * pitch + s

    dl[pl.ds(0, step), :] = jnp.concatenate(
        product(rows, n, row_of, right1, sig_t, pitch, 0, n), axis=0)
    dl[pl.ds(step, step), :] = jnp.concatenate(
        product(rows, n, row_of, sig, right1_t, pitch, 0, n), axis=0)
    dr[pl.ds(0, step), :] = jnp.concatenate(
        product(rows, n, row_of, left1, sig, pitch, 0, n), axis=0)
    dr[pl.ds(step, step), :] = jnp.concatenate(
        product(rows, n, lambda p, s: s * pitch + me + p, sig, left1_t, pitch, 0, n), axis=0)

    mask_rows = mask_of(rows, n, me, 0)
    cot_s = take(cot)
    mixed, _ = normalize(take(mixed1))
    normed, inverse = normalize(take(mid))
    grad_gate = cot_s * matmul(mixed, out_ref[1])
    grad = front_back(
        matmul(normed, front_ref[1]), jnp.concatenate([mask_rows, mask_rows], axis=0),
        rounded(dl[...]), rounded(dr[...]), grad_gate, front_ref[1], normed, inverse)
    grad_mid = rounded(cot_s + grad)
    mixed, inverse = normalize(take(mixed0))
    grow[...] = grad_mid[:step]
    s_gate[...] = grad_mid[:step] * matmul(mixed[:step], out_ref[0])
    grad = rounded(matmul_t(grad_mid * take(gate0), out_ref[0]))
    s_sig[...] = rounded(normalize_back(grad, mixed, inverse))

    grad_left = product(rows, n, lambda p, s: p * n + s, s_sig, right, pitch, mine, cols)
    grad_right = product(rows, n, lambda p, s: step + p * n + s, s_sig, left, pitch, mine, cols)

    normed, inverse = normalize(act_ref[0].astype(F32).reshape(rows * cols, H))
    grad = front_back(
        matmul(normed, front_ref[0]), mask_of(rows, cols, me, mine),
        rounded(jnp.concatenate(grad_left, axis=0)), rounded(jnp.concatenate(grad_right, axis=0)),
        own(s_gate, 0, n), front_ref[0], normed, inverse)
    grad_ref[...] = (own(grow, 0, n) + grad).astype(BF16).reshape(rows, cols, H)


def whole_body(pair_act, cotangent, residue_mask, front_weight, out_weight):
    rows, cols, _ = pair_act.shape
    n = residue_mask.shape[0]
    row_count = lax.axis_size("row")
    bits = row_count.bit_length() - 1
    weights = jnp.concatenate((front_weight, out_weight), axis=2)
    mask = residue_mask.reshape(1, n).astype(F32)
    blocks = [0]
    steps = [1 << b for b in range(1, bits)] + [1]

    def swap(array, step):
        return lax.ppermute(array, "row", [(i, i ^ step) for i in range(row_count)])

    sent = (pair_act[None], cotangent[None])
    held = lax.optimization_barrier(jnp.stack(sent))
    held = (held[0], held[1])
    for step in steps:
        act_late = swap(sent[0], step)
        cot_late = swap(sent[1], step)
        act = jnp.concatenate((held[0], act_late))
        if step != steps[-1]:
            cot = jnp.concatenate((held[1], cot_late))
            sent = held = (act, cot)
        blocks = blocks + [b ^ step for b in blocks]
    act_other = lax.ppermute(act, "col", [(0, 1), (1, 0)])
    full = pltpu.VMEM((n * (n + PAD), H), F32)
    some = pltpu.VMEM((rows * n, H), F32)
    twice = pltpu.VMEM((2 * rows * n, H), F32)
    vmem = pl.BlockSpec(memory_space=pltpu.VMEM)
    part_of = jax.ShapeDtypeStruct((n * cols, H), F32)
    halves = pl.pallas_call(
        functools.partial(half_kernel, n, rows, cols, blocks),
        out_shape=[part_of] * 3 + [jax.ShapeDtypeStruct((n * n, H), F32)],
        in_specs=[vmem] * 3,
        out_specs=[vmem] * 4,
        scratch_shapes=[pltpu.VMEM((n * cols, H), F32), pltpu.VMEM((cols * (n + PAD), H), F32)],
        compiler_params=pltpu.CompilerParams(vmem_limit_bytes=VMEM_BUDGET // 4),
    )(mask, act, weights)
    pairs_of = jax.ShapeDtypeStruct((n * (n + PAD), H), F32)
    act_full, left, right, gate0, mixed0 = pl.pallas_call(
        functools.partial(outgoing_kernel, n, rows, cols, blocks),
        out_shape=[pairs_of] * 5,
        in_specs=[vmem] * 8,
        out_specs=[vmem] * 5,
        scratch_shapes=[full],
        compiler_params=pltpu.CompilerParams(vmem_limit_bytes=VMEM_BUDGET // 4),
    )(mask, act, act_other, weights, *halves)
    cot_late, mixed0 = lax.optimization_barrier((cot_late, mixed0))
    cot = jnp.concatenate((held[1], cot_late))
    cot_other = lax.ppermute(cot, "col", [(0, 1), (1, 0)])
    incoming = pl.pallas_call(
        functools.partial(incoming_kernel, n, rows, cols, blocks),
        out_shape=[pairs_of] * 7,
        in_specs=[vmem] * 5,
        out_specs=[vmem] * 7,
        compiler_params=pltpu.CompilerParams(vmem_limit_bytes=VMEM_BUDGET // 4),
    )(mask, weights, act_full, gate0, mixed0)
    kept = (left, right, gate0, mixed0, *incoming)
    return pl.pallas_call(
        functools.partial(backward_kernel, n, rows, cols, blocks),
        out_shape=jax.ShapeDtypeStruct(pair_act.shape, BF16),
        in_specs=[vmem] * 16,
        out_specs=vmem,
        scratch_shapes=[full] * 3 + [some, some, twice, twice, twice],
        compiler_params=pltpu.CompilerParams(vmem_limit_bytes=VMEM_BUDGET // 2),
    )(mask, act, cot, cot_other, weights, *kept)


def body(pair_act, cotangent, residue_mask, front_weight, out_weight):
    n = residue_mask.shape[0]
    row_count = lax.axis_size("row")
    fits = 20 * n * (n + PAD) * H * 4 <= VMEM_BUDGET
    doubling = row_count >= 4 and row_count & (row_count - 1) == 0 and lax.axis_size("col") == 2
    run = whole_body if fits and doubling else spread_body
    return run(pair_act, cotangent, residue_mask, front_weight, out_weight)


def solution(mesh):
    placed = (P(("grp", "row"), "col", None), P(("grp", "row"), "col", None), P("grp"), P(), P())
    return jax.shard_map(
        body, mesh=mesh, in_specs=placed, out_specs=P(("grp", "row"), "col", None), check_vma=False
    )
```

```python
import functools

import jax
import jax.numpy as jnp
from jax import lax
from jax.experimental import pallas as pl
from jax.experimental.pallas import tpu as pltpu
from jax.sharding import PartitionSpec as P

H = 128
EPS = 1e-05
PAD = 4
VMEM_BUDGET = 40 << 20
F32 = jnp.float32
BF16 = jnp.bfloat16


def from_root(array, axis, root):
    mine = lax.axis_index(axis) == root
    return lax.psum(jnp.where(mine, array, jnp.zeros_like(array)), axis)


def layer_norm(values):
    centred = values - jnp.mean(values, axis=-1, keepdims=True)
    spread = jnp.mean(centred * centred, axis=-1, keepdims=True)
    return centred * lax.rsqrt(spread + 1e-05)


def project_pair(inner_pair, mask_pair, weight):
    normed = layer_norm(inner_pair.astype(jnp.float32)).astype(jnp.bfloat16)
    linear = jnp.dot(normed, weight, preferred_element_type=jnp.float32)
    left_side = jax.nn.sigmoid(linear[..., :H]) * linear[..., H : 2 * H]
    right_side = jax.nn.sigmoid(linear[..., 2 * H : 3 * H]) * linear[..., 3 * H : 4 * H]
    operands = (jnp.stack((left_side, right_side)) * mask_pair[None, :, :, None]).astype(
        jnp.bfloat16
    )
    return (operands, jax.nn.sigmoid(linear[..., 4 * H :]))


def finish(mixed_part, gate_value, inner_pair, weight):
    normed = layer_norm(mixed_part).astype(jnp.bfloat16)
    update = jnp.dot(normed, weight, preferred_element_type=jnp.float32)
    return (inner_pair.astype(jnp.float32) + gate_value * update).astype(jnp.bfloat16)


def spread_body(pair_act, cotangent, residue_mask, front_weight, out_weight):
    local_rows = pair_act.shape[0]
    local_cols = pair_act.shape[1]
    row_index = lax.axis_index("row")
    col_index = lax.axis_index("col")
    block_rows = lax.axis_size("row") // lax.axis_size("col")
    owner_col = row_index // block_rows
    offset = row_index % block_rows * local_rows
    chain_mask = residue_mask.astype(jnp.float32)
    mask_rows = lax.dynamic_slice_in_dim(chain_mask, row_index * local_rows, local_rows)
    mask_cols = lax.dynamic_slice_in_dim(chain_mask, col_index * local_cols, local_cols)
    mask_pair = mask_rows[:, None] * mask_cols[None, :]

    def gather_rows(stacked):
        return lax.all_gather(stacked, "row", axis=1, tiled=True)

    def column_block(gathered):
        slab = lax.dynamic_slice_in_dim(gathered, offset, local_rows, 1)
        return from_root(slab, "col", owner_col)

    def gather_cols(values):
        return lax.all_gather(values, "col", axis=1, tiled=True)

    def sum_cols(partial_term):
        return lax.psum_scatter(
            partial_term.astype(jnp.bfloat16), "col", scatter_dimension=1, tiled=True
        ).astype(jnp.float32)

    (out_ops, out_gate), out_front_back = jax.vjp(
        lambda inner_pair: project_pair(inner_pair, mask_pair, front_weight[0]), pair_act
    )
    fetched = gather_rows(out_ops)
    out_mixed = sum_cols(
        jnp.einsum("ikc,jkc->ijc", out_ops[0], fetched[-1], preferred_element_type=jnp.float32)
    )
    pair_mid, out_finish_back = jax.vjp(
        lambda mixed_part, gate_value, inner_pair: finish(
            mixed_part, gate_value, inner_pair, out_weight[0]
        ),
        out_mixed,
        out_gate,
        pair_act,
    )
    (in_ops, in_gate), in_front_back = jax.vjp(
        lambda inner_pair: project_pair(inner_pair, mask_pair, front_weight[1]), pair_mid
    )
    in_fetched = gather_rows(in_ops)
    left_block = column_block(in_fetched[0])
    in_mixed = jnp.einsum(
        "kic,kjc->ijc", left_block, in_fetched[1], preferred_element_type=jnp.float32
    )
    _, in_finish_back = jax.vjp(
        lambda mixed_part, gate_value, inner_pair: finish(
            mixed_part, gate_value, inner_pair, out_weight[1]
        ),
        in_mixed,
        in_gate,
        pair_mid,
    )
    grad_mixed, grad_gate, grad_inner = in_finish_back(cotangent)
    signal = grad_mixed.astype(jnp.bfloat16)
    signal_rows = gather_rows(signal[None])[0]
    left_rows = gather_cols(in_ops[0])
    grad_right = jnp.einsum(
        "kic,ijc->kjc", left_rows, signal_rows, preferred_element_type=jnp.float32
    )
    grad_left = sum_cols(
        jnp.einsum("kjc,ijc->kic", in_ops[1], signal_rows, preferred_element_type=jnp.float32)
    )
    (grad_front,) = in_front_back(
        (jnp.stack((grad_left, grad_right)).astype(jnp.bfloat16), grad_gate)
    )
    grad_mid = (grad_inner.astype(jnp.float32) + grad_front.astype(jnp.float32)).astype(
        jnp.bfloat16
    )
    grad_mixed, grad_gate, grad_inner = out_finish_back(grad_mid)
    signal = grad_mixed.astype(jnp.bfloat16)
    signal_cols = gather_cols(signal)
    grad_left = jnp.einsum(
        "ijc,jkc->ikc", signal_cols, fetched[-1], preferred_element_type=jnp.float32
    )
    signal_block = column_block(gather_rows(signal[None])[0])
    grad_right = jnp.einsum(
        "ijc,ikc->jkc", signal_block, fetched[0], preferred_element_type=jnp.float32
    )
    (grad_front,) = out_front_back(
        (jnp.stack((grad_left, grad_right)).astype(jnp.bfloat16), grad_gate)
    )
    return (grad_inner.astype(jnp.float32) + grad_front.astype(jnp.float32)).astype(jnp.bfloat16)


def sigmoid(values):
    return 0.5 + 0.5 * jnp.tanh(0.5 * values)


def lane_mean(values):
    return jnp.mean(values, axis=-1, keepdims=True)


def normalize(values):
    centred = values - lane_mean(values)
    inverse = lax.rsqrt(lane_mean(centred * centred) + EPS)
    return centred * inverse, inverse


def normalize_back(grad, normed, inverse):
    return inverse * (grad - lane_mean(grad) - normed * lane_mean(grad * normed))


def rounded(values):
    return values.astype(BF16).astype(F32)


def matmul(values, weight):
    return jnp.dot(values.astype(BF16), weight, preferred_element_type=F32)


def matmul_t(values, weight):
    return lax.dot_general(
        values.astype(BF16), weight, (((1,), (1,)), ((), ())), preferred_element_type=F32
    )


def split(linear):
    return [linear[:, i * H : (i + 1) * H] for i in range(5)]


def front_back(linear, mask, grad_left, grad_right, grad_gate, weight, normed, inverse):
    gate_l, val_l, gate_r, val_r, gate = split(linear)
    gate_l, gate_r, gate = sigmoid(gate_l), sigmoid(gate_r), sigmoid(gate)
    grad_left, grad_right = grad_left * mask, grad_right * mask
    pieces = (
        grad_left * val_l * (gate_l * (1.0 - gate_l)),
        grad_left * gate_l,
        grad_right * val_r * (gate_r * (1.0 - gate_r)),
        grad_right * gate_r,
        grad_gate * (gate * (1.0 - gate)),
    )
    grad = jnp.concatenate([piece.astype(BF16) for piece in pieces], axis=1)
    return rounded(normalize_back(rounded(matmul_t(grad, weight)), normed, inverse))


def chain_length(mask_ref):
    return jnp.sum(mask_ref[...], axis=1, keepdims=True).astype(jnp.int32)


def pair_mask(chain, count, span, start, offset):
    major = lax.broadcasted_iota(jnp.int32, (count, span, H), 0) + start
    minor = lax.broadcasted_iota(jnp.int32, (count, span, H), 1) + offset
    inside = jnp.maximum(major, minor).reshape(count * span, H) < chain
    return jnp.where(inside, 1.0, 0.0)


def projection(weight, source, mask):
    normed, _ = normalize(source)
    gate_l, val_l, gate_r, val_r, gate = split(matmul(normed, weight))
    return (
        mask * (sigmoid(gate_l) * val_l),
        mask * (sigmoid(gate_r) * val_r),
        sigmoid(gate),
    )


def product(count, span, row_of, ref_a, ref_b, pitch, minor, width):
    totals = [None] * count
    for s in range(span):
        block = ref_b[pl.ds(s * pitch + minor, width), :]
        for p in range(count):
            term = jnp.broadcast_to(ref_a[pl.ds(row_of(p, s), 1), :], (width, H)) * block
            totals[p] = term if totals[p] is None else totals[p] + term
    return totals


def half_kernel(
    n, rows, cols, blocks, mask_ref, own_ref, weight_ref, left, right, gate, part, act, right_t,
):
    pitch = n + PAD
    row_index = lax.axis_index("row")
    chain = chain_length(mask_ref)
    for position, block in enumerate(blocks):
        place = (row_index ^ block) * rows
        for a in range(rows):
            where = pl.ds(pl.multiple_of((place + a) * cols, cols), cols)
            act[where, :] = own_ref[position, a].astype(F32)
    mask = pair_mask(chain, n, cols, 0, lax.axis_index("col") * cols)
    a, b, g = projection(weight_ref[0, :, : 5 * H], act[...], mask)
    left[...] = a
    right[...] = b
    gate[...] = g
    for i in range(n):
        right_t[pl.ds(i, cols, stride=pitch), :] = b[i * cols : (i + 1) * cols]
    for start in range(0, n, rows):
        totals = product(
            rows, cols, lambda p, s: (start + p) * cols + s, left, right_t, pitch, 0, n)
        part[pl.ds(start * n, rows * n), :] = jnp.concatenate(totals, axis=0)


def access(n, rows, cols, blocks, mask_ref):
    pitch = n + PAD
    row_index = lax.axis_index("row")
    col_index = lax.axis_index("col")
    chain = chain_length(mask_ref)
    me = row_index * rows
    mine = pl.multiple_of(col_index * cols, cols)
    theirs = pl.multiple_of((1 - col_index) * cols, cols)
    step = rows * n

    def mask_of(count, span, start, offset):
        return pair_mask(chain, count, span, start, offset)

    def get(ref, start=0, count=n):
        return jnp.concatenate(
            [ref[pl.ds((start + a) * pitch, n), :] for a in range(count)], axis=0
        )

    def put(ref, start, values, count=n):
        for a in range(count):
            ref[pl.ds((start + a) * pitch, n), :] = values[a * n : (a + 1) * n]

    def put_t(ref, values):
        for a in range(n):
            ref[pl.ds(a, n, stride=pitch), :] = values[a * n : (a + 1) * n]

    def get_t(ref):
        return [ref[pl.ds(me + a, n, stride=pitch), :] for a in range(rows)]

    def take(ref):
        return jnp.concatenate([get(ref, me, rows)] + get_t(ref), axis=0)

    def own(ref, base, stride):
        return jnp.concatenate(
            [ref[pl.ds(base + a * stride + mine, cols), :] for a in range(rows)], axis=0)

    def place(ref, own_ref, other_ref):
        for position, block in enumerate(blocks):
            start = (row_index ^ block) * rows
            for a in range(rows):
                base = (start + a) * pitch
                ref[pl.ds(base + mine, cols), :] = own_ref[position, a].astype(F32)
                ref[pl.ds(base + theirs, cols), :] = other_ref[position, a].astype(F32)

    return me, mine, theirs, step, pitch, mask_of, place, get, put, put_t, take, own


def outgoing_kernel(
    n, rows, cols, blocks, mask_ref, own_ref, other_ref, weight_ref,
    half_left, half_right, half_gate, part, act, left, right, gate0, mixed0, right_t,
):
    (_, mine, theirs, _, pitch, mask_of, place, _, put, _, _, _) = access(
        n, rows, cols, blocks, mask_ref)
    front_ref = weight_ref.at[:, :, : 5 * H]
    place(act, own_ref, other_ref)

    source = jnp.concatenate(
        [act[pl.ds(i * pitch + theirs, cols), :] for i in range(n)], axis=0)
    a, b, g = projection(front_ref[0], source, mask_of(n, cols, 0, theirs))
    for i in range(n):
        these = slice(i * cols, (i + 1) * cols)
        right_t[pl.ds(i, cols, stride=pitch), :] = b[these]
        for ref, done, new in (
            (left, half_left, a), (right, half_right, b), (gate0, half_gate, g)):
            ref[pl.ds(i * pitch + theirs, cols), :] = new[these]
            ref[pl.ds(i * pitch + mine, cols), :] = done[pl.ds(i * cols, cols), :]

    for start in range(0, n, rows):
        totals = product(
            rows, cols, lambda p, s: (start + p) * pitch + theirs + s, left, right_t, pitch, 0, n)
        rest = part[pl.ds(start * n, rows * n), :]
        put(mixed0, start, jnp.concatenate(totals, axis=0) + rest, rows)


def incoming_kernel(
    n, rows, cols, blocks, mask_ref, weight_ref, act, gate0, mixed0,
    mid, left1, right1, left1_t, right1_t, gate1, mixed1,
):
    (_, _, _, _, pitch, mask_of, _, get, put, put_t, _, _) = access(
        n, rows, cols, blocks, mask_ref)
    front_ref, out_ref = weight_ref.at[:, :, : 5 * H], weight_ref.at[:, :, 5 * H :]
    normed, _ = normalize(get(mixed0))
    value = get(act) + get(gate0) * matmul(normed, out_ref[0])
    put(mid, 0, value)
    a, b, g = projection(front_ref[1], value, mask_of(n, n, 0, 0))
    put(left1, 0, a)
    put(right1, 0, b)
    put_t(left1_t, a)
    put_t(right1_t, b)
    put(gate1, 0, g)

    for start in range(0, n, rows):
        totals = product(rows, n, lambda p, s: s * pitch + start + p, left1, right1, pitch, 0, n)
        put(mixed1, start, jnp.concatenate(totals, axis=0), rows)


def backward_kernel(
    n, rows, cols, blocks, mask_ref, act_ref, own_ref, other_ref, weight_ref,
    left, right, gate0, mixed0, mid, left1, right1, left1_t, right1_t, gate1, mixed1,
    grad_ref, cot, sig, sig_t, grow, s_gate, s_sig, dl, dr,
):
    (me, mine, _, step, pitch, mask_of, place, get, put, put_t, take, own) = access(
        n, rows, cols, blocks, mask_ref)
    front_ref, out_ref = weight_ref.at[:, :, : 5 * H], weight_ref.at[:, :, 5 * H :]
    place(cot, own_ref, other_ref)

    normed, inverse = normalize(get(mixed1))
    grad = rounded(matmul_t(get(cot) * get(gate1), out_ref[1]))
    value = rounded(normalize_back(grad, normed, inverse))
    put(sig, 0, value)
    put_t(sig_t, value)

    def row_of(p, s):
        return (me + p) * pitch + s

    dl[pl.ds(0, step), :] = jnp.concatenate(
        product(rows, n, row_of, right1, sig_t, pitch, 0, n), axis=0)
    dl[pl.ds(step, step), :] = jnp.concatenate(
        product(rows, n, row_of, sig, right1_t, pitch, 0, n), axis=0)
    dr[pl.ds(0, step), :] = jnp.concatenate(
        product(rows, n, row_of, left1, sig, pitch, 0, n), axis=0)
    dr[pl.ds(step, step), :] = jnp.concatenate(
        product(rows, n, lambda p, s: s * pitch + me + p, sig, left1_t, pitch, 0, n), axis=0)

    mask_rows = mask_of(rows, n, me, 0)
    cot_s = take(cot)
    mixed, _ = normalize(take(mixed1))
    normed, inverse = normalize(take(mid))
    grad_gate = cot_s * matmul(mixed, out_ref[1])
    grad = front_back(
        matmul(normed, front_ref[1]), jnp.concatenate([mask_rows, mask_rows], axis=0),
        rounded(dl[...]), rounded(dr[...]), grad_gate, front_ref[1], normed, inverse)
    grad_mid = rounded(cot_s + grad)
    mixed, inverse = normalize(take(mixed0))
    grow[...] = grad_mid[:step]
    s_gate[...] = grad_mid[:step] * matmul(mixed[:step], out_ref[0])
    grad = rounded(matmul_t(grad_mid * take(gate0), out_ref[0]))
    s_sig[...] = rounded(normalize_back(grad, mixed, inverse))

    grad_left = product(rows, n, lambda p, s: p * n + s, s_sig, right, pitch, mine, cols)
    grad_right = product(rows, n, lambda p, s: step + p * n + s, s_sig, left, pitch, mine, cols)

    normed, inverse = normalize(act_ref[0].astype(F32).reshape(rows * cols, H))
    grad = front_back(
        matmul(normed, front_ref[0]), mask_of(rows, cols, me, mine),
        rounded(jnp.concatenate(grad_left, axis=0)), rounded(jnp.concatenate(grad_right, axis=0)),
        own(s_gate, 0, n), front_ref[0], normed, inverse)
    grad_ref[...] = (own(grow, 0, n) + grad).astype(BF16).reshape(rows, cols, H)


def whole_body(pair_act, cotangent, residue_mask, front_weight, out_weight):
    rows, cols, _ = pair_act.shape
    n = residue_mask.shape[0]
    row_count = lax.axis_size("row")
    bits = row_count.bit_length() - 1
    weights = jnp.concatenate((front_weight, out_weight), axis=2)
    mask = residue_mask.reshape(1, n).astype(F32)
    blocks = [0]
    steps = [1] + [1 << b for b in range(bits - 1, 0, -1)]

    def swap(array, step):
        return lax.ppermute(array, "row", [(i, i ^ step) for i in range(row_count)])

    sent = (pair_act[None], cotangent[None])
    held = lax.optimization_barrier(jnp.stack(sent))
    held = (held[0], held[1])
    for step in steps:
        act_late = swap(sent[0], step)
        cot_late = swap(sent[1], step)
        act = jnp.concatenate((held[0], act_late))
        if step != steps[-1]:
            cot = jnp.concatenate((held[1], cot_late))
            sent = held = (act, cot)
        blocks = blocks + [b ^ step for b in blocks]
    act_other = lax.ppermute(act, "col", [(0, 1), (1, 0)])
    full = pltpu.VMEM((n * (n + PAD), H), F32)
    some = pltpu.VMEM((rows * n, H), F32)
    twice = pltpu.VMEM((2 * rows * n, H), F32)
    vmem = pl.BlockSpec(memory_space=pltpu.VMEM)
    part_of = jax.ShapeDtypeStruct((n * cols, H), F32)
    halves = pl.pallas_call(
        functools.partial(half_kernel, n, rows, cols, blocks),
        out_shape=[part_of] * 3 + [jax.ShapeDtypeStruct((n * n, H), F32)],
        in_specs=[vmem] * 3,
        out_specs=[vmem] * 4,
        scratch_shapes=[pltpu.VMEM((n * cols, H), F32), pltpu.VMEM((cols * (n + PAD), H), F32)],
        compiler_params=pltpu.CompilerParams(vmem_limit_bytes=VMEM_BUDGET // 4),
    )(mask, act, weights)
    pairs_of = jax.ShapeDtypeStruct((n * (n + PAD), H), F32)
    act_full, left, right, gate0, mixed0 = pl.pallas_call(
        functools.partial(outgoing_kernel, n, rows, cols, blocks),
        out_shape=[pairs_of] * 5,
        in_specs=[vmem] * 8,
        out_specs=[vmem] * 5,
        scratch_shapes=[full],
        compiler_params=pltpu.CompilerParams(vmem_limit_bytes=VMEM_BUDGET // 4),
    )(mask, act, act_other, weights, *halves)
    cot_late, mixed0 = lax.optimization_barrier((cot_late, mixed0))
    cot = jnp.concatenate((held[1], cot_late))
    cot_other = lax.ppermute(cot, "col", [(0, 1), (1, 0)])
    incoming = pl.pallas_call(
        functools.partial(incoming_kernel, n, rows, cols, blocks),
        out_shape=[pairs_of] * 7,
        in_specs=[vmem] * 5,
        out_specs=[vmem] * 7,
        compiler_params=pltpu.CompilerParams(vmem_limit_bytes=VMEM_BUDGET // 4),
    )(mask, weights, act_full, gate0, mixed0)
    kept = (left, right, gate0, mixed0, *incoming)
    return pl.pallas_call(
        functools.partial(backward_kernel, n, rows, cols, blocks),
        out_shape=jax.ShapeDtypeStruct(pair_act.shape, BF16),
        in_specs=[vmem] * 16,
        out_specs=vmem,
        scratch_shapes=[full] * 3 + [some, some, twice, twice, twice],
        compiler_params=pltpu.CompilerParams(vmem_limit_bytes=VMEM_BUDGET // 2),
    )(mask, act, cot, cot_other, weights, *kept)


def body(pair_act, cotangent, residue_mask, front_weight, out_weight):
    n = residue_mask.shape[0]
    row_count = lax.axis_size("row")
    fits = 20 * n * (n + PAD) * H * 4 <= VMEM_BUDGET
    doubling = row_count >= 4 and row_count & (row_count - 1) == 0 and lax.axis_size("col") == 2
    run = whole_body if fits and doubling else spread_body
    return run(pair_act, cotangent, residue_mask, front_weight, out_weight)


def solution(mesh):
    placed = (P(("grp", "row"), "col", None), P(("grp", "row"), "col", None), P("grp"), P(), P())
    return jax.shard_map(
        body, mesh=mesh, in_specs=placed, out_specs=P(("grp", "row"), "col", None), check_vma=False
    )
```
